256 devices in a mesh: grp: 4 (over x), req: 64 (over y, z, core).
Axes of the slice: x: 4, y: 4, z: 8, core: 2. Of those that a mesh axis runs over, the one named last changes fastest.
Arguments:
- mix_inputs: bfloat16 [512, 16, 8, 384], P('req', None, 'grp'), may hold values from -6 to 6
- conv_weight: float32 [4, 8, 384], P(None, 'grp'), may hold values from -3 to 3
- forget_bias: float32 [8, 128], P('grp'), may hold values from -2 to 4
- norm_gain: float32 [8, 128], P('grp'), may hold values from 0.1 to 1.9
- out_weight: bfloat16 [1024, 2048], P('grp'), may hold values from -0.1875 to 0.1875
- resid: bfloat16 [512, 16, 2048], P('req'), may hold values from -6 to 6
- ffn_gain: float32 [2048], replicated, may hold values from 0.1 to 1.9
- gate_weight: bfloat16 [2048, 2816], P(None, 'grp'), may hold values from -0.125 to 0.125
- up_weight: bfloat16 [2048, 2816], P(None, 'grp'), may hold values from -0.125 to 0.125
- down_weight: bfloat16 [2816, 2048], P('grp'), may hold values from -0.109375 to 0.109375
- held_states: float32 [512, 8, 128, 128], P('req', 'grp'), may hold values from -6 to 6
- held_edges: bfloat16 [512, 3, 8, 384], P('req', None, 'grp'), may hold values from -6 to 6
- draft_lengths: int32 [512], replicated, may hold values from 1 to 16, as said below
- accepted: int32 [512], replicated, may hold values from 1 to 16, as said below
- owner_row: int32 [512], replicated, may hold values from 0 to 511, as said below
Outputs:
- layer_out: bfloat16 [512, 16, 2048], P('req', None, 'grp')
- kept_states: float32 [512, 8, 128, 128], P('req', 'grp')
- kept_edges: bfloat16 [512, 3, 8, 384], P('req', None, 'grp')
The draws below stay inside these ranges and needn't reach their ends.
Inputs may be any that keep to these rules, and one draw needn't show every extreme that they name: draft_lengths[i] + draft_lengths[i + 256] = 17 for i < 256, so the live tokens number 68 per index of req on average; the first 8 requests have 16 tokens each. accepted[i] lies between 1 and draft_lengths[i]. owner_row is a permutation made of pairwise swaps: a request among the last 4 of index d of req may take the row of a request among the first 4 of index d + 1 (modulo the size of req), which then takes its row; every other request keeps its own row. So at most 4 requests of one index take rows of one neighbour, and index 0 reaches that most in every draw.
All inputs are finite; a program needn't handle non-finite values.
Results may differ from the reference program's by a relative error of at most 0.017.
Values may be sent and summed in bfloat16 or wider, within the bound.
No kernel may reach another device: no remote copies, remote signals or barrier semaphores. Data moves between devices by JAX's collectives and lax.ppermute only.
A program may use at most 64 MiB of HBM per device.

```python
import jax
import jax.numpy as jnp
from jax import lax

D = 2048
HEADS = 8
DK = 128
FF_WIN = 2816
DRAFT = 16
CONV = 4
REQ_DEV = 8
REQUESTS = 512
N_REQ = 64


def length_table(key):
    half_count = REQUESTS // 2
    device_key, request_key = jax.random.split(jax.random.fold_in(key, 11))
    heavy = jax.random.randint(device_key, (N_REQ // 2,), 0, DRAFT - 3)
    heavy = heavy.at[0].set(DRAFT - 1)
    floor_len = jnp.repeat(heavy, REQ_DEV)
    first_half = jax.random.randint(request_key, (half_count,), 1 + floor_len, DRAFT + 1)
    return jnp.concatenate([first_half, DRAFT + 1 - first_half]).astype(jnp.int32)


def draw_draft_lengths(key, part):
    return length_table(key)


def draw_accepted(key, part):
    lengths = length_table(key)
    accept_key = jax.random.fold_in(key, 12)
    counts = jax.random.randint(accept_key, (REQUESTS,), 1, lengths + 1)
    counts = counts.at[0].set(lengths[0])
    counts = counts.at[1].set(1)
    return counts.astype(jnp.int32)


def draw_owner_row(key, part):
    half_dev = REQ_DEV // 2
    count_key, upper_key, lower_key = jax.random.split(jax.random.fold_in(key, 13), 3)
    counts_moved = jax.random.randint(count_key, (N_REQ,), 0, half_dev + 1)
    counts_moved = counts_moved.at[0].set(half_dev)
    upper_perm = jax.vmap(lambda sub_key: jax.random.permutation(sub_key, half_dev))(jax.random.split(upper_key, N_REQ)) + half_dev
    lower_perm = jax.vmap(lambda sub_key: jax.random.permutation(sub_key, half_dev))(jax.random.split(lower_key, N_REQ))
    devices_all = jnp.arange(N_REQ)
    next_dev = (devices_all + 1) % N_REQ
    slot_upper = devices_all[:, None] * REQ_DEV + upper_perm
    slot_lower = next_dev[:, None] * REQ_DEV + lower_perm[next_dev]
    moving = jnp.arange(half_dev)[None, :] < counts_moved[:, None]
    table = jnp.arange(REQUESTS)
    table = table.at[slot_upper.reshape(-1)].set(jnp.where(moving, slot_lower, slot_upper).reshape(-1))
    table = table.at[slot_lower.reshape(-1)].set(jnp.where(moving, slot_upper, slot_lower).reshape(-1))
    return table.astype(jnp.int32)


def block_levels(key, shape, cuts, least, high):
    gain = 1.0
    for dim, shards_of in cuts:
        draws = jax.random.uniform(jax.random.fold_in(jax.random.fold_in(key, 6), dim), (shards_of,), jnp.float32, least / len(cuts), high / len(cuts))
        gain = gain * jnp.repeat(jnp.exp(draws), shape[dim] // shards_of).reshape((-1,) + (1,) * (len(shape) - 1 - dim))
    return gain


def gaussian(key, extent, spread, reach, cuts=(), held_as=jnp.bfloat16):
    result = jax.random.normal(key, extent, jnp.float32) * spread
    if len(cuts) > 0:
        result = block_levels(key, extent, cuts, -0.22, 0.18) * result
    return jnp.clip(result, min=-reach, max=reach).astype(held_as)


def setup_inputs(seed: int = 0) -> dict:
    key_list = jax.random.split(jax.random.key(seed), 16)
    mix_inputs = gaussian(key_list[0], (REQUESTS, DRAFT, HEADS, 3 * DK), 1.0, 6.0, ((0, 64), (2, 4)))
    conv_weight = gaussian(key_list[1], (CONV, HEADS, 3 * DK), 0.5, 3.0, ((1, 4),), jnp.float32)
    forget_bias = jnp.clip(-2.0 + 6.0 * jax.random.uniform(key_list[2], (HEADS, DK), jnp.float32) ** block_levels(key_list[2], (HEADS, DK), ((0, 4),), -0.2, 0.2), -2.0, 4.0)
    norm_gain = jnp.clip(1.0 + 0.18 * jax.random.normal(key_list[3], (HEADS, DK), jnp.float32), 0.1, 1.9)
    out_weight = gaussian(key_list[4], (HEADS * DK, D), (HEADS * DK) ** -0.5, 0.1875, ((0, 4),))
    resid = gaussian(key_list[5], (REQUESTS, DRAFT, D), 1.0, 6.0, ((0, 64),))
    ffn_gain = jnp.clip(1.0 + 0.18 * jax.random.normal(key_list[6], (D,), jnp.float32), 0.1, 1.9)
    gate_weight = gaussian(key_list[7], (D, FF_WIN), D ** -0.5, 0.125, ((1, 4),))
    up_weight = gaussian(key_list[8], (D, FF_WIN), D ** -0.5, 0.125, ((1, 4),))
    down_weight = gaussian(key_list[9], (FF_WIN, D), FF_WIN ** -0.5, 0.109375, ((0, 4),))
    held_states = gaussian(key_list[10], (REQUESTS, HEADS, DK, DK), 1.0, 6.0, ((0, 64), (1, 4)), jnp.float32)
    held_edges = gaussian(key_list[11], (REQUESTS, CONV - 1, HEADS, 3 * DK), 1.0, 6.0, ((0, 64), (2, 4)))
    draft_lengths = draw_draft_lengths(jax.random.fold_in(key_list[15], 71), 0)
    accepted = draw_accepted(jax.random.fold_in(key_list[15], 71), 0)
    owner_row = draw_owner_row(jax.random.fold_in(key_list[15], 71), 0)
    return {"mix_inputs": mix_inputs, "conv_weight": conv_weight, "forget_bias": forget_bias, "norm_gain": norm_gain, "out_weight": out_weight, "resid": resid, "ffn_gain": ffn_gain, "gate_weight": gate_weight, "up_weight": up_weight, "down_weight": down_weight, "held_states": held_states, "held_edges": held_edges, "draft_lengths": draft_lengths, "accepted": accepted, "owner_row": owner_row}


def run_mixer(draft_inputs, conv_edges, carried_over, conv_weight, forget_bias, norm_gain, accept_count):
    window_bf = jnp.concatenate([conv_edges, draft_inputs], axis=0)
    window = window_bf.astype(jnp.float32)
    conv_out = conv_weight[0] * window[0:DRAFT]
    for shift_pos in range(1, CONV):
        conv_out = conv_out + conv_weight[shift_pos] * window[shift_pos:shift_pos + DRAFT]
    queries = jax.nn.silu(conv_out[..., :DK]) * DK ** (-0.5)
    forget = jax.nn.sigmoid(conv_out[..., DK:2 * DK] + forget_bias)
    values_in = jax.nn.silu(conv_out[..., 2 * DK:])

    def advance(carry, step_in):
        current_step, kept_state = carry
        present_query, forget_now, value_now, position = step_in
        current_step = forget_now[:, :, None] * current_step + (1.0 - forget_now)[:, :, None] * value_now[:, None, :]
        present_head = jnp.einsum('ul,ulw->uw', present_query, current_step, precision=lax.Precision.HIGHEST)
        kept_state = jnp.where(position == accept_count - 1, current_step, kept_state)
        return ((current_step, kept_state), present_head)
    positions = jnp.arange(DRAFT, dtype=jnp.int32)
    (state_end, kept_state), head_outs = lax.scan(advance, (carried_over, carried_over), (queries, forget, values_in, positions))
    inverse_scale = lax.rsqrt(lax.optimization_barrier(jnp.mean(head_outs * head_outs, axis=-1, keepdims=True)) + 1e-05)
    mixed_out = (head_outs * inverse_scale * norm_gain).astype(jnp.bfloat16)
    edges_out = lax.dynamic_slice_in_dim(window_bf, accept_count, CONV - 1, 0)
    return (mixed_out, kept_state, edges_out)

def reference(mix_inputs, conv_weight, forget_bias, norm_gain, out_weight, resid, ffn_gain, gate_weight, up_weight, down_weight, held_states, held_edges, draft_lengths, accepted, owner_row):
    request_ids = jnp.arange(REQUESTS, dtype=jnp.int32)
    inverse = jnp.zeros((REQUESTS,), jnp.int32).at[owner_row].set(request_ids)

    def per_request(request):
        source_row = owner_row[request]
        return run_mixer(mix_inputs[request], held_edges[source_row], held_states[source_row], conv_weight, forget_bias, norm_gain, accepted[request])
    mixed_out, kept_all, edges_all = lax.map(per_request, request_ids)
    kept_states = kept_all[inverse]
    kept_edges = edges_all[inverse]
    slot_count = REQUESTS * DRAFT
    projected = jnp.dot(mixed_out.reshape(slot_count, HEADS * DK), out_weight, preferred_element_type=jnp.float32)
    stream = (resid.reshape(slot_count, D).astype(jnp.float32) + projected).astype(jnp.bfloat16)
    stream_f = stream.astype(jnp.float32)
    mean_sq = lax.optimization_barrier(jnp.mean(stream_f * stream_f, axis=-1, keepdims=True))
    normed = (stream_f * lax.rsqrt(mean_sq + 1e-05) * ffn_gain).astype(jnp.bfloat16)
    gate_pre = jnp.dot(normed, gate_weight, preferred_element_type=jnp.float32)
    up_pre = jnp.dot(normed, up_weight, preferred_element_type=jnp.float32)
    hidden = (jax.nn.silu(gate_pre) * up_pre).astype(jnp.bfloat16)
    down_sum = jnp.dot(hidden, down_weight, preferred_element_type=jnp.float32).astype(jnp.bfloat16)
    live_mask = (jnp.arange(DRAFT, dtype=jnp.int32)[None, :] < draft_lengths[:, None]).reshape(slot_count)
    summed = (stream_f + down_sum.astype(jnp.float32)).astype(jnp.bfloat16)
    layer_out = jnp.where(live_mask[:, None], summed, jnp.zeros_like(summed)).reshape(REQUESTS, DRAFT, D)
    return (layer_out, kept_states, kept_edges)
```

```python
import jax
import jax.numpy as jnp
from jax import lax
from jax.experimental import pallas as pl
from jax.experimental.pallas import tpu as pltpu
from jax.sharding import PartitionSpec as P

DK = 128
DRAFT = 16
CONV = 4
HALF = 4
ROWS = 2 * HALF
BF = jnp.bfloat16
F32 = jnp.float32
VM = pl.BlockSpec(memory_space=pltpu.VMEM)
SM = pl.BlockSpec(memory_space=pltpu.SMEM)


def source_of(owner_ref, row):
    me = lax.axis_index("req")
    partner = owner_ref[me * ROWS + row]
    local = partner // ROWS == me
    return partner, local, partner % HALF


def mixer_kernel(
    owner_ref,
    accept_ref,
    own_ref,
    low_ref,
    high_ref,
    edge_ref,
    state_ref,
    conv_ref,
    bias_ref,
    gain_ref,
    mixed_low_ref,
    mixed_high_ref,
    value_ref,
    weight_ref,
    decay_ref,
    edges_out_ref,
    window,
    query_scr,
    forget_scr,
):
    heads = 2
    for row in range(ROWS):
        _, local, place = source_of(owner_ref, row)
        other_ref = low_ref if row < HALF else high_ref
        own = own_ref[row].astype(F32)
        other = other_ref[place].astype(F32)
        picked = jnp.where(local, own, other)
        edge = edge_ref[row].astype(F32)
        for block in range(3):
            columns = slice(block * DK, (block + 1) * DK)
            window[row, block, 8:40, :] = picked[:, columns]
            window[row, block, 2:8, :] = edge[:, columns]

    sub_iota = lax.broadcasted_iota(jnp.int32, (1, DRAFT, DK), 1)

    def pair(step, _):
        base = step * 2
        for sub in range(2):
            row = base + sub
            for head in range(heads):
                sums = []
                for block in range(3):
                    acc = None
                    for shift in range(CONV):
                        taps = conv_ref[shift, head, block * DK : (block + 1) * DK]
                        start = 2 + 2 * shift + head
                        rows = window[row, block, pl.ds(start, DRAFT, stride=2), :]
                        term = taps[None, :] * rows
                        acc = term if acc is None else acc + term
                    sums.append(acc)
                slot = sub * heads + head
                queries, gates, values = sums
                query_scr[slot] = queries * jax.nn.sigmoid(queries) * DK ** (-0.5)
                forget_scr[slot] = jax.nn.sigmoid(gates + bias_ref[head, :][None, :])
                value_ref[row, head] = values * jax.nn.sigmoid(values)
        queries = query_scr[...]
        forget = forget_scr[...]
        values = value_ref[pl.ds(base, 2)].reshape(4, DRAFT, DK)
        lengths = []
        for sub in range(2):
            partner, _, _ = source_of(owner_ref, base + sub)
            lengths.append(accept_ref[partner])
        weights = jnp.zeros((4, DRAFT, DK), F32)
        kept = [jnp.zeros((heads, DRAFT, DK), F32) for _ in range(2)]
        kept_decay = [jnp.zeros((heads, 1, DK), F32) for _ in range(2)]
        decay = jnp.ones((4, 1, DK), F32)
        head_rows = []
        query_rows = []
        for t in range(DRAFT):
            forget_t = forget[:, t : t + 1, :]
            query_t = queries[:, t : t + 1, :]
            decay = decay * forget_t
            weights = jnp.where(sub_iota == t, 1.0 - forget_t, weights * forget_t)
            scores = jnp.sum(weights * query_t, axis=-1, keepdims=True)
            head_rows.append(jnp.sum(scores * values, axis=1, keepdims=True))
            query_rows.append(query_t * decay)
            for sub in range(2):
                now = lengths[sub] == t + 1
                part = slice(sub * heads, (sub + 1) * heads)
                kept[sub] = jnp.where(now, weights[part], kept[sub])
                kept_decay[sub] = jnp.where(now, decay[part], kept_decay[sub])
        local_out = jnp.concatenate(head_rows, axis=1)
        decayed = jnp.concatenate(query_rows, axis=1)
        for sub in range(2):
            row = base + sub
            weight_ref[row] = kept[sub]
            decay_ref[row] = kept_decay[sub]
            for head in range(heads):
                slot = sub * heads + head
                out = local_out[slot] + jnp.dot(
                    decayed[slot],
                    state_ref[row, head],
                    preferred_element_type=F32,
                    precision=lax.Precision.HIGHEST,
                )
                scale = lax.rsqrt(jnp.mean(out * out, axis=-1, keepdims=True) + 1e-05)
                mixed = (out * scale * gain_ref[head, :][None, :]).astype(BF)
                columns = slice(head * DK, (head + 1) * DK)

                @pl.when(row < HALF)
                def _():
                    mixed_low_ref[jnp.minimum(row, HALF - 1), :, columns] = mixed

                @pl.when(row >= HALF)
                def _():
                    mixed_high_ref[jnp.maximum(row - HALF, 0), :, columns] = mixed

        return 0

    lax.fori_loop(0, ROWS // 2, pair, 0)
    for row in range(ROWS):
        partner, _, _ = source_of(owner_ref, row)
        start = 2 + 2 * accept_ref[partner]
        for block in range(3):
            turned = pltpu.roll(window[row, block], 40 - start, 0)
            columns = slice(block * DK, (block + 1) * DK)
            edges_out_ref[row, :, columns] = turned[:6].astype(BF)


def mixer(owner, accept, own, low, high, edges, states, conv, bias, gain):
    shape = jax.ShapeDtypeStruct
    return pl.pallas_call(
        mixer_kernel,
        name="mixer",
        out_shape=(
            shape((HALF, DRAFT, 2 * DK), BF),
            shape((HALF, DRAFT, 2 * DK), BF),
            shape((ROWS, 2, DRAFT, DK), F32),
            shape((ROWS, 2, DRAFT, DK), F32),
            shape((ROWS, 2, 1, DK), F32),
            shape((ROWS, 6, 3 * DK), BF),
        ),
        in_specs=[SM, SM] + [VM] * 8,
        out_specs=tuple([VM] * 6),
        scratch_shapes=[
            pltpu.VMEM((ROWS, 3, 40, DK), F32),
            pltpu.VMEM((4, DRAFT, DK), F32),
            pltpu.VMEM((4, DRAFT, DK), F32),
        ],
        cost_estimate=pl.CostEstimate(
            flops=20_000_000, bytes_accessed=2_000_000, transcendentals=400_000
        ),
    )(owner, accept, own, low, high, edges, states, conv, bias, gain)


def keep_kernel(state_ref, value_ref, weight_ref, decay_ref, kept_ref):
    for row in range(ROWS):
        for head in range(2):
            update = lax.dot_general(
                weight_ref[row, head],
                value_ref[row, head],
                (((0,), (0,)), ((), ())),
                preferred_element_type=F32,
                precision=lax.Precision.HIGHEST,
            )
            column = jnp.transpose(jnp.broadcast_to(decay_ref[row, head], (DK, DK)))
            kept_ref[row, head] = column * state_ref[row, head] + update


def keep(states, values, weights, decay):
    return pl.pallas_call(
        keep_kernel,
        name="keep",
        out_shape=jax.ShapeDtypeStruct(states.shape, F32),
        in_specs=[VM] * 4,
        out_specs=VM,
        cost_estimate=pl.CostEstimate(
            flops=20_000_000, bytes_accessed=3_000_000, transcendentals=0
        ),
    )(states, values, weights, decay)


def columns_of(step, width):
    place = (lax.axis_index("grp") + step) % 4
    return pl.ds(pl.multiple_of(place * width, width), width)


def project_kernel(
    owner_ref, low_ref, high_ref, from_low_ref, from_high_ref, weight_ref, resid_ref,
    own_ref, next_ref, far_ref, prev_ref, rows_scr,
):
    width = own_ref.shape[1]
    for row in range(ROWS):
        _, local, place = source_of(owner_ref, row)
        mine = low_ref[row] if row < HALF else high_ref[row - HALF]
        other = from_low_ref[place] if row < HALF else from_high_ref[place]
        picked = jnp.where(local, mine.astype(F32), other.astype(F32)).astype(BF)
        rows_scr[row * DRAFT : (row + 1) * DRAFT, :] = picked
    rows = rows_scr[...]
    for step, out_ref in ((2, far_ref), (1, next_ref), (3, prev_ref)):
        part = jnp.dot(rows, weight_ref[:, columns_of(step, width)], preferred_element_type=F32)
        out_ref[...] = part.astype(BF)
    part = jnp.dot(rows, weight_ref[:, columns_of(0, width)], preferred_element_type=F32)
    own_ref[...] = part + resid_ref[:, columns_of(0, width)].astype(F32)


def project(owner, low, high, from_low, from_high, weight, resid):
    slots, model = resid.shape
    width = model // 4
    shape = jax.ShapeDtypeStruct
    return pl.pallas_call(
        project_kernel,
        name="project",
        out_shape=(
            shape((slots, width), F32),
            shape((slots, width), BF),
            shape((slots, width), BF),
            shape((slots, width), BF),
        ),
        in_specs=[SM] + [VM] * 6,
        out_specs=tuple([VM] * 4),
        scratch_shapes=[pltpu.VMEM((slots, 2 * DK), BF)],
        cost_estimate=pl.CostEstimate(
            flops=140_000_000, bytes_accessed=2_000_000, transcendentals=0
        ),
    )(owner, low, high, from_low, from_high, weight, resid)


def ffn_kernel(
    length_ref, own_ref, next_ref, far_ref, prev_ref, gain_ref, gate_ref, up_ref, down_ref,
    own_out_ref, next_out_ref, far_out_ref, prev_out_ref, normed_scr,
):
    width = own_ref.shape[1]
    parts = ((0, own_ref), (1, next_ref), (2, far_ref), (3, prev_ref))
    total = None
    for _, ref in parts:
        block = ref[...].astype(F32)
        square = jnp.sum(block * block, axis=-1, keepdims=True)
        total = square if total is None else total + square
    scale = lax.rsqrt(total / (4 * width) + 1e-05)
    for step, ref in parts:
        columns = columns_of(step, width)
        normed_scr[:, columns] = (ref[...].astype(F32) * scale * gain_ref[:, columns]).astype(BF)
    normed = normed_scr[...]
    dims = (((1,), (1,)), ((), ()))
    gate = lax.dot_general(normed, gate_ref[...], dims, preferred_element_type=F32)
    up = lax.dot_general(normed, up_ref[...], dims, preferred_element_type=F32)
    hidden = (gate * jax.nn.sigmoid(gate) * up).astype(BF)
    me = lax.axis_index("req")
    position = lax.broadcasted_iota(jnp.int32, (DRAFT, 1), 0)
    live = jnp.concatenate(
        [(position < length_ref[me * ROWS + row]).astype(F32) for row in range(ROWS)], axis=0
    )
    for step, out_ref in ((2, far_out_ref), (1, next_out_ref), (3, prev_out_ref)):
        part = jnp.dot(hidden, down_ref[:, columns_of(step, width)], preferred_element_type=F32)
        out_ref[...] = (part * live).astype(BF)
    part = jnp.dot(hidden, down_ref[:, columns_of(0, width)], preferred_element_type=F32)
    own_out_ref[...] = (part + own_ref[...].astype(F32)) * live


def ffn(lengths, own, following, far, preceding, gain, gate_t, up_t, down):
    slots, width = own.shape
    shape = jax.ShapeDtypeStruct
    return pl.pallas_call(
        ffn_kernel,
        name="ffn",
        out_shape=(
            shape((slots, width), F32),
            shape((slots, width), BF),
            shape((slots, width), BF),
            shape((slots, width), BF),
        ),
        in_specs=[SM] + [VM] * 8,
        out_specs=tuple([VM] * 4),
        scratch_shapes=[pltpu.VMEM((slots, 4 * width), BF)],
        cost_estimate=pl.CostEstimate(
            flops=1_100_000_000, bytes_accessed=9_000_000, transcendentals=100_000
        ),
    )(lengths, own, following, far, preceding, gain, gate_t, up_t, down)


def shifted(block, axis, step):
    count = lax.axis_size(axis)
    return lax.ppermute(block, axis, [(i, (i + step) % count) for i in range(count)])


def shards(
    mix_inputs,
    conv_weight,
    forget_bias,
    norm_gain,
    out_weight,
    resid,
    ffn_gain,
    gate_weight,
    up_weight,
    down_weight,
    held_states,
    held_edges,
    draft_lengths,
    accepted,
    owner_row,
):
    slots = ROWS * DRAFT
    lanes = 3 * DK
    low = shifted(mix_inputs[HALF:].reshape(HALF, 2 * DRAFT, lanes), "req", 1)
    high = shifted(mix_inputs[:HALF].reshape(HALF, 2 * DRAFT, lanes), "req", -1)
    own = mix_inputs.reshape(ROWS, 2 * DRAFT, lanes)
    edges = held_edges.reshape(ROWS, 6, lanes)
    mixed_low, mixed_high, values, weights, decay, edges_out = mixer(
        owner_row, accepted, own, low, high, edges, held_states,
        conv_weight, forget_bias, norm_gain,
    )
    from_low = shifted(mixed_high, "req", 1)
    from_high = shifted(mixed_low, "req", -1)
    kept_states = keep(held_states, values, weights, decay)
    kept_edges = edges_out.reshape(held_edges.shape)
    rows = resid.reshape(slots, resid.shape[2])
    own_part, to_next, to_far, to_prev = project(
        owner_row, mixed_low, mixed_high, from_low, from_high, out_weight, rows
    )
    far = shifted(to_far, "grp", 2)
    following = shifted(to_next, "grp", 1)
    preceding = shifted(to_prev, "grp", -1)
    stream = (
        own_part + far.astype(F32) + following.astype(F32) + preceding.astype(F32)
    ).astype(BF)
    far = shifted(stream, "grp", 2)
    preceding = shifted(stream, "grp", 1)
    following = shifted(stream, "grp", -1)
    own_part, to_next, to_far, to_prev = ffn(
        draft_lengths, stream, following, far, preceding, ffn_gain[None, :],
        gate_weight.T, up_weight.T, down_weight,
    )
    far = shifted(to_far, "grp", 2)
    following = shifted(to_next, "grp", 1)
    preceding = shifted(to_prev, "grp", -1)
    layer_out = (
        own_part + far.astype(F32) + following.astype(F32) + preceding.astype(F32)
    ).astype(BF)
    return (layer_out.reshape(ROWS, DRAFT, -1), kept_states, kept_edges)


def solution(mesh):
    return jax.shard_map(
        shards,
        mesh=mesh,
        in_specs=(
            P("req", None, "grp", None),
            P(None, "grp", None),
            P("grp", None),
            P("grp", None),
            P("grp", None),
            P("req", None, None),
            P(),
            P(None, "grp"),
            P(None, "grp"),
            P("grp", None),
            P("req", "grp", None, None),
            P("req", None, "grp", None),
            P(),
            P(),
            P(),
        ),
        out_specs=(P("req", None, "grp"), P("req", "grp", None, None), P("req", None, "grp", None)),
        check_vma=False,
    )
```

```python
import jax
import jax.numpy as jnp
from jax import lax
from jax.experimental import pallas as pl
from jax.experimental.pallas import tpu as pltpu
from jax.sharding import PartitionSpec as P

DK = 128
DRAFT = 16
CONV = 4
HALF = 4
ROWS = 2 * HALF
BF = jnp.bfloat16
PARAMS = pltpu.CompilerParams(vmem_limit_bytes=12 * 1024 * 1024)
F32 = jnp.float32
VM = pl.BlockSpec(memory_space=pltpu.VMEM)
SM = pl.BlockSpec(memory_space=pltpu.SMEM)


def source_of(owner_ref, row):
    me = lax.axis_index("req")
    partner = owner_ref[me * ROWS + row]
    local = partner // ROWS == me
    return partner, local, partner % HALF


def mixer_kernel(
    owner_ref,
    accept_ref,
    own_ref,
    low_ref,
    high_ref,
    edge_ref,
    state_ref,
    conv_ref,
    bias_ref,
    gain_ref,
    mixed_low_ref,
    mixed_high_ref,
    value_ref,
    weight_ref,
    decay_ref,
    edges_out_ref,
    window,
    query_scr,
    forget_scr,
):
    heads = 2
    for row in range(ROWS):
        _, local, place = source_of(owner_ref, row)
        other_ref = low_ref if row < HALF else high_ref
        own = own_ref[row].astype(F32)
        other = other_ref[place].astype(F32)
        picked = jnp.where(local, own, other)
        edge = edge_ref[row].astype(F32)
        for block in range(3):
            columns = slice(block * DK, (block + 1) * DK)
            window[row, block, 8:40, :] = picked[:, columns]
            window[row, block, 2:8, :] = edge[:, columns]

    sub_iota = lax.broadcasted_iota(jnp.int32, (1, DRAFT, DK), 1)

    def pair(step, _):
        base = step * 2
        for sub in range(2):
            row = base + sub
            for head in range(heads):
                sums = []
                for block in range(3):
                    acc = None
                    for shift in range(CONV):
                        taps = conv_ref[shift, head, block * DK : (block + 1) * DK]
                        start = 2 + 2 * shift + head
                        rows = window[row, block, pl.ds(start, DRAFT, stride=2), :]
                        term = taps[None, :] * rows
                        acc = term if acc is None else acc + term
                    sums.append(acc)
                slot = sub * heads + head
                queries, gates, values = sums
                query_scr[slot] = queries * jax.nn.sigmoid(queries) * DK ** (-0.5)
                forget_scr[slot] = jax.nn.sigmoid(gates + bias_ref[head, :][None, :])
                value_ref[row, head] = values * jax.nn.sigmoid(values)
        queries = query_scr[...]
        forget = forget_scr[...]
        values = value_ref[pl.ds(base, 2)].reshape(4, DRAFT, DK)
        lengths = []
        for sub in range(2):
            partner, _, _ = source_of(owner_ref, base + sub)
            lengths.append(accept_ref[partner])
        weights = jnp.zeros((4, DRAFT, DK), F32)
        kept = [jnp.zeros((heads, DRAFT, DK), F32) for _ in range(2)]
        kept_decay = [jnp.zeros((heads, 1, DK), F32) for _ in range(2)]
        decay = jnp.ones((4, 1, DK), F32)
        head_rows = []
        query_rows = []
        for t in range(DRAFT):
            forget_t = forget[:, t : t + 1, :]
            query_t = queries[:, t : t + 1, :]
            decay = decay * forget_t
            weights = jnp.where(sub_iota == t, 1.0 - forget_t, weights * forget_t)
            scores = jnp.sum(weights * query_t, axis=-1, keepdims=True)
            head_rows.append(jnp.sum(scores * values, axis=1, keepdims=True))
            query_rows.append(query_t * decay)
            for sub in range(2):
                now = lengths[sub] == t + 1
                part = slice(sub * heads, (sub + 1) * heads)
                kept[sub] = jnp.where(now, weights[part], kept[sub])
                kept_decay[sub] = jnp.where(now, decay[part], kept_decay[sub])
        local_out = jnp.concatenate(head_rows, axis=1)
        decayed = jnp.concatenate(query_rows, axis=1)
        for sub in range(2):
            row = base + sub
            weight_ref[row] = kept[sub]
            decay_ref[row] = kept_decay[sub]
            for head in range(heads):
                slot = sub * heads + head
                out = local_out[slot] + jnp.dot(
                    decayed[slot],
                    state_ref[row, head],
                    preferred_element_type=F32,
                    precision=lax.Precision.HIGHEST,
                )
                scale = lax.rsqrt(jnp.mean(out * out, axis=-1, keepdims=True) + 1e-05)
                mixed = (out * scale * gain_ref[head, :][None, :]).astype(BF)
                columns = slice(head * DK, (head + 1) * DK)

                @pl.when(row < HALF)
                def _():
                    mixed_low_ref[jnp.minimum(row, HALF - 1), :, columns] = mixed

                @pl.when(row >= HALF)
                def _():
                    mixed_high_ref[jnp.maximum(row - HALF, 0), :, columns] = mixed

        return 0

    lax.fori_loop(0, ROWS // 2, pair, 0)
    for row in range(ROWS):
        partner, _, _ = source_of(owner_ref, row)
        start = 2 + 2 * accept_ref[partner]
        for block in range(3):
            turned = pltpu.roll(window[row, block], 40 - start, 0)
            columns = slice(block * DK, (block + 1) * DK)
            edges_out_ref[row, :, columns] = turned[:6].astype(BF)


def mixer(owner, accept, own, low, high, edges, states, conv, bias, gain):
    shape = jax.ShapeDtypeStruct
    return pl.pallas_call(
        mixer_kernel,
        name="mixer",
        out_shape=(
            shape((HALF, DRAFT, 2 * DK), BF),
            shape((HALF, DRAFT, 2 * DK), BF),
            shape((ROWS, 2, DRAFT, DK), F32),
            shape((ROWS, 2, DRAFT, DK), F32),
            shape((ROWS, 2, 1, DK), F32),
            shape((ROWS, 6, 3 * DK), BF),
        ),
        in_specs=[SM, SM] + [VM] * 8,
        out_specs=tuple([VM] * 6),
        scratch_shapes=[
            pltpu.VMEM((ROWS, 3, 40, DK), F32),
            pltpu.VMEM((4, DRAFT, DK), F32),
            pltpu.VMEM((4, DRAFT, DK), F32),
        ],
        compiler_params=PARAMS,
        cost_estimate=pl.CostEstimate(
            flops=20_000_000, bytes_accessed=2_000_000, transcendentals=400_000
        ),
    )(owner, accept, own, low, high, edges, states, conv, bias, gain)


def keep_kernel(state_ref, value_ref, weight_ref, decay_ref, kept_ref):
    for row in range(ROWS):
        for head in range(2):
            update = lax.dot_general(
                weight_ref[row, head],
                value_ref[row, head],
                (((0,), (0,)), ((), ())),
                preferred_element_type=F32,
                precision=lax.Precision.HIGHEST,
            )
            column = jnp.transpose(jnp.broadcast_to(decay_ref[row, head], (DK, DK)))
            kept_ref[row, head] = column * state_ref[row, head] + update


def keep(states, values, weights, decay):
    return pl.pallas_call(
        keep_kernel,
        name="keep",
        out_shape=jax.ShapeDtypeStruct(states.shape, F32),
        in_specs=[VM] * 4,
        out_specs=VM,
        compiler_params=PARAMS,
        cost_estimate=pl.CostEstimate(
            flops=20_000_000, bytes_accessed=3_000_000, transcendentals=0
        ),
    )(states, values, weights, decay)


def columns_of(step, width):
    place = (lax.axis_index("grp") + step) % 4
    return pl.ds(pl.multiple_of(place * width, width), width)


def project_kernel(
    owner_ref, low_ref, high_ref, from_low_ref, from_high_ref, weight_ref, resid_ref,
    own_ref, next_ref, far_ref, prev_ref, rows_scr,
):
    width = own_ref.shape[1]
    for row in range(ROWS):
        _, local, place = source_of(owner_ref, row)
        mine = low_ref[row] if row < HALF else high_ref[row - HALF]
        other = from_low_ref[place] if row < HALF else from_high_ref[place]
        picked = jnp.where(local, mine.astype(F32), other.astype(F32)).astype(BF)
        rows_scr[row * DRAFT : (row + 1) * DRAFT, :] = picked
    rows = rows_scr[...]
    for step, out_ref in ((2, far_ref), (1, next_ref), (3, prev_ref)):
        part = jnp.dot(rows, weight_ref[:, columns_of(step, width)], preferred_element_type=F32)
        out_ref[...] = part.astype(BF)
    part = jnp.dot(rows, weight_ref[:, columns_of(0, width)], preferred_element_type=F32)
    own_ref[...] = part + resid_ref[:, columns_of(0, width)].astype(F32)


def project(owner, low, high, from_low, from_high, weight, resid):
    slots, model = resid.shape
    width = model // 4
    shape = jax.ShapeDtypeStruct
    return pl.pallas_call(
        project_kernel,
        name="project",
        out_shape=(
            shape((slots, width), F32),
            shape((slots, width), BF),
            shape((slots, width), BF),
            shape((slots, width), BF),
        ),
        in_specs=[SM] + [VM] * 6,
        out_specs=tuple([VM] * 4),
        scratch_shapes=[pltpu.VMEM((slots, 2 * DK), BF)],
        compiler_params=PARAMS,
        cost_estimate=pl.CostEstimate(
            flops=140_000_000, bytes_accessed=2_000_000, transcendentals=0
        ),
    )(owner, low, high, from_low, from_high, weight, resid)


def ffn_kernel(
    length_ref, own_ref, next_ref, far_ref, prev_ref, gain_ref, gate_ref, up_ref, down_ref,
    own_out_ref, next_out_ref, far_out_ref, prev_out_ref, normed_scr,
):
    width = own_ref.shape[1]
    parts = ((0, own_ref), (1, next_ref), (2, far_ref), (3, prev_ref))
    total = None
    for _, ref in parts:
        block = ref[...].astype(F32)
        square = jnp.sum(block * block, axis=-1, keepdims=True)
        total = square if total is None else total + square
    scale = lax.rsqrt(total / (4 * width) + 1e-05)
    for step, ref in parts:
        columns = columns_of(step, width)
        normed_scr[:, columns] = (ref[...].astype(F32) * scale * gain_ref[:, columns]).astype(BF)
    normed = normed_scr[...]
    dims = (((1,), (1,)), ((), ()))
    gate = lax.dot_general(normed, gate_ref[...], dims, preferred_element_type=F32)
    up = lax.dot_general(normed, up_ref[...], dims, preferred_element_type=F32)
    hidden = (gate * jax.nn.sigmoid(gate) * up).astype(BF)
    me = lax.axis_index("req")
    position = lax.broadcasted_iota(jnp.int32, (DRAFT, 1), 0)
    live = jnp.concatenate(
        [(position < length_ref[me * ROWS + row]).astype(F32) for row in range(ROWS)], axis=0
    )
    for step, out_ref in ((2, far_out_ref), (1, next_out_ref), (3, prev_out_ref)):
        part = jnp.dot(hidden, down_ref[:, columns_of(step, width)], preferred_element_type=F32)
        out_ref[...] = (part * live).astype(BF)
    part = jnp.dot(hidden, down_ref[:, columns_of(0, width)], preferred_element_type=F32)
    own_out_ref[...] = (part + own_ref[...].astype(F32)) * live


def ffn(lengths, own, following, far, preceding, gain, gate_t, up_t, down):
    slots, width = own.shape
    shape = jax.ShapeDtypeStruct
    return pl.pallas_call(
        ffn_kernel,
        name="ffn",
        out_shape=(
            shape((slots, width), F32),
            shape((slots, width), BF),
            shape((slots, width), BF),
            shape((slots, width), BF),
        ),
        in_specs=[SM] + [VM] * 8,
        out_specs=tuple([VM] * 4),
        scratch_shapes=[pltpu.VMEM((slots, 4 * width), BF)],
        compiler_params=PARAMS,
        cost_estimate=pl.CostEstimate(
            flops=1_100_000_000, bytes_accessed=9_000_000, transcendentals=100_000
        ),
    )(lengths, own, following, far, preceding, gain, gate_t, up_t, down)


def shifted(block, axis, step):
    count = lax.axis_size(axis)
    return lax.ppermute(block, axis, [(i, (i + step) % count) for i in range(count)])


def shards(
    mix_inputs,
    conv_weight,
    forget_bias,
    norm_gain,
    out_weight,
    resid,
    ffn_gain,
    gate_weight,
    up_weight,
    down_weight,
    held_states,
    held_edges,
    draft_lengths,
    accepted,
    owner_row,
):
    slots = ROWS * DRAFT
    lanes = 3 * DK
    low = shifted(mix_inputs[HALF:].reshape(HALF, 2 * DRAFT, lanes), "req", 1)
    high = shifted(mix_inputs[:HALF].reshape(HALF, 2 * DRAFT, lanes), "req", -1)
    own = mix_inputs.reshape(ROWS, 2 * DRAFT, lanes)
    edges = held_edges.reshape(ROWS, 6, lanes)
    mixed_low, mixed_high, values, weights, decay, edges_out = mixer(
        owner_row, accepted, own, low, high, edges, held_states,
        conv_weight, forget_bias, norm_gain,
    )
    from_low = shifted(mixed_high, "req", 1)
    from_high = shifted(mixed_low, "req", -1)
    kept_states = keep(held_states, values, weights, decay)
    kept_edges = edges_out.reshape(held_edges.shape)
    rows = resid.reshape(slots, resid.shape[2])
    own_part, to_next, to_far, to_prev = project(
        owner_row, mixed_low, mixed_high, from_low, from_high, out_weight, rows
    )
    far = shifted(to_far, "grp", 2)
    following = shifted(to_next, "grp", 1)
    preceding = shifted(to_prev, "grp", -1)
    stream = (
        own_part + far.astype(F32) + following.astype(F32) + preceding.astype(F32)
    ).astype(BF)
    far = shifted(stream, "grp", 2)
    preceding = shifted(stream, "grp", 1)
    following = shifted(stream, "grp", -1)
    own_part, to_next, to_far, to_prev = ffn(
        draft_lengths, stream, following, far, preceding, ffn_gain[None, :],
        gate_weight.T, up_weight.T, down_weight,
    )
    far = shifted(to_far, "grp", 2)
    following = shifted(to_next, "grp", 1)
    preceding = shifted(to_prev, "grp", -1)
    layer_out = (
        own_part + far.astype(F32) + following.astype(F32) + preceding.astype(F32)
    ).astype(BF)
    return (layer_out.reshape(ROWS, DRAFT, -1), kept_states, kept_edges)


def solution(mesh):
    return jax.shard_map(
        shards,
        mesh=mesh,
        in_specs=(
            P("req", None, "grp", None),
            P(None, "grp", None),
            P("grp", None),
            P("grp", None),
            P("grp", None),
            P("req", None, None),
            P(),
            P(None, "grp"),
            P(None, "grp"),
            P("grp", None),
            P("req", "grp", None, None),
            P("req", None, "grp", None),
            P(),
            P(),
            P(),
        ),
        out_specs=(P("req", None, "grp"), P("req", "grp", None, None), P("req", None, "grp", None)),
        check_vma=False,
    )
```

```python
import jax
import jax.numpy as jnp
from jax import lax
from jax.experimental import pallas as pl
from jax.experimental.pallas import tpu as pltpu
from jax.sharding import PartitionSpec as P

DK = 128
DRAFT = 16
CONV = 4
HALF = 4
ROWS = 2 * HALF
BF = jnp.bfloat16
PARAMS = pltpu.CompilerParams(vmem_limit_bytes=12 * 1024 * 1024)
F32 = jnp.float32
PACKED = 2 * DK + 3 * DRAFT
VM = pl.BlockSpec(memory_space=pltpu.VMEM)
SM = pl.BlockSpec(memory_space=pltpu.SMEM)
HB = pl.BlockSpec(memory_space=pltpu.HBM)


def source_of(owner_ref, row):
    me = lax.axis_index("req")
    partner = owner_ref[me * ROWS + row]
    local = partner // ROWS == me
    return partner, local, partner % HALF


def block_of(block):
    return slice(block * DK, (block + 1) * DK)


def call(kernel, out_shape, in_specs, scratch, flops, moved, *args):
    return pl.pallas_call(
        kernel,
        name=kernel.__name__,
        out_shape=out_shape,
        in_specs=in_specs,
        out_specs=jax.tree.map(lambda _: VM, out_shape),
        scratch_shapes=scratch,
        compiler_params=PARAMS,
        cost_estimate=pl.CostEstimate(flops=flops, bytes_accessed=moved, transcendentals=0),
    )(*args)


def pack(state_ref, edge_ref, low_ref, high_ref, states, edges, rows_scr, sems, edge_sem):
    copies = [
        pltpu.make_async_copy(state_ref.at[row], states.at[row], sems.at[row])
        for row in range(ROWS)
    ]
    edge_copy = pltpu.make_async_copy(edge_ref, edges, edge_sem)
    edge_copy.start()
    for copy in copies:
        copy.start()
    rows_scr[...] = jnp.zeros_like(rows_scr)
    edge_copy.wait()
    for row in range(ROWS):
        out_ref = low_ref if row < HALF else high_ref
        place = row % HALF
        for step in range(CONV - 1):
            both = edges[row, step].astype(F32)
            for block in range(3):
                rows_scr[row, block, 2 * step : 2 * step + 2, :] = both[:, block_of(block)]
        for block in range(3):
            start = 2 * DK + block * DRAFT
            out_ref[place, start : start + DRAFT, :] = rows_scr[row, block].astype(BF)
    for row in range(ROWS):
        out_ref = low_ref if row < HALF else high_ref
        copies[row].wait()
        for head in range(2):
            out_ref[row % HALF, block_of(head), :] = states[row, head].astype(BF)


def pack_call(states, edges):
    half = jax.ShapeDtypeStruct((HALF, PACKED, DK), BF)
    return call(
        pack, (half, half), [HB, HB],
        [
            pltpu.VMEM(states.shape, F32),
            pltpu.VMEM(edges.shape, BF),
            pltpu.VMEM((ROWS, 3, DRAFT, DK), F32),
            pltpu.SemaphoreType.DMA((ROWS,)),
            pltpu.SemaphoreType.DMA,
        ],
        1_000_000, 2_000_000, states, edges,
    )


def fill_window(window, row, drafts):
    for step in range(DRAFT):
        both = drafts[step].astype(F32)
        for block in range(3):
            window[row, block, 8 + 2 * step : 10 + 2 * step, :] = both[:, block_of(block)]


def convolve(window, conv_ref, row, head, block):
    total = None
    for shift in range(CONV):
        taps = conv_ref[shift, head, block_of(block)]
        rows = window[row, block, pl.ds(2 + 2 * shift + head, DRAFT, stride=2), :]
        term = taps[None, :] * rows
        total = term if total is None else total + term
    return total


def as_query(x):
    return x * jax.nn.sigmoid(x) * DK ** (-0.5)


def as_value(x):
    return x * jax.nn.sigmoid(x)


def prepare(
    draft_ref, conv_hbm, bias_hbm, gain_hbm, gate_hbm, up_hbm, down_hbm,
    query_ref, forget_ref, value_ref, conv_ref, bias_ref, gain_ref, gate_ref, up_ref, down_ref,
    drafts, window, sems,
):
    pairs = (
        (draft_ref, drafts), (conv_hbm, conv_ref), (bias_hbm, bias_ref), (gain_hbm, gain_ref),
        (gate_hbm, gate_ref), (up_hbm, up_ref), (down_hbm, down_ref),
    )
    copies = [
        pltpu.make_async_copy(src, dst, sems.at[i]) for i, (src, dst) in enumerate(pairs)
    ]
    for copy in copies:
        copy.start()
    window[...] = jnp.zeros_like(window)
    for copy in copies[:4]:
        copy.wait()
    for row in range(ROWS):
        fill_window(window, row, drafts[row])
    half = DRAFT // 2
    for row in range(ROWS):
        for head in range(2):
            queries, gates, values = [
                convolve(window, conv_ref, row, head, block) for block in range(3)
            ]
            query_ref[row, head, :half] = queries[:half]
            query_ref[row, head, half:] = as_query(queries[half:])
            gates = gates + bias_ref[head, :][None, :]
            forget_ref[row, head, :half] = gates[:half]
            forget_ref[row, head, half:] = jax.nn.sigmoid(gates[half:])
            value_ref[row, head, :half] = values[:half]
            value_ref[row, head, half:] = as_value(values[half:])
    for copy in copies[4:]:
        copy.wait()


def prepare_call(drafts, conv, bias, gain, gate_t, up_t, down):
    rows = jax.ShapeDtypeStruct((ROWS, 2, DRAFT, DK), F32)
    copied = [jax.ShapeDtypeStruct(x.shape, x.dtype) for x in (conv, bias, gain, gate_t, up_t, down)]
    return call(
        prepare, (rows, rows, rows, *copied), [HB] * 7,
        [
            pltpu.VMEM(drafts.shape, BF),
            pltpu.VMEM((ROWS, 3, 40, DK), F32),
            pltpu.SemaphoreType.DMA((7,)),
        ],
        5_000_000, 18_000_000, drafts, conv, bias, gain, gate_t, up_t, down,
    )


def mixer(
    owner_ref, low_ref, high_ref, from_low_ref, from_high_ref, query_ref, forget_ref, value_ref,
    conv_ref, bias_ref, gain_ref, mixed_ref, edges, states, query_scr, forget_scr, value_scr,
):
    half = DRAFT // 2
    edges[...] = jnp.zeros_like(edges)
    for row in range(ROWS):
        _, local, place = source_of(owner_ref, row)
        mine_ref, other_ref = (low_ref, from_low_ref) if row < HALF else (high_ref, from_high_ref)
        for block in range(3):
            start = 2 * DK + block * DRAFT
            mine = mine_ref[row % HALF, start : start + DRAFT, :].astype(F32)
            other = other_ref[place, start : start + DRAFT, :].astype(F32)
            edges[row, block, :DRAFT, :] = jnp.where(local, mine, other)

        @pl.when(local)
        def _():
            states[row] = mine_ref[row % HALF, : 2 * DK, :]

        @pl.when(jnp.logical_not(local))
        def _():
            states[row] = other_ref[place, : 2 * DK, :]

    sub_iota = lax.broadcasted_iota(jnp.int32, (1, DRAFT, DK), 1)

    def pair(step, _):
        base = step * 2
        for sub in range(2):
            row = base + sub
            for head in range(2):
                slot = sub * 2 + head
                for block, (in_ref, out, act) in enumerate(
                    (
                        (query_ref, query_scr, as_query),
                        (forget_ref, forget_scr, jax.nn.sigmoid),
                        (value_ref, value_scr, as_value),
                    )
                ):
                    first = in_ref[row, head, :half]
                    for shift in range(CONV - 1):
                        taps = conv_ref[shift, head, block_of(block)]
                        rows = edges[row, block, pl.ds(2 * shift + head, half, stride=2), :]
                        first = first + taps[None, :] * rows
                    out[slot, :half] = act(first)
                    out[slot, half:] = in_ref[row, head, half:]
        queries = query_scr[...]
        forget = forget_scr[...]
        values = value_scr[...]
        weights = jnp.zeros((4, DRAFT, DK), F32)
        decay = jnp.ones((4, 1, DK), F32)
        head_rows = []
        query_rows = []
        for t in range(DRAFT):
            forget_t = forget[:, t : t + 1, :]
            query_t = queries[:, t : t + 1, :]
            decay = decay * forget_t
            weights = jnp.where(sub_iota == t, 1.0 - forget_t, weights * forget_t)
            scores = jnp.sum(weights * query_t, axis=-1, keepdims=True)
            head_rows.append(jnp.sum(scores * values, axis=1, keepdims=True))
            query_rows.append(query_t * decay)
        local_out = jnp.concatenate(head_rows, axis=1)
        decayed = jnp.concatenate(query_rows, axis=1)
        for sub in range(2):
            row = base + sub
            for head in range(2):
                slot = sub * 2 + head
                fine = decayed[slot]
                coarse = fine.astype(BF)
                stacked = jnp.concatenate([coarse, (fine - coarse.astype(F32)).astype(BF)], axis=0)
                both = jnp.dot(
                    stacked, states[row, block_of(head), :], preferred_element_type=F32
                )
                out = local_out[slot] + (both[:DRAFT] + both[DRAFT:])
                scale = lax.rsqrt(jnp.mean(out * out, axis=-1, keepdims=True) + 1e-05)
                mixed_ref[row, :, block_of(head)] = (
                    out * scale * gain_ref[head, :][None, :]
                ).astype(BF)
        return 0

    lax.fori_loop(0, ROWS // 2, pair, 0)


def mixer_call(owner, low, high, from_low, from_high, queries, forget, values, conv, bias, gain):
    return call(
        mixer, jax.ShapeDtypeStruct((ROWS, DRAFT, 2 * DK), BF), [SM] + [VM] * 10,
        [
            pltpu.VMEM((ROWS, 3, 24, DK), F32),
            pltpu.VMEM((ROWS, 2 * DK, DK), BF),
            pltpu.VMEM((4, DRAFT, DK), F32),
            pltpu.VMEM((4, DRAFT, DK), F32),
            pltpu.VMEM((4, DRAFT, DK), F32),
        ],
        20_000_000, 2_000_000,
        owner, low, high, from_low, from_high, queries, forget, values, conv, bias, gain,
    )


def later(x, shift):
    return jnp.concatenate([x[shift:], jnp.ones((shift, DK), F32)], axis=0)


def keep(
    owner_ref, accept_ref, draft_ref, low_ref, high_ref, edge_ref, state_ref, conv_ref, bias_ref,
    kept_ref, edges_out_ref, drafts, edges, states, picked, window, sems,
):
    state_copies = [
        pltpu.make_async_copy(state_ref.at[row], states.at[row], sems.at[row])
        for row in range(ROWS)
    ]
    draft_copy = pltpu.make_async_copy(draft_ref, drafts, sems.at[ROWS])
    edge_copy = pltpu.make_async_copy(edge_ref, edges, sems.at[ROWS + 1])
    draft_copy.start()
    edge_copy.start()
    for copy in state_copies:
        copy.start()
    draft_copy.wait()
    edge_copy.wait()
    position = lax.broadcasted_iota(jnp.int32, (DRAFT, DK), 0)
    for row in range(ROWS):
        partner, local, place = source_of(owner_ref, row)
        other_ref = low_ref if row < HALF else high_ref

        @pl.when(local)
        def _():
            picked[row] = drafts[row]

        @pl.when(jnp.logical_not(local))
        def _():
            picked[row] = other_ref[place]

    for row in range(ROWS):
        fill_window(window, row, picked[row])
        for step in range(CONV - 1):
            both = edges[row, step].astype(F32)
            for block in range(3):
                window[row, block, 2 + 2 * step : 4 + 2 * step, :] = both[:, block_of(block)]
    for row in range(ROWS):
        partner, _, _ = source_of(owner_ref, row)
        length = accept_ref[partner]
        state_copies[row].wait()
        for head in range(2):
            gates = convolve(window, conv_ref, row, head, 1) + bias_ref[head, :][None, :]
            values = as_value(convolve(window, conv_ref, row, head, 2))
            forget = jax.nn.sigmoid(gates)
            inside = position < length
            weights = jnp.where(inside, 1.0 - forget, 0.0)
            factors = jnp.where(inside, forget, 1.0)
            after = later(factors, 1)
            for shift in (1, 2, 4, 8):
                after = after * later(after, shift)
            update = lax.dot_general(
                weights * after,
                values,
                (((0,), (0,)), ((), ())),
                preferred_element_type=F32,
                precision=lax.Precision.HIGHEST,
            )
            decay = (factors * after)[:1, :]
            column = jnp.transpose(jnp.broadcast_to(decay, (DK, DK)))
            kept_ref[row, head] = column * states[row, head] + update
        for block in range(3):
            turned = pltpu.roll(window[row, block], 38 - 2 * length, 0)
            for step in range(CONV - 1):
                edges_out_ref[row, step, :, block_of(block)] = turned[
                    2 * step : 2 * step + 2
                ].astype(BF)


def keep_call(owner, accept, drafts, low, high, edges, states, conv, bias):
    shape = jax.ShapeDtypeStruct
    return call(
        keep, (shape(states.shape, F32), shape(edges.shape, BF)),
        [SM, SM, HB, VM, VM, HB, HB, VM, VM],
        [
            pltpu.VMEM(drafts.shape, BF),
            pltpu.VMEM(edges.shape, BF),
            pltpu.VMEM(states.shape, F32),
            pltpu.VMEM(drafts.shape, BF),
            pltpu.VMEM((ROWS, 3, 40, DK), F32),
            pltpu.SemaphoreType.DMA((ROWS + 2,)),
        ],
        20_000_000, 3_000_000, owner, accept, drafts, low, high, edges, states, conv, bias,
    )


def columns_of(step, width):
    place = (lax.axis_index("grp") + step) % 4
    return pl.ds(pl.multiple_of(place * width, width), width)


def project_kernel(
    rows_ref, weight_ref, resid_ref, own_ref, next_ref, far_ref, prev_ref,
):
    width = own_ref.shape[1]
    rows = rows_ref[...]
    for step, out_ref in ((2, far_ref), (1, next_ref), (3, prev_ref)):
        part = jnp.dot(rows, weight_ref[:, columns_of(step, width)], preferred_element_type=F32)
        out_ref[...] = part.astype(BF)
    part = jnp.dot(rows, weight_ref[:, columns_of(0, width)], preferred_element_type=F32)
    own_ref[...] = part + resid_ref[:, columns_of(0, width)].astype(F32)


def project(rows, weight, resid):
    slots, model = resid.shape
    width = model // 4
    shape = jax.ShapeDtypeStruct
    return pl.pallas_call(
        project_kernel,
        name="project",
        out_shape=(
            shape((slots, width), F32),
            shape((slots, width), BF),
            shape((slots, width), BF),
            shape((slots, width), BF),
        ),
        in_specs=[VM] * 3,
        out_specs=tuple([VM] * 4),
        compiler_params=PARAMS,
        cost_estimate=pl.CostEstimate(
            flops=140_000_000, bytes_accessed=2_000_000, transcendentals=0
        ),
    )(rows, weight, resid)


def ffn_kernel(
    length_ref, own_ref, next_ref, far_ref, prev_ref, gain_ref, gate_ref, up_ref, down_ref,
    own_out_ref, next_out_ref, far_out_ref, prev_out_ref, normed_scr,
):
    width = own_ref.shape[1]
    parts = ((0, own_ref), (1, next_ref), (2, far_ref), (3, prev_ref))
    total = None
    for _, ref in parts:
        block = ref[...].astype(F32)
        square = jnp.sum(block * block, axis=-1, keepdims=True)
        total = square if total is None else total + square
    scale = lax.rsqrt(total / (4 * width) + 1e-05)
    for step, ref in parts:
        columns = columns_of(step, width)
        normed_scr[:, columns] = (ref[...].astype(F32) * scale * gain_ref[:, columns]).astype(BF)
    normed = normed_scr[...]
    dims = (((1,), (1,)), ((), ()))
    gate = lax.dot_general(normed, gate_ref[...], dims, preferred_element_type=F32)
    up = lax.dot_general(normed, up_ref[...], dims, preferred_element_type=F32)
    hidden = (gate * jax.nn.sigmoid(gate) * up).astype(BF)
    me = lax.axis_index("req")
    position = lax.broadcasted_iota(jnp.int32, (DRAFT, 1), 0)
    live = jnp.concatenate(
        [(position < length_ref[me * ROWS + row]).astype(F32) for row in range(ROWS)], axis=0
    )
    for step, out_ref in ((2, far_out_ref), (1, next_out_ref), (3, prev_out_ref)):
        part = jnp.dot(hidden, down_ref[:, columns_of(step, width)], preferred_element_type=F32)
        out_ref[...] = (part * live).astype(BF)
    part = jnp.dot(hidden, down_ref[:, columns_of(0, width)], preferred_element_type=F32)
    own_out_ref[...] = (part + own_ref[...].astype(F32)) * live


def ffn(lengths, own, following, far, preceding, gain, gate_t, up_t, down):
    slots, width = own.shape
    shape = jax.ShapeDtypeStruct
    return pl.pallas_call(
        ffn_kernel,
        name="ffn",
        out_shape=(
            shape((slots, width), F32),
            shape((slots, width), BF),
            shape((slots, width), BF),
            shape((slots, width), BF),
        ),
        in_specs=[SM] + [VM] * 8,
        out_specs=tuple([VM] * 4),
        scratch_shapes=[pltpu.VMEM((slots, 4 * width), BF)],
        compiler_params=PARAMS,
        cost_estimate=pl.CostEstimate(
            flops=1_100_000_000, bytes_accessed=9_000_000, transcendentals=100_000
        ),
    )(lengths, own, following, far, preceding, gain, gate_t, up_t, down)


def shifted(block, axis, step):
    count = lax.axis_size(axis)
    return lax.ppermute(block, axis, [(i, (i + step) % count) for i in range(count)])


def shards(
    mix_inputs,
    conv_weight,
    forget_bias,
    norm_gain,
    out_weight,
    resid,
    ffn_gain,
    gate_weight,
    up_weight,
    down_weight,
    held_states,
    held_edges,
    draft_lengths,
    accepted,
    owner_row,
):
    slots = ROWS * DRAFT
    low, high = pack_call(held_states, held_edges)
    from_low = shifted(high, "req", 1)
    from_high = shifted(low, "req", -1)
    queries, forget, values, conv, bias, gain, gate_t, up_t, down = prepare_call(
        mix_inputs, conv_weight, forget_bias, norm_gain,
        gate_weight.T, up_weight.T, down_weight,
    )
    mixed = mixer_call(
        owner_row, low, high, from_low, from_high, queries, forget, values, conv, bias, gain
    )
    drafts_low = shifted(mix_inputs[HALF:], "req", 1)
    drafts_high = shifted(mix_inputs[:HALF], "req", -1)
    kept_states, kept_edges = keep_call(
        owner_row, accepted, mix_inputs, drafts_low, drafts_high, held_edges, held_states,
        conv, bias,
    )
    own_part, to_next, to_far, to_prev = project(
        mixed.reshape(slots, -1), out_weight, resid.reshape(slots, -1)
    )
    far = shifted(to_far, "grp", 2)
    following = shifted(to_next, "grp", 1)
    preceding = shifted(to_prev, "grp", -1)
    stream = (
        own_part + far.astype(F32) + following.astype(F32) + preceding.astype(F32)
    ).astype(BF)
    far = shifted(stream, "grp", 2)
    preceding = shifted(stream, "grp", 1)
    following = shifted(stream, "grp", -1)
    own_part, to_next, to_far, to_prev = ffn(
        draft_lengths, stream, following, far, preceding, ffn_gain[None, :], gate_t, up_t, down
    )
    far = shifted(to_far, "grp", 2)
    following = shifted(to_next, "grp", 1)
    preceding = shifted(to_prev, "grp", -1)
    layer_out = (
        own_part + far.astype(F32) + following.astype(F32) + preceding.astype(F32)
    ).astype(BF)
    return (layer_out.reshape(ROWS, DRAFT, -1), kept_states, kept_edges)


def solution(mesh):
    return jax.shard_map(
        shards,
        mesh=mesh,
        in_specs=(
            P("req", None, "grp", None),
            P(None, "grp", None),
            P("grp", None),
            P("grp", None),
            P("grp", None),
            P("req", None, None),
            P(),
            P(None, "grp"),
            P(None, "grp"),
            P("grp", None),
            P("req", "grp", None, None),
            P("req", None, "grp", None),
            P(),
            P(),
            P(),
        ),
        out_specs=(P("req", None, "grp"), P("req", "grp", None, None), P("req", None, "grp", None)),
        check_vma=False,
    )
```

```python
import jax
import jax.numpy as jnp
from jax import lax
from jax.experimental import pallas as pl
from jax.experimental.pallas import tpu as pltpu
from jax.sharding import PartitionSpec as P

DK = 128
DRAFT = 16
CONV = 4
HALF = 4
ROWS = 2 * HALF
BF = jnp.bfloat16
PARAMS = pltpu.CompilerParams(vmem_limit_bytes=12 * 1024 * 1024)
F32 = jnp.float32
PACKED = 2 * DK + 3 * DRAFT
VM = pl.BlockSpec(memory_space=pltpu.VMEM)
SM = pl.BlockSpec(memory_space=pltpu.SMEM)
HB = pl.BlockSpec(memory_space=pltpu.HBM)


def source_of(owner_ref, row):
    me = lax.axis_index("req")
    partner = owner_ref[me * ROWS + row]
    local = partner // ROWS == me
    return partner, local, partner % HALF


def block_of(block):
    return slice(block * DK, (block + 1) * DK)


def call(kernel, out_shape, in_specs, scratch, flops, moved, *args):
    return pl.pallas_call(
        kernel,
        name=kernel.__name__,
        out_shape=out_shape,
        in_specs=in_specs,
        out_specs=jax.tree.map(lambda _: VM, out_shape),
        scratch_shapes=scratch,
        compiler_params=PARAMS,
        cost_estimate=pl.CostEstimate(flops=flops, bytes_accessed=moved, transcendentals=0),
    )(*args)


def pack(state_ref, edge_ref, low_ref, high_ref, states, edges, rows_scr, sems, edge_sem):
    copies = [
        pltpu.make_async_copy(state_ref.at[row], states.at[row], sems.at[row])
        for row in range(ROWS)
    ]
    edge_copy = pltpu.make_async_copy(edge_ref, edges, edge_sem)
    edge_copy.start()
    for copy in copies:
        copy.start()
    rows_scr[...] = jnp.zeros_like(rows_scr)
    edge_copy.wait()
    for row in range(ROWS):
        out_ref = low_ref if row < HALF else high_ref
        place = row % HALF
        for step in range(CONV - 1):
            both = edges[row, step].astype(F32)
            for block in range(3):
                rows_scr[row, block, 2 * step : 2 * step + 2, :] = both[:, block_of(block)]
        for block in range(3):
            start = 2 * DK + block * DRAFT
            out_ref[place, start : start + DRAFT, :] = rows_scr[row, block].astype(BF)
    for row in range(ROWS):
        out_ref = low_ref if row < HALF else high_ref
        copies[row].wait()
        for head in range(2):
            out_ref[row % HALF, block_of(head), :] = states[row, head].astype(BF)


def pack_call(states, edges):
    half = jax.ShapeDtypeStruct((HALF, PACKED, DK), BF)
    return call(
        pack, (half, half), [HB, HB],
        [
            pltpu.VMEM(states.shape, F32),
            pltpu.VMEM(edges.shape, BF),
            pltpu.VMEM((ROWS, 3, DRAFT, DK), F32),
            pltpu.SemaphoreType.DMA((ROWS,)),
            pltpu.SemaphoreType.DMA,
        ],
        1_000_000, 2_000_000, states, edges,
    )


def fill_window(window, row, drafts):
    for step in range(DRAFT):
        both = drafts[step].astype(F32)
        for block in range(3):
            window[row, block, 8 + 2 * step : 10 + 2 * step, :] = both[:, block_of(block)]


def convolve(window, conv_ref, row, head, block):
    total = None
    for shift in range(CONV):
        taps = conv_ref[shift, head, block_of(block)]
        rows = window[row, block, pl.ds(2 + 2 * shift + head, DRAFT, stride=2), :]
        term = taps[None, :] * rows
        total = term if total is None else total + term
    return total


def as_query(x):
    return x * jax.nn.sigmoid(x) * DK ** (-0.5)


def as_value(x):
    return x * jax.nn.sigmoid(x)


def prepare(
    draft_ref, conv_hbm, bias_hbm, gain_hbm, gate_hbm, up_hbm, down_hbm,
    query_ref, forget_ref, value_ref, conv_ref, bias_ref, gain_ref, gate_ref, up_ref, down_ref,
    drafts, window, sems,
):
    pairs = (
        (draft_ref, drafts), (conv_hbm, conv_ref), (bias_hbm, bias_ref), (gain_hbm, gain_ref),
        (gate_hbm, gate_ref), (up_hbm, up_ref), (down_hbm, down_ref),
    )
    copies = [
        pltpu.make_async_copy(src, dst, sems.at[i]) for i, (src, dst) in enumerate(pairs)
    ]
    for copy in copies:
        copy.start()
    window[...] = jnp.zeros_like(window)
    for copy in copies[:4]:
        copy.wait()
    for row in range(ROWS):
        fill_window(window, row, drafts[row])
    half = DRAFT // 2
    for row in range(ROWS):
        for head in range(2):
            queries, gates, values = [
                convolve(window, conv_ref, row, head, block) for block in range(3)
            ]
            query_ref[row, head, :half] = queries[:half]
            query_ref[row, head, half:] = as_query(queries[half:])
            gates = gates + bias_ref[head, :][None, :]
            forget_ref[row, head, :half] = gates[:half]
            forget_ref[row, head, half:] = jax.nn.sigmoid(gates[half:])
            value_ref[row, head, :half] = values[:half]
            value_ref[row, head, half:] = as_value(values[half:])
    for copy in copies[4:]:
        copy.wait()


def prepare_call(drafts, conv, bias, gain, gate_t, up_t, down):
    rows = jax.ShapeDtypeStruct((ROWS, 2, DRAFT, DK), F32)
    copied = [jax.ShapeDtypeStruct(x.shape, x.dtype) for x in (conv, bias, gain, gate_t, up_t, down)]
    return call(
        prepare, (rows, rows, rows, *copied), [HB] * 7,
        [
            pltpu.VMEM(drafts.shape, BF),
            pltpu.VMEM((ROWS, 3, 40, DK), F32),
            pltpu.SemaphoreType.DMA((7,)),
        ],
        5_000_000, 18_000_000, drafts, conv, bias, gain, gate_t, up_t, down,
    )


def mixer(
    owner_ref, low_ref, high_ref, from_low_ref, from_high_ref, query_ref, forget_ref, value_ref,
    conv_ref, bias_ref, gain_ref, mixed_ref, edges, states, query_scr, forget_scr, value_scr,
):
    half = DRAFT // 2
    edges[...] = jnp.zeros_like(edges)
    for row in range(ROWS):
        _, local, place = source_of(owner_ref, row)
        mine_ref, other_ref = (low_ref, from_low_ref) if row < HALF else (high_ref, from_high_ref)
        for block in range(3):
            start = 2 * DK + block * DRAFT
            mine = mine_ref[row % HALF, start : start + DRAFT, :].astype(F32)
            other = other_ref[place, start : start + DRAFT, :].astype(F32)
            edges[row, block, :DRAFT, :] = jnp.where(local, mine, other)

        @pl.when(local)
        def _():
            states[row] = mine_ref[row % HALF, : 2 * DK, :]

        @pl.when(jnp.logical_not(local))
        def _():
            states[row] = other_ref[place, : 2 * DK, :]

    sub_iota = lax.broadcasted_iota(jnp.int32, (1, DRAFT, DK), 1)

    def pair(step, _):
        base = step * 2
        for sub in range(2):
            row = base + sub
            for head in range(2):
                slot = sub * 2 + head
                for block, (in_ref, out, act) in enumerate(
                    (
                        (query_ref, query_scr, as_query),
                        (forget_ref, forget_scr, jax.nn.sigmoid),
                        (value_ref, value_scr, as_value),
                    )
                ):
                    first = in_ref[row, head, :half]
                    for shift in range(CONV - 1):
                        taps = conv_ref[shift, head, block_of(block)]
                        rows = edges[row, block, pl.ds(2 * shift + head, half, stride=2), :]
                        first = first + taps[None, :] * rows
                    out[slot, :half] = act(first)
                    out[slot, half:] = in_ref[row, head, half:]
        queries = query_scr[...]
        forget = forget_scr[...]
        values = value_scr[...]
        weights = jnp.zeros((4, DRAFT, DK), F32)
        decay = jnp.ones((4, 1, DK), F32)
        head_rows = []
        query_rows = []
        for t in range(DRAFT):
            forget_t = forget[:, t : t + 1, :]
            query_t = queries[:, t : t + 1, :]
            decay = decay * forget_t
            weights = jnp.where(sub_iota == t, 1.0 - forget_t, weights * forget_t)
            scores = jnp.sum(weights * query_t, axis=-1, keepdims=True)
            head_rows.append(jnp.sum(scores * values, axis=1, keepdims=True))
            query_rows.append(query_t * decay)
        local_out = jnp.concatenate(head_rows, axis=1)
        decayed = jnp.concatenate(query_rows, axis=1)
        for sub in range(2):
            row = base + sub
            for head in range(2):
                slot = sub * 2 + head
                fine = decayed[slot]
                coarse = fine.astype(BF)
                stacked = jnp.concatenate([coarse, (fine - coarse.astype(F32)).astype(BF)], axis=0)
                both = jnp.dot(
                    stacked, states[row, block_of(head), :], preferred_element_type=F32
                )
                out = local_out[slot] + (both[:DRAFT] + both[DRAFT:])
                scale = lax.rsqrt(jnp.mean(out * out, axis=-1, keepdims=True) + 1e-05)
                mixed_ref[row, :, block_of(head)] = (
                    out * scale * gain_ref[head, :][None, :]
                ).astype(BF)
        return 0

    lax.fori_loop(0, ROWS // 2, pair, 0)


def mixer_call(owner, low, high, from_low, from_high, queries, forget, values, conv, bias, gain):
    return call(
        mixer, jax.ShapeDtypeStruct((ROWS, DRAFT, 2 * DK), BF), [SM] + [VM] * 10,
        [
            pltpu.VMEM((ROWS, 3, 24, DK), F32),
            pltpu.VMEM((ROWS, 2 * DK, DK), BF),
            pltpu.VMEM((4, DRAFT, DK), F32),
            pltpu.VMEM((4, DRAFT, DK), F32),
            pltpu.VMEM((4, DRAFT, DK), F32),
        ],
        20_000_000, 2_000_000,
        owner, low, high, from_low, from_high, queries, forget, values, conv, bias, gain,
    )


def later(x, shift):
    return jnp.concatenate([x[shift:], jnp.ones((shift, DK), F32)], axis=0)


def keep(
    owner_ref, accept_ref, draft_ref, low_ref, high_ref, edge_ref, state_ref, conv_ref, bias_ref,
    kept_ref, edges_out_ref, drafts, edges, states, picked, window, sems,
):
    state_copies = [
        pltpu.make_async_copy(state_ref.at[row], states.at[row], sems.at[row])
        for row in range(ROWS)
    ]
    draft_copy = pltpu.make_async_copy(draft_ref, drafts, sems.at[ROWS])
    edge_copy = pltpu.make_async_copy(edge_ref, edges, sems.at[ROWS + 1])
    draft_copy.start()
    edge_copy.start()
    for copy in state_copies:
        copy.start()
    draft_copy.wait()
    edge_copy.wait()
    position = lax.broadcasted_iota(jnp.int32, (DRAFT, DK), 0)
    for row in range(ROWS):
        partner, local, place = source_of(owner_ref, row)
        other_ref = low_ref if row < HALF else high_ref

        @pl.when(local)
        def _():
            picked[row] = drafts[row]

        @pl.when(jnp.logical_not(local))
        def _():
            picked[row] = other_ref[place]

    for row in range(ROWS):
        fill_window(window, row, picked[row])
        for step in range(CONV - 1):
            both = edges[row, step].astype(F32)
            for block in range(3):
                window[row, block, 2 + 2 * step : 4 + 2 * step, :] = both[:, block_of(block)]
    for row in range(ROWS):
        partner, _, _ = source_of(owner_ref, row)
        length = accept_ref[partner]
        state_copies[row].wait()
        for head in range(2):
            gates = convolve(window, conv_ref, row, head, 1) + bias_ref[head, :][None, :]
            values = as_value(convolve(window, conv_ref, row, head, 2))
            forget = jax.nn.sigmoid(gates)
            inside = position < length
            weights = jnp.where(inside, 1.0 - forget, 0.0)
            factors = jnp.where(inside, forget, 1.0)
            after = later(factors, 1)
            for shift in (1, 2, 4, 8):
                after = after * later(after, shift)
            update = lax.dot_general(
                weights * after,
                values,
                (((0,), (0,)), ((), ())),
                preferred_element_type=F32,
                precision=lax.Precision.HIGHEST,
            )
            decay = (factors * after)[:1, :]
            column = jnp.transpose(jnp.broadcast_to(decay, (DK, DK)))
            kept_ref[row, head] = column * states[row, head] + update
        for block in range(3):
            turned = pltpu.roll(window[row, block], 38 - 2 * length, 0)
            for step in range(CONV - 1):
                edges_out_ref[row, step, :, block_of(block)] = turned[
                    2 * step : 2 * step + 2
                ].astype(BF)


def keep_call(owner, accept, drafts, low, high, edges, states, conv, bias):
    shape = jax.ShapeDtypeStruct
    return call(
        keep, (shape(states.shape, F32), shape(edges.shape, BF)),
        [SM, SM, HB, VM, VM, HB, HB, VM, VM],
        [
            pltpu.VMEM(drafts.shape, BF),
            pltpu.VMEM(edges.shape, BF),
            pltpu.VMEM(states.shape, F32),
            pltpu.VMEM(drafts.shape, BF),
            pltpu.VMEM((ROWS, 3, 40, DK), F32),
            pltpu.SemaphoreType.DMA((ROWS + 2,)),
        ],
        20_000_000, 3_000_000, owner, accept, drafts, low, high, edges, states, conv, bias,
    )


def columns_of(step, width):
    place = lax.bitwise_xor(lax.axis_index("grp"), step)
    return pl.ds(pl.multiple_of(place * width, width), width)


def project_kernel(
    rows_ref, weight_ref, resid_ref, own_ref, next_ref, far_ref, prev_ref,
):
    width = own_ref.shape[1]
    rows = rows_ref[...]
    for step, out_ref in ((2, far_ref), (1, next_ref), (3, prev_ref)):
        part = jnp.dot(rows, weight_ref[:, columns_of(step, width)], preferred_element_type=F32)
        out_ref[...] = part.astype(BF)
    part = jnp.dot(rows, weight_ref[:, columns_of(0, width)], preferred_element_type=F32)
    own_ref[...] = part + resid_ref[:, columns_of(0, width)].astype(F32)


def project(rows, weight, resid):
    slots, model = resid.shape
    width = model // 4
    shape = jax.ShapeDtypeStruct
    return pl.pallas_call(
        project_kernel,
        name="project",
        out_shape=(
            shape((slots, width), F32),
            shape((slots, width), BF),
            shape((slots, width), BF),
            shape((slots, width), BF),
        ),
        in_specs=[VM] * 3,
        out_specs=tuple([VM] * 4),
        compiler_params=PARAMS,
        cost_estimate=pl.CostEstimate(
            flops=140_000_000, bytes_accessed=2_000_000, transcendentals=0
        ),
    )(rows, weight, resid)


def ffn_kernel(
    length_ref, own_ref, next_ref, far_ref, prev_ref, gain_ref, gate_ref, up_ref, down_ref,
    own_out_ref, next_out_ref, far_out_ref, prev_out_ref, normed_scr,
):
    width = own_ref.shape[1]
    parts = ((0, own_ref), (1, next_ref), (2, far_ref), (3, prev_ref))
    total = None
    for _, ref in parts:
        block = ref[...].astype(F32)
        square = jnp.sum(block * block, axis=-1, keepdims=True)
        total = square if total is None else total + square
    scale = lax.rsqrt(total / (4 * width) + 1e-05)
    for step, ref in parts:
        columns = columns_of(step, width)
        normed_scr[:, columns] = (ref[...].astype(F32) * scale * gain_ref[:, columns]).astype(BF)
    normed = normed_scr[...]
    dims = (((1,), (1,)), ((), ()))
    gate = lax.dot_general(normed, gate_ref[...], dims, preferred_element_type=F32)
    up = lax.dot_general(normed, up_ref[...], dims, preferred_element_type=F32)
    hidden = (gate * jax.nn.sigmoid(gate) * up).astype(BF)
    me = lax.axis_index("req")
    position = lax.broadcasted_iota(jnp.int32, (DRAFT, 1), 0)
    live = jnp.concatenate(
        [(position < length_ref[me * ROWS + row]).astype(F32) for row in range(ROWS)], axis=0
    )
    for step, out_ref in ((2, far_out_ref), (1, next_out_ref), (3, prev_out_ref)):
        part = jnp.dot(hidden, down_ref[:, columns_of(step, width)], preferred_element_type=F32)
        out_ref[...] = (part * live).astype(BF)
    part = jnp.dot(hidden, down_ref[:, columns_of(0, width)], preferred_element_type=F32)
    own_out_ref[...] = (part + own_ref[...].astype(F32)) * live


def ffn(lengths, own, following, far, preceding, gain, gate_t, up_t, down):
    slots, width = own.shape
    shape = jax.ShapeDtypeStruct
    return pl.pallas_call(
        ffn_kernel,
        name="ffn",
        out_shape=(
            shape((slots, width), F32),
            shape((slots, width), BF),
            shape((slots, width), BF),
            shape((slots, width), BF),
        ),
        in_specs=[SM] + [VM] * 8,
        out_specs=tuple([VM] * 4),
        scratch_shapes=[pltpu.VMEM((slots, 4 * width), BF)],
        compiler_params=PARAMS,
        cost_estimate=pl.CostEstimate(
            flops=1_100_000_000, bytes_accessed=9_000_000, transcendentals=100_000
        ),
    )(lengths, own, following, far, preceding, gain, gate_t, up_t, down)


def in_hbm(array):
    return pltpu.with_memory_space_constraint(array, pltpu.HBM)


def swapped(block, step):
    return lax.ppermute(block, "grp", [(i, i ^ step) for i in range(4)])


def shifted(block, axis, step):
    count = lax.axis_size(axis)
    return lax.ppermute(block, axis, [(i, (i + step) % count) for i in range(count)])


def shards(
    mix_inputs,
    conv_weight,
    forget_bias,
    norm_gain,
    out_weight,
    resid,
    ffn_gain,
    gate_weight,
    up_weight,
    down_weight,
    held_states,
    held_edges,
    draft_lengths,
    accepted,
    owner_row,
):
    slots = ROWS * DRAFT
    drafts = in_hbm(mix_inputs)
    states = in_hbm(held_states)
    held = in_hbm(held_edges)
    low, high = pack_call(states, held)
    from_low = shifted(high, "req", 1)
    from_high = shifted(low, "req", -1)
    drafts_low = shifted(mix_inputs[HALF:], "req", 1)
    drafts_high = shifted(mix_inputs[:HALF], "req", -1)
    queries, forget, values, conv, bias, gain, gate_t, up_t, down = prepare_call(
        drafts, in_hbm(conv_weight), in_hbm(forget_bias), in_hbm(norm_gain),
        in_hbm(gate_weight.T), in_hbm(up_weight.T), in_hbm(down_weight),
    )
    mixed = mixer_call(
        owner_row, low, high, from_low, from_high, queries, forget, values, conv, bias, gain
    )
    mixed, drafts_low, drafts_high = lax.optimization_barrier((mixed, drafts_low, drafts_high))
    own_part, to_one, to_two, to_three = project(
        mixed.reshape(slots, -1), out_weight, resid.reshape(slots, -1)
    )
    two = swapped(to_two, 2)
    one = swapped(to_one, 1)
    three = swapped(to_three, 3)
    stream = (own_part + two.astype(F32) + one.astype(F32) + three.astype(F32)).astype(BF)
    stream, drafts_low, drafts_high = lax.optimization_barrier((stream, drafts_low, drafts_high))
    two = swapped(stream, 2)
    one = swapped(stream, 1)
    three = swapped(stream, 3)
    kept_states, kept_edges = keep_call(
        owner_row, accepted, drafts, drafts_low, drafts_high, held, states, conv, bias
    )
    one, two, three, kept_states, kept_edges = lax.optimization_barrier(
        (one, two, three, kept_states, kept_edges)
    )
    own_part, to_one, to_two, to_three = ffn(
        draft_lengths, stream, one, two, three, ffn_gain[None, :], gate_t, up_t, down
    )
    two = swapped(to_two, 2)
    one = swapped(to_one, 1)
    three = swapped(to_three, 3)
    layer_out = (own_part + two.astype(F32) + one.astype(F32) + three.astype(F32)).astype(BF)
    return (layer_out.reshape(ROWS, DRAFT, -1), kept_states, kept_edges)


def solution(mesh):
    return jax.shard_map(
        shards,
        mesh=mesh,
        in_specs=(
            P("req", None, "grp", None),
            P(None, "grp", None),
            P("grp", None),
            P("grp", None),
            P("grp", None),
            P("req", None, None),
            P(),
            P(None, "grp"),
            P(None, "grp"),
            P("grp", None),
            P("req", "grp", None, None),
            P("req", None, "grp", None),
            P(),
            P(),
            P(),
        ),
        out_specs=(P("req", None, "grp"), P("req", "grp", None, None), P("req", None, "grp", None)),
        check_vma=False,
    )
```

```python
import jax
import jax.numpy as jnp
from jax import lax
from jax.experimental import pallas as pl
from jax.experimental.pallas import tpu as pltpu
from jax.sharding import PartitionSpec as P

DK = 128
DRAFT = 16
CONV = 4
HALF = 4
ROWS = 2 * HALF
BF = jnp.bfloat16
PARAMS = pltpu.CompilerParams(vmem_limit_bytes=12 * 1024 * 1024)
F32 = jnp.float32
EDGES_AT = 2 * DK
DRAFTS_AT = EDGES_AT + 3 * DRAFT
PACKED = DRAFTS_AT + 3 * 2 * DRAFT
VM = pl.BlockSpec(memory_space=pltpu.VMEM)
SM = pl.BlockSpec(memory_space=pltpu.SMEM)
HB = pl.BlockSpec(memory_space=pltpu.HBM)


def row_of(half, place):
    parity = lax.axis_index("req") % 2
    base = (1 - parity if half == 0 else parity) * HALF
    return base + place


def source_of(owner_ref, row):
    me = lax.axis_index("req")
    partner = owner_ref[me * ROWS + row]
    return partner, partner // ROWS == me, partner % HALF


def block_of(block):
    return slice(block * DK, (block + 1) * DK)


def edges_of(block):
    return slice(EDGES_AT + block * DRAFT, EDGES_AT + (block + 1) * DRAFT)


def drafts_of(block):
    return slice(DRAFTS_AT + block * 2 * DRAFT, DRAFTS_AT + (block + 1) * 2 * DRAFT)


def call(kernel, out_shape, in_specs, scratch, flops, moved, *args):
    return pl.pallas_call(
        kernel,
        name=kernel.__name__,
        out_shape=out_shape,
        in_specs=in_specs,
        out_specs=jax.tree.map(lambda _: VM, out_shape),
        scratch_shapes=scratch,
        compiler_params=PARAMS,
        cost_estimate=pl.CostEstimate(flops=flops, bytes_accessed=moved, transcendentals=0),
    )(*args)


def pack(state_ref, edge_ref, draft_ref, far_ref, near_ref, states, edges, drafts, sems):
    copies = [
        pltpu.make_async_copy(state_ref.at[row], states.at[row], sems.at[row])
        for row in range(ROWS)
    ]
    edge_copy = pltpu.make_async_copy(edge_ref, edges, sems.at[ROWS])
    draft_copy = pltpu.make_async_copy(draft_ref, drafts, sems.at[ROWS + 1])
    draft_copy.start()
    edge_copy.start()
    for copy in copies:
        copy.start()
    edge_copy.wait()
    draft_copy.wait()
    for half, out_ref in ((1, far_ref), (0, near_ref)):
        for place in range(HALF):
            row = row_of(half, place)
            for block in range(3):
                columns = block_of(block)
                out_ref[place, edges_of(block), :] = jnp.zeros((DRAFT, DK), BF)
                start = EDGES_AT + block * DRAFT
                for step in range(CONV - 1):
                    out_ref[place, start + 2 * step : start + 2 * step + 2, :] = edges[
                        row, step, :, columns
                    ]
                start = DRAFTS_AT + block * 2 * DRAFT
                for step in range(DRAFT):
                    out_ref[place, start + 2 * step : start + 2 * step + 2, :] = drafts[
                        row, step, :, columns
                    ]
    for copy in copies:
        copy.wait()
    for half, out_ref in ((1, far_ref), (0, near_ref)):
        for place in range(HALF):
            for head in range(2):
                out_ref[place, block_of(head), :] = states[row_of(half, place), head].astype(BF)


def pack_call(states, edges, drafts):
    half = jax.ShapeDtypeStruct((HALF, PACKED, DK), BF)
    return call(
        pack, (half, half), [HB] * 3,
        [
            pltpu.VMEM(states.shape, F32),
            pltpu.VMEM(edges.shape, BF),
            pltpu.VMEM(drafts.shape, BF),
            pltpu.SemaphoreType.DMA((ROWS + 2,)),
        ],
        1_000_000, 2_000_000, states, edges, drafts,
    )


def convolve(window, conv_ref, slot, head, block):
    total = None
    for shift in range(CONV):
        taps = conv_ref[shift, head, block_of(block)]
        rows = window[slot, block, pl.ds(2 + 2 * shift + head, DRAFT, stride=2), :]
        term = taps[None, :] * rows
        total = term if total is None else total + term
    return total


def as_query(x):
    return x * jax.nn.sigmoid(x) * DK ** (-0.5)


def as_value(x):
    return x * jax.nn.sigmoid(x)


def prepare(
    near_ref, far_ref, conv_hbm, bias_hbm, gain_hbm,
    query_ref, forget_ref, value_ref, conv_ref, bias_ref, gain_ref, window, sems,
):
    pairs = ((conv_hbm, conv_ref), (bias_hbm, bias_ref), (gain_hbm, gain_ref))
    copies = [
        pltpu.make_async_copy(src, dst, sems.at[i]) for i, (src, dst) in enumerate(pairs)
    ]
    for copy in copies:
        copy.start()
    for slot in range(ROWS):
        own_ref = near_ref if slot < HALF else far_ref
        for block in range(3):
            window[slot, block, :8, :] = jnp.zeros((8, DK), F32)
            window[slot, block, 8:, :] = own_ref[slot % HALF, drafts_of(block), :].astype(F32)
    for copy in copies:
        copy.wait()
    half = DRAFT // 2
    for slot in range(ROWS):
        for head in range(2):
            queries, gates, values = [
                convolve(window, conv_ref, slot, head, block) for block in range(3)
            ]
            query_ref[slot, head, :half] = queries[:half]
            query_ref[slot, head, half:] = as_query(queries[half:])
            gates = gates + bias_ref[head, :][None, :]
            forget_ref[slot, head, :half] = gates[:half]
            forget_ref[slot, head, half:] = jax.nn.sigmoid(gates[half:])
            value_ref[slot, head, :half] = values[:half]
            value_ref[slot, head, half:] = as_value(values[half:])


def prepare_call(near, far, conv, bias, gain):
    rows = jax.ShapeDtypeStruct((ROWS, 2, DRAFT, DK), F32)
    copied = [jax.ShapeDtypeStruct(x.shape, x.dtype) for x in (conv, bias, gain)]
    return call(
        prepare, (rows, rows, rows, *copied), [VM, VM, HB, HB, HB],
        [pltpu.VMEM((ROWS, 3, 40, DK), F32), pltpu.SemaphoreType.DMA((3,))],
        5_000_000, 3_000_000, near, far, conv, bias, gain,
    )


def fetch(*refs):
    count = len(refs) // 2
    sems = refs[-1]
    copies = [
        pltpu.make_async_copy(refs[i], refs[count + i], sems.at[i]) for i in range(count)
    ]
    for copy in copies:
        copy.start()
    for copy in copies:
        copy.wait()


def fetch_call(*arrays):
    return call(
        fetch, tuple(jax.ShapeDtypeStruct(x.shape, x.dtype) for x in arrays), [HB] * len(arrays),
        [pltpu.SemaphoreType.DMA((len(arrays),))], 0, 17_000_000, *arrays,
    )


def mixer(
    owner_ref, near_ref, far_ref, from_near_ref, from_far_ref, query_ref, forget_ref, value_ref,
    conv_ref, bias_ref, gain_ref, mixed_ref, edges, states, query_scr, forget_scr, value_scr,
):
    half = DRAFT // 2
    for slot in range(ROWS):
        side = slot // HALF
        _, local, place = source_of(owner_ref, row_of(side, slot % HALF))
        mine_ref, other_ref = (near_ref, from_near_ref) if side == 0 else (far_ref, from_far_ref)
        for block in range(3):
            mine = mine_ref[slot % HALF, edges_of(block), :].astype(F32)
            other = other_ref[place, edges_of(block), :].astype(F32)
            edges[slot, block, :DRAFT, :] = jnp.where(local, mine, other)
            edges[slot, block, DRAFT:, :] = jnp.zeros((8, DK), F32)

        @pl.when(local)
        def _():
            states[slot] = mine_ref[slot % HALF, : 2 * DK, :]

        @pl.when(jnp.logical_not(local))
        def _():
            states[slot] = other_ref[place, : 2 * DK, :]

    sub_iota = lax.broadcasted_iota(jnp.int32, (1, DRAFT, DK), 1)

    def pair(step, _):
        base = step * 2
        for sub in range(2):
            slot = base + sub
            for head in range(2):
                lane = sub * 2 + head
                for block, (in_ref, out, act) in enumerate(
                    (
                        (query_ref, query_scr, as_query),
                        (forget_ref, forget_scr, jax.nn.sigmoid),
                        (value_ref, value_scr, as_value),
                    )
                ):
                    first = in_ref[slot, head, :half]
                    for shift in range(CONV - 1):
                        taps = conv_ref[shift, head, block_of(block)]
                        rows = edges[slot, block, pl.ds(2 * shift + head, half, stride=2), :]
                        first = first + taps[None, :] * rows
                    out[lane, :half] = act(first)
                    out[lane, half:] = in_ref[slot, head, half:]
        queries = query_scr[...]
        forget = forget_scr[...]
        values = value_scr[...]
        weights = jnp.zeros((4, DRAFT, DK), F32)
        decay = jnp.ones((4, 1, DK), F32)
        head_rows = []
        query_rows = []
        for t in range(DRAFT):
            forget_t = forget[:, t : t + 1, :]
            query_t = queries[:, t : t + 1, :]
            decay = decay * forget_t
            weights = jnp.where(sub_iota == t, 1.0 - forget_t, weights * forget_t)
            scores = jnp.sum(weights * query_t, axis=-1, keepdims=True)
            head_rows.append(jnp.sum(scores * values, axis=1, keepdims=True))
            query_rows.append(query_t * decay)
        local_out = jnp.concatenate(head_rows, axis=1)
        decayed = jnp.concatenate(query_rows, axis=1)
        for sub in range(2):
            slot = base + sub
            parity = lax.axis_index("req") % 2
            near_row = (1 - parity) * HALF + slot
            far_row = parity * HALF + slot - HALF
            row = jnp.where(slot < HALF, near_row, far_row)
            for head in range(2):
                lane = sub * 2 + head
                fine = decayed[lane]
                coarse = fine.astype(BF)
                stacked = jnp.concatenate([coarse, (fine - coarse.astype(F32)).astype(BF)], axis=0)
                both = jnp.dot(
                    stacked, states[slot, block_of(head), :], preferred_element_type=F32
                )
                out = local_out[lane] + (both[:DRAFT] + both[DRAFT:])
                scale = lax.rsqrt(jnp.mean(out * out, axis=-1, keepdims=True) + 1e-05)
                mixed_ref[row, :, block_of(head)] = (
                    out * scale * gain_ref[head, :][None, :]
                ).astype(BF)
        return 0

    lax.fori_loop(0, ROWS // 2, pair, 0)


def mixer_call(owner, near, far, from_near, from_far, queries, forget, values, conv, bias, gain):
    return call(
        mixer, jax.ShapeDtypeStruct((ROWS, DRAFT, 2 * DK), BF), [SM] + [VM] * 10,
        [
            pltpu.VMEM((ROWS, 3, 24, DK), F32),
            pltpu.VMEM((ROWS, 2 * DK, DK), BF),
            pltpu.VMEM((4, DRAFT, DK), F32),
            pltpu.VMEM((4, DRAFT, DK), F32),
            pltpu.VMEM((4, DRAFT, DK), F32),
        ],
        20_000_000, 2_000_000,
        owner, near, far, from_near, from_far, queries, forget, values, conv, bias, gain,
    )


def later(x, shift):
    return jnp.concatenate([x[shift:], jnp.ones((shift, DK), F32)], axis=0)


def split(x):
    coarse = x.astype(BF)
    return coarse, (x - coarse.astype(F32)).astype(BF)


def keep(
    owner_ref, accept_ref, near_ref, far_ref, from_near_ref, from_far_ref, state_ref, conv_ref,
    bias_ref, kept_ref, edges_out_ref, states, window, left, right, decays, sems,
):
    state_copies = [
        pltpu.make_async_copy(state_ref.at[row], states.at[row], sems.at[row])
        for row in range(ROWS)
    ]
    for copy in state_copies:
        copy.start()
    position = lax.broadcasted_iota(jnp.int32, (DRAFT, DK), 0)
    for slot in range(ROWS):
        side = slot // HALF
        row = row_of(side, slot % HALF)
        partner, local, place = source_of(owner_ref, row)
        length = accept_ref[partner]
        mine_ref, other_ref = (near_ref, from_near_ref) if side == 0 else (far_ref, from_far_ref)
        for block in range(3):
            mine = mine_ref[slot % HALF, drafts_of(block), :].astype(F32)
            other = other_ref[place, drafts_of(block), :].astype(F32)
            window[slot, block, 8:, :] = jnp.where(local, mine, other)
            window[slot, block, 2:8, :] = mine_ref[slot % HALF, edges_of(block), :].astype(F32)[:6]
        for head in range(2):
            gates = convolve(window, conv_ref, slot, head, 1) + bias_ref[head, :][None, :]
            values = as_value(convolve(window, conv_ref, slot, head, 2))
            forget = jax.nn.sigmoid(gates)
            inside = position < length
            weights = jnp.where(inside, 1.0 - forget, 0.0)
            factors = jnp.where(inside, forget, 1.0)
            after = later(factors, 1)
            for shift in (1, 2, 4, 8):
                after = after * later(after, shift)
            weight_high, weight_low = split(weights * after)
            value_high, value_low = split(values)
            left[slot, head] = jnp.concatenate([weight_high, weight_low, weight_high], axis=0)
            right[slot, head] = jnp.concatenate([value_high, value_high, value_low], axis=0)
            lane = 2 * slot + head
            decays[lane : lane + 1, :] = (factors * after)[:1, :]
        for block in range(3):
            turned = pltpu.roll(window[slot, block], 38 - 2 * length, 0)
            for step in range(CONV - 1):
                edges_out_ref[row, step, :, block_of(block)] = turned[
                    2 * step : 2 * step + 2
                ].astype(BF)
    columns = jnp.transpose(decays[...])
    for copy in state_copies:
        copy.wait()
    for slot in range(ROWS):
        row = row_of(slot // HALF, slot % HALF)
        for head in range(2):
            lane = 2 * slot + head
            update = lax.dot_general(
                left[slot, head], right[slot, head], (((0,), (0,)), ((), ())),
                preferred_element_type=F32,
            )
            kept_ref[row, head] = columns[:, lane : lane + 1] * states[row, head] + update


def keep_call(owner, accept, near, far, from_near, from_far, states, conv, bias):
    shape = jax.ShapeDtypeStruct
    return call(
        keep, (shape(states.shape, F32), shape((ROWS, CONV - 1, 2, 3 * DK), BF)),
        [SM, SM, VM, VM, VM, VM, HB, VM, VM],
        [
            pltpu.VMEM(states.shape, F32),
            pltpu.VMEM((ROWS, 3, 40, DK), F32),
            pltpu.VMEM((ROWS, 2, 3 * DRAFT, DK), BF),
            pltpu.VMEM((ROWS, 2, 3 * DRAFT, DK), BF),
            pltpu.VMEM((2 * ROWS, DK), F32),
            pltpu.SemaphoreType.DMA((ROWS,)),
        ],
        20_000_000, 3_000_000, owner, accept, near, far, from_near, from_far, states, conv, bias,
    )


def columns_of(step, width):
    place = lax.bitwise_xor(lax.axis_index("grp"), step)
    return pl.ds(pl.multiple_of(place * width, width), width)


def project_kernel(
    rows_ref, weight_ref, resid_ref, own_ref, next_ref, far_ref, prev_ref,
):
    width = own_ref.shape[1]
    rows = rows_ref[...]
    for step, out_ref in ((2, far_ref), (1, next_ref), (3, prev_ref)):
        part = jnp.dot(rows, weight_ref[:, columns_of(step, width)], preferred_element_type=F32)
        out_ref[...] = part.astype(BF)
    part = jnp.dot(rows, weight_ref[:, columns_of(0, width)], preferred_element_type=F32)
    own_ref[...] = part + resid_ref[:, columns_of(0, width)].astype(F32)


def project(rows, weight, resid):
    slots, model = resid.shape
    width = model // 4
    shape = jax.ShapeDtypeStruct
    return pl.pallas_call(
        project_kernel,
        name="project",
        out_shape=(
            shape((slots, width), F32),
            shape((slots, width), BF),
            shape((slots, width), BF),
            shape((slots, width), BF),
        ),
        in_specs=[VM] * 3,
        out_specs=tuple([VM] * 4),
        compiler_params=PARAMS,
        cost_estimate=pl.CostEstimate(
            flops=140_000_000, bytes_accessed=2_000_000, transcendentals=0
        ),
    )(rows, weight, resid)


def ffn_kernel(
    length_ref, own_ref, next_ref, far_ref, prev_ref, gain_ref, gate_ref, up_ref, down_ref,
    own_out_ref, next_out_ref, far_out_ref, prev_out_ref, normed_scr,
):
    width = own_ref.shape[1]
    parts = ((0, own_ref), (1, next_ref), (2, far_ref), (3, prev_ref))
    total = None
    for _, ref in parts:
        block = ref[...].astype(F32)
        square = jnp.sum(block * block, axis=-1, keepdims=True)
        total = square if total is None else total + square
    scale = lax.rsqrt(total / (4 * width) + 1e-05)
    for step, ref in parts:
        columns = columns_of(step, width)
        normed_scr[:, columns] = (ref[...].astype(F32) * scale * gain_ref[:, columns]).astype(BF)
    normed = normed_scr[...]
    dims = (((1,), (1,)), ((), ()))
    gate = lax.dot_general(normed, gate_ref[...], dims, preferred_element_type=F32)
    up = lax.dot_general(normed, up_ref[...], dims, preferred_element_type=F32)
    hidden = (gate * jax.nn.sigmoid(gate) * up).astype(BF)
    me = lax.axis_index("req")
    position = lax.broadcasted_iota(jnp.int32, (DRAFT, 1), 0)
    live = jnp.concatenate(
        [(position < length_ref[me * ROWS + row]).astype(F32) for row in range(ROWS)], axis=0
    )
    for step, out_ref in ((2, far_out_ref), (1, next_out_ref), (3, prev_out_ref)):
        part = jnp.dot(hidden, down_ref[:, columns_of(step, width)], preferred_element_type=F32)
        out_ref[...] = (part * live).astype(BF)
    part = jnp.dot(hidden, down_ref[:, columns_of(0, width)], preferred_element_type=F32)
    own_out_ref[...] = (part + own_ref[...].astype(F32)) * live


def ffn(lengths, own, following, far, preceding, gain, gate_t, up_t, down):
    slots, width = own.shape
    shape = jax.ShapeDtypeStruct
    return pl.pallas_call(
        ffn_kernel,
        name="ffn",
        out_shape=(
            shape((slots, width), F32),
            shape((slots, width), BF),
            shape((slots, width), BF),
            shape((slots, width), BF),
        ),
        in_specs=[SM] + [VM] * 8,
        out_specs=tuple([VM] * 4),
        scratch_shapes=[pltpu.VMEM((slots, 4 * width), BF)],
        compiler_params=PARAMS,
        cost_estimate=pl.CostEstimate(
            flops=1_100_000_000, bytes_accessed=9_000_000, transcendentals=100_000
        ),
    )(lengths, own, following, far, preceding, gain, gate_t, up_t, down)


def in_hbm(array):
    return pltpu.with_memory_space_constraint(array, pltpu.HBM)


def swapped(block, step):
    return lax.ppermute(block, "grp", [(i, i ^ step) for i in range(4)])


def shards(
    mix_inputs,
    conv_weight,
    forget_bias,
    norm_gain,
    out_weight,
    resid,
    ffn_gain,
    gate_weight,
    up_weight,
    down_weight,
    held_states,
    held_edges,
    draft_lengths,
    accepted,
    owner_row,
):
    slots = ROWS * DRAFT
    owner_row, accepted, draft_lengths = in_hbm(owner_row), in_hbm(accepted), in_hbm(draft_lengths)
    count = lax.axis_size("req")
    states = in_hbm(held_states)
    far, near = pack_call(states, in_hbm(held_edges), in_hbm(mix_inputs))
    across = [(i, (i + (1 if i % 2 else -1)) % count) for i in range(count)]
    from_far = lax.ppermute(far, "req", across)
    queries, forget, values, conv, bias, gain = prepare_call(
        near, far, in_hbm(conv_weight), in_hbm(forget_bias), in_hbm(norm_gain)
    )
    near, queries = lax.optimization_barrier((near, queries))
    from_near = lax.ppermute(near, "req", [(i, i ^ 1) for i in range(count)])
    mixed = mixer_call(
        owner_row, near, far, from_near, from_far, queries, forget, values, conv, bias, gain
    )
    own_part, to_one, to_two, to_three = project(
        mixed.reshape(slots, -1), out_weight, resid.reshape(slots, -1)
    )
    own_part, gate_weight, up_weight, down_weight = lax.optimization_barrier(
        (own_part, gate_weight, up_weight, down_weight)
    )
    gate_t, up_t, down = fetch_call(
        in_hbm(gate_weight.T), in_hbm(up_weight.T), in_hbm(down_weight)
    )
    two = swapped(to_two, 2)
    one = swapped(to_one, 1)
    three = swapped(to_three, 3)
    one, two, three, gate_t, up_t, down = lax.optimization_barrier(
        (one, two, three, gate_t, up_t, down)
    )
    stream = (own_part + two.astype(F32) + one.astype(F32) + three.astype(F32)).astype(BF)
    stream, from_near, from_far = lax.optimization_barrier((stream, from_near, from_far))
    two = swapped(stream, 2)
    one = swapped(stream, 1)
    three = swapped(stream, 3)
    kept_states, kept_edges = keep_call(
        owner_row, accepted, near, far, from_near, from_far, states, conv, bias
    )
    one, two, three, kept_states, kept_edges = lax.optimization_barrier(
        (one, two, three, kept_states, kept_edges)
    )
    own_part, to_one, to_two, to_three = ffn(
        draft_lengths, stream, one, two, three, ffn_gain[None, :], gate_t, up_t, down
    )
    two = swapped(to_two, 2)
    one = swapped(to_one, 1)
    three = swapped(to_three, 3)
    layer_out = (own_part + two.astype(F32) + one.astype(F32) + three.astype(F32)).astype(BF)
    return (layer_out.reshape(ROWS, DRAFT, -1), kept_states, kept_edges)


def solution(mesh):
    return jax.shard_map(
        shards,
        mesh=mesh,
        in_specs=(
            P("req", None, "grp", None),
            P(None, "grp", None),
            P("grp", None),
            P("grp", None),
            P("grp", None),
            P("req", None, None),
            P(),
            P(None, "grp"),
            P(None, "grp"),
            P("grp", None),
            P("req", "grp", None, None),
            P("req", None, "grp", None),
            P(),
            P(),
            P(),
        ),
        out_specs=(P("req", None, "grp"), P("req", "grp", None, None), P("req", None, "grp", None)),
        check_vma=False,
    )
```

```python
import jax
import jax.numpy as jnp
from jax import lax
from jax.experimental import pallas as pl
from jax.experimental.pallas import tpu as pltpu
from jax.sharding import PartitionSpec as P

DK = 128
DRAFT = 16
CONV = 4
HALF = 4
ROWS = 2 * HALF
BF = jnp.bfloat16
PARAMS = pltpu.CompilerParams(vmem_limit_bytes=12 * 1024 * 1024)
F32 = jnp.float32
EDGES_AT = 2 * DK
DRAFTS_AT = EDGES_AT + 3 * DRAFT
PACKED = DRAFTS_AT + 3 * 2 * DRAFT
VM = pl.BlockSpec(memory_space=pltpu.VMEM)
SM = pl.BlockSpec(memory_space=pltpu.SMEM)
HB = pl.BlockSpec(memory_space=pltpu.HBM)


def row_of(half, place):
    parity = lax.axis_index("req") % 2
    base = (1 - parity if half == 0 else parity) * HALF
    return base + place


def source_of(owner_ref, row):
    me = lax.axis_index("req")
    partner = owner_ref[me * ROWS + row]
    return partner, partner // ROWS == me, partner % HALF


def block_of(block):
    return slice(block * DK, (block + 1) * DK)


def edges_of(block):
    return slice(EDGES_AT + block * DRAFT, EDGES_AT + (block + 1) * DRAFT)


def drafts_of(block):
    return slice(DRAFTS_AT + block * 2 * DRAFT, DRAFTS_AT + (block + 1) * 2 * DRAFT)


def call(kernel, out_shape, in_specs, scratch, flops, moved, *args):
    return pl.pallas_call(
        kernel,
        name=kernel.__name__,
        out_shape=out_shape,
        in_specs=in_specs,
        out_specs=jax.tree.map(lambda _: VM, out_shape),
        scratch_shapes=scratch,
        compiler_params=PARAMS,
        cost_estimate=pl.CostEstimate(flops=flops, bytes_accessed=moved, transcendentals=0),
    )(*args)


def columns_of(step, width):
    place = lax.bitwise_xor(lax.axis_index("grp"), step)
    return pl.ds(pl.multiple_of(place * width, width), width)


def pack(
    state_ref, edge_ref, draft_ref, weight_ref, far_ref, near_ref, one_ref, two_ref, three_ref,
    states, edges, drafts, sems,
):
    width = one_ref.shape[1]
    cuts = [
        pltpu.make_async_copy(
            weight_ref.at[:, columns_of(step, width)], out_ref, sems.at[ROWS + 1 + step]
        )
        for step, out_ref in ((1, one_ref), (2, two_ref), (3, three_ref))
    ]
    copies = [
        pltpu.make_async_copy(state_ref.at[row], states.at[row], sems.at[row])
        for row in range(ROWS)
    ]
    edge_copy = pltpu.make_async_copy(edge_ref, edges, sems.at[ROWS])
    draft_copy = pltpu.make_async_copy(draft_ref, drafts, sems.at[ROWS + 1])
    draft_copy.start()
    edge_copy.start()
    for copy in copies:
        copy.start()
    for copy in cuts:
        copy.start()
    edge_copy.wait()
    draft_copy.wait()
    for half, out_ref in ((1, far_ref), (0, near_ref)):
        for place in range(HALF):
            row = row_of(half, place)
            for block in range(3):
                columns = block_of(block)
                out_ref[place, edges_of(block), :] = jnp.zeros((DRAFT, DK), BF)
                start = EDGES_AT + block * DRAFT
                for step in range(CONV - 1):
                    out_ref[place, start + 2 * step : start + 2 * step + 2, :] = edges[
                        row, step, :, columns
                    ]
                start = DRAFTS_AT + block * 2 * DRAFT
                for step in range(DRAFT):
                    out_ref[place, start + 2 * step : start + 2 * step + 2, :] = drafts[
                        row, step, :, columns
                    ]
    for copy in copies:
        copy.wait()
    for half, out_ref in ((1, far_ref), (0, near_ref)):
        for place in range(HALF):
            for head in range(2):
                out_ref[place, block_of(head), :] = states[row_of(half, place), head].astype(BF)
    for copy in cuts:
        copy.wait()


def pack_call(states, edges, drafts, weight):
    half = jax.ShapeDtypeStruct((HALF, PACKED, DK), BF)
    cut = jax.ShapeDtypeStruct((weight.shape[0], weight.shape[1] // 4), BF)
    return call(
        pack, (half, half, cut, cut, cut), [HB] * 4,
        [
            pltpu.VMEM(states.shape, F32),
            pltpu.VMEM(edges.shape, BF),
            pltpu.VMEM(drafts.shape, BF),
            pltpu.SemaphoreType.DMA((ROWS + 5,)),
        ],
        1_000_000, 3_000_000, states, edges, drafts, weight,
    )


def convolve(window, conv_ref, slot, head, block):
    total = None
    for shift in range(CONV):
        taps = conv_ref[shift, head, block_of(block)]
        rows = window[slot, block, pl.ds(2 + 2 * shift + head, DRAFT, stride=2), :]
        term = taps[None, :] * rows
        total = term if total is None else total + term
    return total


def as_query(x):
    return x * jax.nn.sigmoid(x) * DK ** (-0.5)


def as_value(x):
    return x * jax.nn.sigmoid(x)


def prepare(slots, own_refs, window, conv_ref, bias_ref, query_ref, forget_ref, value_ref):
    for slot in slots:
        own_ref = own_refs[slot // HALF]
        for block in range(3):
            window[slot, block, :8, :] = jnp.zeros((8, DK), F32)
            window[slot, block, 8:, :] = own_ref[slot % HALF, drafts_of(block), :].astype(F32)
    half = DRAFT // 2
    for slot in slots:
        for head in range(2):
            queries, gates, values = [
                convolve(window, conv_ref, slot, head, block) for block in range(3)
            ]
            place = slot % HALF
            query_ref[place, head, :half] = queries[:half]
            query_ref[place, head, half:] = as_query(queries[half:])
            gates = gates + bias_ref[head, :][None, :]
            forget_ref[place, head, :half] = gates[:half]
            forget_ref[place, head, half:] = jax.nn.sigmoid(gates[half:])
            value_ref[place, head, :half] = values[:half]
            value_ref[place, head, half:] = as_value(values[half:])


def mix(
    side, owner_ref, mine_ref, other_ref, query_ref, forget_ref, value_ref, conv_ref, gain_ref,
    edges, states, query_scr, forget_scr, value_scr, store,
):
    half = DRAFT // 2
    for slot in range(HALF):
        _, local, place = source_of(owner_ref, row_of(side, slot))
        for block in range(3):
            mine = mine_ref[slot, edges_of(block), :].astype(F32)
            other = other_ref[place, edges_of(block), :].astype(F32)
            edges[slot, block, :DRAFT, :] = jnp.where(local, mine, other)
            edges[slot, block, DRAFT:, :] = jnp.zeros((8, DK), F32)

        @pl.when(local)
        def _():
            states[slot] = mine_ref[slot, : 2 * DK, :]

        @pl.when(jnp.logical_not(local))
        def _():
            states[slot] = other_ref[place, : 2 * DK, :]

    sub_iota = lax.broadcasted_iota(jnp.int32, (1, DRAFT, DK), 1)

    def pair(step, _):
        base = step * 2
        for sub in range(2):
            slot = base + sub
            for head in range(2):
                lane = sub * 2 + head
                for block, (in_ref, out, act) in enumerate(
                    (
                        (query_ref, query_scr, as_query),
                        (forget_ref, forget_scr, jax.nn.sigmoid),
                        (value_ref, value_scr, as_value),
                    )
                ):
                    first = in_ref[slot, head, :half]
                    for shift in range(CONV - 1):
                        taps = conv_ref[shift, head, block_of(block)]
                        rows = edges[slot, block, pl.ds(2 * shift + head, half, stride=2), :]
                        first = first + taps[None, :] * rows
                    out[lane, :half] = act(first)
                    out[lane, half:] = in_ref[slot, head, half:]
        queries = query_scr[...]
        forget = forget_scr[...]
        values = value_scr[...]
        weights = jnp.zeros((4, DRAFT, DK), F32)
        decay = jnp.ones((4, 1, DK), F32)
        head_rows = []
        query_rows = []
        for t in range(DRAFT):
            forget_t = forget[:, t : t + 1, :]
            query_t = queries[:, t : t + 1, :]
            decay = decay * forget_t
            weights = jnp.where(sub_iota == t, 1.0 - forget_t, weights * forget_t)
            scores = jnp.sum(weights * query_t, axis=-1, keepdims=True)
            head_rows.append(jnp.sum(scores * values, axis=1, keepdims=True))
            query_rows.append(query_t * decay)
        local_out = jnp.concatenate(head_rows, axis=1)
        decayed = jnp.concatenate(query_rows, axis=1)
        for sub in range(2):
            slot = base + sub
            for head in range(2):
                lane = sub * 2 + head
                fine = decayed[lane]
                coarse = fine.astype(BF)
                stacked = jnp.concatenate([coarse, (fine - coarse.astype(F32)).astype(BF)], axis=0)
                both = jnp.dot(
                    stacked, states[slot, block_of(head), :], preferred_element_type=F32
                )
                out = local_out[lane] + (both[:DRAFT] + both[DRAFT:])
                scale = lax.rsqrt(jnp.mean(out * out, axis=-1, keepdims=True) + 1e-05)
                store(slot, head, (out * scale * gain_ref[head, :][None, :]).astype(BF))
        return 0

    lax.fori_loop(0, HALF // 2, pair, 0)


MIX_SCRATCH = [
    pltpu.VMEM((HALF, 3, 24, DK), F32),
    pltpu.VMEM((HALF, 2 * DK, DK), BF),
    pltpu.VMEM((4, DRAFT, DK), F32),
    pltpu.VMEM((4, DRAFT, DK), F32),
    pltpu.VMEM((4, DRAFT, DK), F32),
]


def mix_near(
    owner_ref, near_ref, far_ref, from_near_ref, conv_hbm, bias_hbm, gain_hbm,
    mixed_ref, query_ref, forget_ref, value_ref, conv_ref, bias_ref, gain_ref,
    window, near_query, near_forget, near_value, edges, states, query_scr, forget_scr, value_scr,
    sems,
):
    pairs = ((conv_hbm, conv_ref), (bias_hbm, bias_ref), (gain_hbm, gain_ref))
    copies = [
        pltpu.make_async_copy(src, dst, sems.at[i]) for i, (src, dst) in enumerate(pairs)
    ]
    for copy in copies:
        copy.start()
    for copy in copies:
        copy.wait()
    own_refs = (near_ref, far_ref)
    prepare(
        range(HALF), own_refs, window, conv_ref, bias_ref, near_query, near_forget, near_value
    )
    prepare(
        range(HALF, ROWS), own_refs, window, conv_ref, bias_ref, query_ref, forget_ref, value_ref
    )

    def store(slot, head, block):
        mixed_ref[slot, :, block_of(head)] = block

    mix(
        0, owner_ref, near_ref, from_near_ref, near_query, near_forget, near_value, conv_ref,
        gain_ref, edges, states, query_scr, forget_scr, value_scr, store,
    )


def mix_near_call(owner, near, far, from_near, conv, bias, gain):
    shape = jax.ShapeDtypeStruct
    rows = (HALF, 2, DRAFT, DK)
    copied = [shape(x.shape, x.dtype) for x in (conv, bias, gain)]
    return call(
        mix_near,
        (shape((HALF, DRAFT, 2 * DK), BF), *[shape(rows, F32)] * 3, *copied),
        [SM, VM, VM, VM, HB, HB, HB],
        [pltpu.VMEM((ROWS, 3, 40, DK), F32)]
        + [pltpu.VMEM(rows, F32)] * 3
        + MIX_SCRATCH
        + [pltpu.SemaphoreType.DMA((3,))],
        15_000_000, 3_000_000, owner, near, far, from_near, conv, bias, gain,
    )


def mix_far(
    owner_ref, near_mixed_ref, far_ref, from_far_ref, query_ref, forget_ref, value_ref,
    conv_ref, gain_ref, mixed_ref, edges, states, query_scr, forget_scr, value_scr,
):
    parity = lax.axis_index("req") % 2
    for slot in range(HALF):
        mixed_ref[row_of(0, slot)] = near_mixed_ref[slot]

    def store(slot, head, block):
        mixed_ref[parity * HALF + slot, :, block_of(head)] = block

    mix(
        1, owner_ref, far_ref, from_far_ref, query_ref, forget_ref, value_ref, conv_ref,
        gain_ref, edges, states, query_scr, forget_scr, value_scr, store,
    )


def mix_far_call(owner, near_mixed, far, from_far, queries, forget, values, conv, gain):
    return call(
        mix_far, jax.ShapeDtypeStruct((ROWS, DRAFT, 2 * DK), BF), [SM] + [VM] * 8, MIX_SCRATCH,
        10_000_000, 2_000_000,
        owner, near_mixed, far, from_far, queries, forget, values, conv, gain,
    )


def fetch(*refs):
    count = len(refs) // 2
    sems = refs[-1]
    copies = [
        pltpu.make_async_copy(refs[i], refs[count + i], sems.at[i]) for i in range(count)
    ]
    for copy in copies:
        copy.start()
    for copy in copies:
        copy.wait()


def fetch_call(*arrays):
    return call(
        fetch, tuple(jax.ShapeDtypeStruct(x.shape, x.dtype) for x in arrays), [HB] * len(arrays),
        [pltpu.SemaphoreType.DMA((len(arrays),))], 0, 17_000_000, *arrays,
    )


def mixer(
    owner_ref, near_ref, far_ref, from_near_ref, from_far_ref, query_ref, forget_ref, value_ref,
    conv_ref, bias_ref, gain_ref, mixed_ref, edges, states, query_scr, forget_scr, value_scr,
):
    half = DRAFT // 2
    for slot in range(ROWS):
        side = slot // HALF
        _, local, place = source_of(owner_ref, row_of(side, slot % HALF))
        mine_ref, other_ref = (near_ref, from_near_ref) if side == 0 else (far_ref, from_far_ref)
        for block in range(3):
            mine = mine_ref[slot % HALF, edges_of(block), :].astype(F32)
            other = other_ref[place, edges_of(block), :].astype(F32)
            edges[slot, block, :DRAFT, :] = jnp.where(local, mine, other)
            edges[slot, block, DRAFT:, :] = jnp.zeros((8, DK), F32)

        @pl.when(local)
        def _():
            states[slot] = mine_ref[slot % HALF, : 2 * DK, :]

        @pl.when(jnp.logical_not(local))
        def _():
            states[slot] = other_ref[place, : 2 * DK, :]

    sub_iota = lax.broadcasted_iota(jnp.int32, (1, DRAFT, DK), 1)

    def pair(step, _):
        base = step * 2
        for sub in range(2):
            slot = base + sub
            for head in range(2):
                lane = sub * 2 + head
                for block, (in_ref, out, act) in enumerate(
                    (
                        (query_ref, query_scr, as_query),
                        (forget_ref, forget_scr, jax.nn.sigmoid),
                        (value_ref, value_scr, as_value),
                    )
                ):
                    first = in_ref[slot, head, :half]
                    for shift in range(CONV - 1):
                        taps = conv_ref[shift, head, block_of(block)]
                        rows = edges[slot, block, pl.ds(2 * shift + head, half, stride=2), :]
                        first = first + taps[None, :] * rows
                    out[lane, :half] = act(first)
                    out[lane, half:] = in_ref[slot, head, half:]
        queries = query_scr[...]
        forget = forget_scr[...]
        values = value_scr[...]
        weights = jnp.zeros((4, DRAFT, DK), F32)
        decay = jnp.ones((4, 1, DK), F32)
        head_rows = []
        query_rows = []
        for t in range(DRAFT):
            forget_t = forget[:, t : t + 1, :]
            query_t = queries[:, t : t + 1, :]
            decay = decay * forget_t
            weights = jnp.where(sub_iota == t, 1.0 - forget_t, weights * forget_t)
            scores = jnp.sum(weights * query_t, axis=-1, keepdims=True)
            head_rows.append(jnp.sum(scores * values, axis=1, keepdims=True))
            query_rows.append(query_t * decay)
        local_out = jnp.concatenate(head_rows, axis=1)
        decayed = jnp.concatenate(query_rows, axis=1)
        for sub in range(2):
            slot = base + sub
            parity = lax.axis_index("req") % 2
            near_row = (1 - parity) * HALF + slot
            far_row = parity * HALF + slot - HALF
            row = jnp.where(slot < HALF, near_row, far_row)
            for head in range(2):
                lane = sub * 2 + head
                fine = decayed[lane]
                coarse = fine.astype(BF)
                stacked = jnp.concatenate([coarse, (fine - coarse.astype(F32)).astype(BF)], axis=0)
                both = jnp.dot(
                    stacked, states[slot, block_of(head), :], preferred_element_type=F32
                )
                out = local_out[lane] + (both[:DRAFT] + both[DRAFT:])
                scale = lax.rsqrt(jnp.mean(out * out, axis=-1, keepdims=True) + 1e-05)
                mixed_ref[row, :, block_of(head)] = (
                    out * scale * gain_ref[head, :][None, :]
                ).astype(BF)
        return 0

    lax.fori_loop(0, ROWS // 2, pair, 0)


def mixer_call(owner, near, far, from_near, from_far, queries, forget, values, conv, bias, gain):
    return call(
        mixer, jax.ShapeDtypeStruct((ROWS, DRAFT, 2 * DK), BF), [SM] + [VM] * 10,
        [
            pltpu.VMEM((ROWS, 3, 24, DK), F32),
            pltpu.VMEM((ROWS, 2 * DK, DK), BF),
            pltpu.VMEM((4, DRAFT, DK), F32),
            pltpu.VMEM((4, DRAFT, DK), F32),
            pltpu.VMEM((4, DRAFT, DK), F32),
        ],
        20_000_000, 2_000_000,
        owner, near, far, from_near, from_far, queries, forget, values, conv, bias, gain,
    )


def later(x, shift):
    return jnp.concatenate([x[shift:], jnp.ones((shift, DK), F32)], axis=0)


def split(x):
    coarse = x.astype(BF)
    return coarse, (x - coarse.astype(F32)).astype(BF)


def keep(
    owner_ref, accept_ref, near_ref, far_ref, from_near_ref, from_far_ref, state_ref, conv_ref,
    bias_ref, kept_ref, edges_out_ref, states, window, left, right, decays, sems,
):
    state_copies = [
        pltpu.make_async_copy(state_ref.at[row], states.at[row], sems.at[row])
        for row in range(ROWS)
    ]
    for copy in state_copies:
        copy.start()
    position = lax.broadcasted_iota(jnp.int32, (DRAFT, DK), 0)
    for slot in range(ROWS):
        side = slot // HALF
        row = row_of(side, slot % HALF)
        partner, local, place = source_of(owner_ref, row)
        length = accept_ref[partner]
        mine_ref, other_ref = (near_ref, from_near_ref) if side == 0 else (far_ref, from_far_ref)
        for block in range(3):
            mine = mine_ref[slot % HALF, drafts_of(block), :].astype(F32)
            other = other_ref[place, drafts_of(block), :].astype(F32)
            window[slot, block, 8:, :] = jnp.where(local, mine, other)
            window[slot, block, 2:8, :] = mine_ref[slot % HALF, edges_of(block), :].astype(F32)[:6]
        for head in range(2):
            gates = convolve(window, conv_ref, slot, head, 1) + bias_ref[head, :][None, :]
            values = as_value(convolve(window, conv_ref, slot, head, 2))
            forget = jax.nn.sigmoid(gates)
            inside = position < length
            weights = jnp.where(inside, 1.0 - forget, 0.0)
            factors = jnp.where(inside, forget, 1.0)
            after = later(factors, 1)
            for shift in (1, 2, 4, 8):
                after = after * later(after, shift)
            weight_high, weight_low = split(weights * after)
            value_high, value_low = split(values)
            left[slot, head] = jnp.concatenate([weight_high, weight_low, weight_high], axis=0)
            right[slot, head] = jnp.concatenate([value_high, value_high, value_low], axis=0)
            lane = 2 * slot + head
            decays[lane : lane + 1, :] = (factors * after)[:1, :]
        for block in range(3):
            turned = pltpu.roll(window[slot, block], 38 - 2 * length, 0)
            for step in range(CONV - 1):
                edges_out_ref[row, step, :, block_of(block)] = turned[
                    2 * step : 2 * step + 2
                ].astype(BF)
    columns = jnp.transpose(decays[...])
    for copy in state_copies:
        copy.wait()
    for slot in range(ROWS):
        row = row_of(slot // HALF, slot % HALF)
        for head in range(2):
            lane = 2 * slot + head
            update = lax.dot_general(
                left[slot, head], right[slot, head], (((0,), (0,)), ((), ())),
                preferred_element_type=F32,
            )
            kept_ref[row, head] = columns[:, lane : lane + 1] * states[row, head] + update


def keep_call(owner, accept, near, far, from_near, from_far, states, conv, bias):
    shape = jax.ShapeDtypeStruct
    return call(
        keep, (shape(states.shape, F32), shape((ROWS, CONV - 1, 2, 3 * DK), BF)),
        [SM, SM, VM, VM, VM, VM, HB, VM, VM],
        [
            pltpu.VMEM(states.shape, F32),
            pltpu.VMEM((ROWS, 3, 40, DK), F32),
            pltpu.VMEM((ROWS, 2, 3 * DRAFT, DK), BF),
            pltpu.VMEM((ROWS, 2, 3 * DRAFT, DK), BF),
            pltpu.VMEM((2 * ROWS, DK), F32),
            pltpu.SemaphoreType.DMA((ROWS,)),
        ],
        20_000_000, 3_000_000, owner, accept, near, far, from_near, from_far, states, conv, bias,
    )


def project(
    own_ref, one_ref, two_ref, three_ref, weight_ref, from_one_ref, from_two_ref, from_three_ref,
    resid_ref, stream_ref,
):
    width = stream_ref.shape[1]
    columns = columns_of(0, width)
    total = jnp.dot(own_ref[...], weight_ref[:, columns], preferred_element_type=F32)
    for rows_ref, part_ref in (
        (one_ref, from_one_ref), (two_ref, from_two_ref), (three_ref, from_three_ref)
    ):
        total = total + jnp.dot(rows_ref[...], part_ref[...], preferred_element_type=F32)
    stream_ref[...] = (resid_ref[:, columns].astype(F32) + total).astype(BF)


def project_call(mixed, others, weight, parts, resid):
    slots, model = resid.shape
    return call(
        project, jax.ShapeDtypeStruct((slots, model // 4), BF), [VM] * 9, [],
        140_000_000, 3_000_000, mixed, *others, weight, *parts, resid,
    )


def ffn_kernel(
    length_ref, own_ref, next_ref, far_ref, prev_ref, gain_ref, gate_ref, up_ref, down_ref,
    own_out_ref, next_out_ref, far_out_ref, prev_out_ref, normed_scr,
):
    width = own_ref.shape[1]
    parts = ((0, own_ref), (1, next_ref), (2, far_ref), (3, prev_ref))
    total = None
    for _, ref in parts:
        block = ref[...].astype(F32)
        square = jnp.sum(block * block, axis=-1, keepdims=True)
        total = square if total is None else total + square
    scale = lax.rsqrt(total / (4 * width) + 1e-05)
    for step, ref in parts:
        columns = columns_of(step, width)
        normed_scr[:, columns] = (ref[...].astype(F32) * scale * gain_ref[:, columns]).astype(BF)
    normed = normed_scr[...]
    dims = (((1,), (1,)), ((), ()))
    gate = lax.dot_general(normed, gate_ref[...], dims, preferred_element_type=F32)
    up = lax.dot_general(normed, up_ref[...], dims, preferred_element_type=F32)
    hidden = (gate * jax.nn.sigmoid(gate) * up).astype(BF)
    me = lax.axis_index("req")
    position = lax.broadcasted_iota(jnp.int32, (DRAFT, 1), 0)
    live = jnp.concatenate(
        [(position < length_ref[me * ROWS + row]).astype(F32) for row in range(ROWS)], axis=0
    )
    for step, out_ref in ((2, far_out_ref), (1, next_out_ref), (3, prev_out_ref)):
        part = jnp.dot(hidden, down_ref[:, columns_of(step, width)], preferred_element_type=F32)
        out_ref[...] = (part * live).astype(BF)
    part = jnp.dot(hidden, down_ref[:, columns_of(0, width)], preferred_element_type=F32)
    own_out_ref[...] = (part + own_ref[...].astype(F32)) * live


def ffn(lengths, own, following, far, preceding, gain, gate_t, up_t, down):
    slots, width = own.shape
    shape = jax.ShapeDtypeStruct
    return pl.pallas_call(
        ffn_kernel,
        name="ffn",
        out_shape=(
            shape((slots, width), F32),
            shape((slots, width), BF),
            shape((slots, width), BF),
            shape((slots, width), BF),
        ),
        in_specs=[SM] + [VM] * 8,
        out_specs=tuple([VM] * 4),
        scratch_shapes=[pltpu.VMEM((slots, 4 * width), BF)],
        compiler_params=PARAMS,
        cost_estimate=pl.CostEstimate(
            flops=1_100_000_000, bytes_accessed=9_000_000, transcendentals=100_000
        ),
    )(lengths, own, following, far, preceding, gain, gate_t, up_t, down)


def in_hbm(array):
    return pltpu.with_memory_space_constraint(array, pltpu.HBM)


def swapped(block, step):
    return lax.ppermute(block, "grp", [(i, i ^ step) for i in range(4)])


def shards(
    mix_inputs,
    conv_weight,
    forget_bias,
    norm_gain,
    out_weight,
    resid,
    ffn_gain,
    gate_weight,
    up_weight,
    down_weight,
    held_states,
    held_edges,
    draft_lengths,
    accepted,
    owner_row,
):
    slots = ROWS * DRAFT
    owner_row, accepted, draft_lengths = in_hbm(owner_row), in_hbm(accepted), in_hbm(draft_lengths)
    count = lax.axis_size("req")
    states = in_hbm(held_states)
    far, near, *cuts = pack_call(
        states, in_hbm(held_edges), in_hbm(mix_inputs), in_hbm(out_weight)
    )
    across = [(i, (i + (1 if i % 2 else -1)) % count) for i in range(count)]
    from_far = lax.ppermute(far, "req", across)
    from_near = lax.ppermute(near, "req", [(i, i ^ 1) for i in range(count)])
    parts = [swapped(cut, step) for step, cut in ((1, cuts[0]), (2, cuts[1]), (3, cuts[2]))]
    near_mixed, queries, forget, values, conv, bias, gain = mix_near_call(
        owner_row, near, far, from_near,
        in_hbm(conv_weight), in_hbm(forget_bias), in_hbm(norm_gain),
    )
    mixed = mix_far_call(
        owner_row, near_mixed, far, from_far, queries, forget, values, conv, gain
    ).reshape(slots, -1)
    mixed, parts[0], gate_weight, up_weight, down_weight = lax.optimization_barrier(
        (mixed, parts[0], gate_weight, up_weight, down_weight)
    )
    others = [swapped(mixed, step) for step in (1, 2, 3)]
    gate_t, up_t, down = fetch_call(
        in_hbm(gate_weight.T), in_hbm(up_weight.T), in_hbm(down_weight)
    )
    *others, gate_t, up_t, down = lax.optimization_barrier((*others, gate_t, up_t, down))
    stream = project_call(mixed, others, out_weight, parts, resid.reshape(slots, -1))
    stream, from_near, from_far = lax.optimization_barrier((stream, from_near, from_far))
    two = swapped(stream, 2)
    one = swapped(stream, 1)
    three = swapped(stream, 3)
    kept_states, kept_edges = keep_call(
        owner_row, accepted, near, far, from_near, from_far, states, conv, bias
    )
    one, two, three, kept_states, kept_edges = lax.optimization_barrier(
        (one, two, three, kept_states, kept_edges)
    )
    own_part, to_one, to_two, to_three = ffn(
        draft_lengths, stream, one, two, three, ffn_gain[None, :], gate_t, up_t, down
    )
    two = swapped(to_two, 2)
    one = swapped(to_one, 1)
    three = swapped(to_three, 3)
    layer_out = (own_part + two.astype(F32) + one.astype(F32) + three.astype(F32)).astype(BF)
    return (layer_out.reshape(ROWS, DRAFT, -1), kept_states, kept_edges)


def solution(mesh):
    return jax.shard_map(
        shards,
        mesh=mesh,
        in_specs=(
            P("req", None, "grp", None),
            P(None, "grp", None),
            P("grp", None),
            P("grp", None),
            P("grp", None),
            P("req", None, None),
            P(),
            P(None, "grp"),
            P(None, "grp"),
            P("grp", None),
            P("req", "grp", None, None),
            P("req", None, "grp", None),
            P(),
            P(),
            P(),
        ),
        out_specs=(P("req", None, "grp"), P("req", "grp", None, None), P("req", None, "grp", None)),
        check_vma=False,
    )
```

```python
import jax
import jax.numpy as jnp
from jax import lax
from jax.experimental import pallas as pl
from jax.experimental.pallas import tpu as pltpu
from jax.sharding import PartitionSpec as P

DK = 128
DRAFT = 16
CONV = 4
HALF = 4
ROWS = 2 * HALF
BF = jnp.bfloat16
PARAMS = pltpu.CompilerParams(vmem_limit_bytes=12 * 1024 * 1024)
F32 = jnp.float32
EDGES_AT = 2 * DK
DRAFTS_AT = EDGES_AT + 3 * DRAFT
PACKED = DRAFTS_AT + 3 * 2 * DRAFT
VM = pl.BlockSpec(memory_space=pltpu.VMEM)
SM = pl.BlockSpec(memory_space=pltpu.SMEM)
HB = pl.BlockSpec(memory_space=pltpu.HBM)


def row_of(half, place):
    parity = lax.axis_index("req") % 2
    base = (1 - parity if half == 0 else parity) * HALF
    return base + place


def source_of(owner_ref, row):
    me = lax.axis_index("req")
    partner = owner_ref[me * ROWS + row]
    return partner, partner // ROWS == me, partner % HALF


def block_of(block):
    return slice(block * DK, (block + 1) * DK)


def edges_of(block):
    return slice(EDGES_AT + block * DRAFT, EDGES_AT + (block + 1) * DRAFT)


def drafts_of(block):
    return slice(DRAFTS_AT + block * 2 * DRAFT, DRAFTS_AT + (block + 1) * 2 * DRAFT)


def call(kernel, out_shape, in_specs, scratch, flops, moved, *args):
    return pl.pallas_call(
        kernel,
        name=kernel.__name__,
        out_shape=out_shape,
        in_specs=in_specs,
        out_specs=jax.tree.map(lambda _: VM, out_shape),
        scratch_shapes=scratch,
        compiler_params=PARAMS,
        cost_estimate=pl.CostEstimate(flops=flops, bytes_accessed=moved, transcendentals=0),
    )(*args)


def first_step():
    return 1 + 2 * (lax.axis_index("req") % 2)


def second_step():
    return 3 - 2 * (lax.axis_index("req") % 2)


def columns_of(step, width):
    place = lax.bitwise_xor(lax.axis_index("grp"), step)
    return pl.ds(pl.multiple_of(place * width, width), width)


def pack(
    state_ref, edge_ref, draft_ref, weight_ref, far_ref, near_ref, first_ref, both_ref,
    states, edges, drafts, sems,
):
    width = first_ref.shape[1]
    upper = both_ref.shape[0]
    start = pl.multiple_of((lax.axis_index("req") % 2) * upper, upper)
    cuts = [
        pltpu.make_async_copy(
            weight_ref.at[:, columns_of(first_step(), width)], first_ref, sems.at[ROWS + 2]
        ),
        pltpu.make_async_copy(
            weight_ref.at[pl.ds(start, upper), columns_of(2, width)], both_ref, sems.at[ROWS + 3]
        ),
    ]
    copies = [
        pltpu.make_async_copy(state_ref.at[row], states.at[row], sems.at[row])
        for row in range(ROWS)
    ]
    edge_copy = pltpu.make_async_copy(edge_ref, edges, sems.at[ROWS])
    draft_copy = pltpu.make_async_copy(draft_ref, drafts, sems.at[ROWS + 1])
    draft_copy.start()
    edge_copy.start()
    for copy in copies:
        copy.start()
    for copy in cuts:
        copy.start()
    edge_copy.wait()
    draft_copy.wait()
    for half, out_ref in ((1, far_ref), (0, near_ref)):
        for place in range(HALF):
            row = row_of(half, place)
            for block in range(3):
                columns = block_of(block)
                out_ref[place, edges_of(block), :] = jnp.zeros((DRAFT, DK), BF)
                start = EDGES_AT + block * DRAFT
                for step in range(CONV - 1):
                    out_ref[place, start + 2 * step : start + 2 * step + 2, :] = edges[
                        row, step, :, columns
                    ]
                start = DRAFTS_AT + block * 2 * DRAFT
                for step in range(DRAFT):
                    out_ref[place, start + 2 * step : start + 2 * step + 2, :] = drafts[
                        row, step, :, columns
                    ]
    for copy in copies:
        copy.wait()
    for half, out_ref in ((1, far_ref), (0, near_ref)):
        for place in range(HALF):
            for head in range(2):
                out_ref[place, block_of(head), :] = states[row_of(half, place), head].astype(BF)
    for copy in cuts:
        copy.wait()


def pack_call(states, edges, drafts, weight):
    half = jax.ShapeDtypeStruct((HALF, PACKED, DK), BF)
    width = weight.shape[1] // 4
    first = jax.ShapeDtypeStruct((weight.shape[0], width), BF)
    both = jax.ShapeDtypeStruct((weight.shape[0] // 2, width), BF)
    return call(
        pack, (half, half, first, both), [HB] * 4,
        [
            pltpu.VMEM(states.shape, F32),
            pltpu.VMEM(edges.shape, BF),
            pltpu.VMEM(drafts.shape, BF),
            pltpu.SemaphoreType.DMA((ROWS + 4,)),
        ],
        1_000_000, 3_000_000, states, edges, drafts, weight,
    )


def convolve(window, conv_ref, slot, head, block):
    total = None
    for shift in range(CONV):
        taps = conv_ref[shift, head, block_of(block)]
        rows = window[slot, block, pl.ds(2 + 2 * shift + head, DRAFT, stride=2), :]
        term = taps[None, :] * rows
        total = term if total is None else total + term
    return total


def as_query(x):
    return x * jax.nn.sigmoid(x) * DK ** (-0.5)


def as_value(x):
    return x * jax.nn.sigmoid(x)


def prepare(slots, own_refs, window, conv_ref, bias_ref, query_ref, forget_ref, value_ref):
    for slot in slots:
        own_ref = own_refs[slot // HALF]
        for block in range(3):
            window[slot, block, :8, :] = jnp.zeros((8, DK), F32)
            window[slot, block, 8:, :] = own_ref[slot % HALF, drafts_of(block), :].astype(F32)
    half = DRAFT // 2
    for slot in slots:
        for head in range(2):
            queries, gates, values = [
                convolve(window, conv_ref, slot, head, block) for block in range(3)
            ]
            place = slot % HALF
            query_ref[place, head, :half] = queries[:half]
            query_ref[place, head, half:] = as_query(queries[half:])
            gates = gates + bias_ref[head, :][None, :]
            forget_ref[place, head, :half] = gates[:half]
            forget_ref[place, head, half:] = jax.nn.sigmoid(gates[half:])
            value_ref[place, head, :half] = values[:half]
            value_ref[place, head, half:] = as_value(values[half:])


def mix(
    side, owner_ref, mine_ref, other_ref, query_ref, forget_ref, value_ref, conv_ref, gain_ref,
    edges, states, query_scr, forget_scr, value_scr, store,
):
    half = DRAFT // 2
    for slot in range(HALF):
        _, local, place = source_of(owner_ref, row_of(side, slot))
        for block in range(3):
            mine = mine_ref[slot, edges_of(block), :].astype(F32)
            other = other_ref[place, edges_of(block), :].astype(F32)
            edges[slot, block, :DRAFT, :] = jnp.where(local, mine, other)
            edges[slot, block, DRAFT:, :] = jnp.zeros((8, DK), F32)

        @pl.when(local)
        def _():
            states[slot] = mine_ref[slot, : 2 * DK, :]

        @pl.when(jnp.logical_not(local))
        def _():
            states[slot] = other_ref[place, : 2 * DK, :]

    sub_iota = lax.broadcasted_iota(jnp.int32, (1, DRAFT, DK), 1)

    def pair(step, _):
        base = step * 2
        for sub in range(2):
            slot = base + sub
            for head in range(2):
                lane = sub * 2 + head
                for block, (in_ref, out, act) in enumerate(
                    (
                        (query_ref, query_scr, as_query),
                        (forget_ref, forget_scr, jax.nn.sigmoid),
                        (value_ref, value_scr, as_value),
                    )
                ):
                    first = in_ref[slot, head, :half]
                    for shift in range(CONV - 1):
                        taps = conv_ref[shift, head, block_of(block)]
                        rows = edges[slot, block, pl.ds(2 * shift + head, half, stride=2), :]
                        first = first + taps[None, :] * rows
                    out[lane, :half] = act(first)
                    out[lane, half:] = in_ref[slot, head, half:]
        queries = query_scr[...]
        forget = forget_scr[...]
        values = value_scr[...]
        weights = jnp.zeros((4, DRAFT, DK), F32)
        decay = jnp.ones((4, 1, DK), F32)
        head_rows = []
        query_rows = []
        for t in range(DRAFT):
            forget_t = forget[:, t : t + 1, :]
            query_t = queries[:, t : t + 1, :]
            decay = decay * forget_t
            weights = jnp.where(sub_iota == t, 1.0 - forget_t, weights * forget_t)
            scores = jnp.sum(weights * query_t, axis=-1, keepdims=True)
            head_rows.append(jnp.sum(scores * values, axis=1, keepdims=True))
            query_rows.append(query_t * decay)
        local_out = jnp.concatenate(head_rows, axis=1)
        decayed = jnp.concatenate(query_rows, axis=1)
        for sub in range(2):
            slot = base + sub
            for head in range(2):
                lane = sub * 2 + head
                fine = decayed[lane]
                coarse = fine.astype(BF)
                stacked = jnp.concatenate([coarse, (fine - coarse.astype(F32)).astype(BF)], axis=0)
                both = jnp.dot(
                    stacked, states[slot, block_of(head), :], preferred_element_type=F32
                )
                out = local_out[lane] + (both[:DRAFT] + both[DRAFT:])
                scale = lax.rsqrt(jnp.mean(out * out, axis=-1, keepdims=True) + 1e-05)
                store(slot, head, (out * scale * gain_ref[head, :][None, :]).astype(BF))
        return 0

    lax.fori_loop(0, HALF // 2, pair, 0)


MIX_SCRATCH = [
    pltpu.VMEM((HALF, 3, 24, DK), F32),
    pltpu.VMEM((HALF, 2 * DK, DK), BF),
    pltpu.VMEM((4, DRAFT, DK), F32),
    pltpu.VMEM((4, DRAFT, DK), F32),
    pltpu.VMEM((4, DRAFT, DK), F32),
]


def mix_near(
    owner_ref, near_ref, far_ref, from_near_ref, conv_hbm, bias_hbm, gain_hbm,
    mixed_ref, query_ref, forget_ref, value_ref, conv_ref, bias_ref, gain_ref,
    window, near_query, near_forget, near_value, edges, states, query_scr, forget_scr, value_scr,
    sems,
):
    pairs = ((conv_hbm, conv_ref), (bias_hbm, bias_ref), (gain_hbm, gain_ref))
    copies = [
        pltpu.make_async_copy(src, dst, sems.at[i]) for i, (src, dst) in enumerate(pairs)
    ]
    for copy in copies:
        copy.start()
    for copy in copies:
        copy.wait()
    own_refs = (near_ref, far_ref)
    prepare(
        range(HALF), own_refs, window, conv_ref, bias_ref, near_query, near_forget, near_value
    )
    prepare(
        range(HALF, ROWS), own_refs, window, conv_ref, bias_ref, query_ref, forget_ref, value_ref
    )

    def store(slot, head, block):
        mixed_ref[slot, :, block_of(head)] = block

    mix(
        0, owner_ref, near_ref, from_near_ref, near_query, near_forget, near_value, conv_ref,
        gain_ref, edges, states, query_scr, forget_scr, value_scr, store,
    )


def mix_near_call(owner, near, far, from_near, conv, bias, gain):
    shape = jax.ShapeDtypeStruct
    rows = (HALF, 2, DRAFT, DK)
    copied = [shape(x.shape, x.dtype) for x in (conv, bias, gain)]
    return call(
        mix_near,
        (shape((HALF, DRAFT, 2 * DK), BF), *[shape(rows, F32)] * 3, *copied),
        [SM, VM, VM, VM, HB, HB, HB],
        [pltpu.VMEM((ROWS, 3, 40, DK), F32)]
        + [pltpu.VMEM(rows, F32)] * 3
        + MIX_SCRATCH
        + [pltpu.SemaphoreType.DMA((3,))],
        15_000_000, 3_000_000, owner, near, far, from_near, conv, bias, gain,
    )


def mix_far(
    owner_ref, near_mixed_ref, far_ref, from_far_ref, query_ref, forget_ref, value_ref,
    conv_ref, gain_ref, mixed_ref, edges, states, query_scr, forget_scr, value_scr,
):
    parity = lax.axis_index("req") % 2
    for slot in range(HALF):
        mixed_ref[row_of(0, slot)] = near_mixed_ref[slot]

    def store(slot, head, block):
        mixed_ref[parity * HALF + slot, :, block_of(head)] = block

    mix(
        1, owner_ref, far_ref, from_far_ref, query_ref, forget_ref, value_ref, conv_ref,
        gain_ref, edges, states, query_scr, forget_scr, value_scr, store,
    )


def mix_far_call(owner, near_mixed, far, from_far, queries, forget, values, conv, gain):
    return call(
        mix_far, jax.ShapeDtypeStruct((ROWS, DRAFT, 2 * DK), BF), [SM] + [VM] * 8, MIX_SCRATCH,
        10_000_000, 2_000_000,
        owner, near_mixed, far, from_far, queries, forget, values, conv, gain,
    )


def fetch(*refs):
    count = len(refs) // 2
    sems = refs[-1]
    copies = [
        pltpu.make_async_copy(refs[i], refs[count + i], sems.at[i]) for i in range(count)
    ]
    for copy in copies:
        copy.start()
    for copy in copies:
        copy.wait()


def fetch_call(*arrays):
    return call(
        fetch, tuple(jax.ShapeDtypeStruct(x.shape, x.dtype) for x in arrays), [HB] * len(arrays),
        [pltpu.SemaphoreType.DMA((len(arrays),))], 0, 17_000_000, *arrays,
    )


def mixer(
    owner_ref, near_ref, far_ref, from_near_ref, from_far_ref, query_ref, forget_ref, value_ref,
    conv_ref, bias_ref, gain_ref, mixed_ref, edges, states, query_scr, forget_scr, value_scr,
):
    half = DRAFT // 2
    for slot in range(ROWS):
        side = slot // HALF
        _, local, place = source_of(owner_ref, row_of(side, slot % HALF))
        mine_ref, other_ref = (near_ref, from_near_ref) if side == 0 else (far_ref, from_far_ref)
        for block in range(3):
            mine = mine_ref[slot % HALF, edges_of(block), :].astype(F32)
            other = other_ref[place, edges_of(block), :].astype(F32)
            edges[slot, block, :DRAFT, :] = jnp.where(local, mine, other)
            edges[slot, block, DRAFT:, :] = jnp.zeros((8, DK), F32)

        @pl.when(local)
        def _():
            states[slot] = mine_ref[slot % HALF, : 2 * DK, :]

        @pl.when(jnp.logical_not(local))
        def _():
            states[slot] = other_ref[place, : 2 * DK, :]

    sub_iota = lax.broadcasted_iota(jnp.int32, (1, DRAFT, DK), 1)

    def pair(step, _):
        base = step * 2
        for sub in range(2):
            slot = base + sub
            for head in range(2):
                lane = sub * 2 + head
                for block, (in_ref, out, act) in enumerate(
                    (
                        (query_ref, query_scr, as_query),
                        (forget_ref, forget_scr, jax.nn.sigmoid),
                        (value_ref, value_scr, as_value),
                    )
                ):
                    first = in_ref[slot, head, :half]
                    for shift in range(CONV - 1):
                        taps = conv_ref[shift, head, block_of(block)]
                        rows = edges[slot, block, pl.ds(2 * shift + head, half, stride=2), :]
                        first = first + taps[None, :] * rows
                    out[lane, :half] = act(first)
                    out[lane, half:] = in_ref[slot, head, half:]
        queries = query_scr[...]
        forget = forget_scr[...]
        values = value_scr[...]
        weights = jnp.zeros((4, DRAFT, DK), F32)
        decay = jnp.ones((4, 1, DK), F32)
        head_rows = []
        query_rows = []
        for t in range(DRAFT):
            forget_t = forget[:, t : t + 1, :]
            query_t = queries[:, t : t + 1, :]
            decay = decay * forget_t
            weights = jnp.where(sub_iota == t, 1.0 - forget_t, weights * forget_t)
            scores = jnp.sum(weights * query_t, axis=-1, keepdims=True)
            head_rows.append(jnp.sum(scores * values, axis=1, keepdims=True))
            query_rows.append(query_t * decay)
        local_out = jnp.concatenate(head_rows, axis=1)
        decayed = jnp.concatenate(query_rows, axis=1)
        for sub in range(2):
            slot = base + sub
            parity = lax.axis_index("req") % 2
            near_row = (1 - parity) * HALF + slot
            far_row = parity * HALF + slot - HALF
            row = jnp.where(slot < HALF, near_row, far_row)
            for head in range(2):
                lane = sub * 2 + head
                fine = decayed[lane]
                coarse = fine.astype(BF)
                stacked = jnp.concatenate([coarse, (fine - coarse.astype(F32)).astype(BF)], axis=0)
                both = jnp.dot(
                    stacked, states[slot, block_of(head), :], preferred_element_type=F32
                )
                out = local_out[lane] + (both[:DRAFT] + both[DRAFT:])
                scale = lax.rsqrt(jnp.mean(out * out, axis=-1, keepdims=True) + 1e-05)
                mixed_ref[row, :, block_of(head)] = (
                    out * scale * gain_ref[head, :][None, :]
                ).astype(BF)
        return 0

    lax.fori_loop(0, ROWS // 2, pair, 0)


def mixer_call(owner, near, far, from_near, from_far, queries, forget, values, conv, bias, gain):
    return call(
        mixer, jax.ShapeDtypeStruct((ROWS, DRAFT, 2 * DK), BF), [SM] + [VM] * 10,
        [
            pltpu.VMEM((ROWS, 3, 24, DK), F32),
            pltpu.VMEM((ROWS, 2 * DK, DK), BF),
            pltpu.VMEM((4, DRAFT, DK), F32),
            pltpu.VMEM((4, DRAFT, DK), F32),
            pltpu.VMEM((4, DRAFT, DK), F32),
        ],
        20_000_000, 2_000_000,
        owner, near, far, from_near, from_far, queries, forget, values, conv, bias, gain,
    )


def later(x, shift):
    return jnp.concatenate([x[shift:], jnp.ones((shift, DK), F32)], axis=0)


def split(x):
    coarse = x.astype(BF)
    return coarse, (x - coarse.astype(F32)).astype(BF)


def keep(
    owner_ref, accept_ref, near_ref, far_ref, from_near_ref, from_far_ref, state_ref, conv_ref,
    bias_ref, kept_ref, edges_out_ref, states, window, left, right, decays, sems,
):
    state_copies = [
        pltpu.make_async_copy(state_ref.at[row], states.at[row], sems.at[row])
        for row in range(ROWS)
    ]
    for copy in state_copies:
        copy.start()
    position = lax.broadcasted_iota(jnp.int32, (DRAFT, DK), 0)
    for slot in range(ROWS):
        side = slot // HALF
        row = row_of(side, slot % HALF)
        partner, local, place = source_of(owner_ref, row)
        length = accept_ref[partner]
        mine_ref, other_ref = (near_ref, from_near_ref) if side == 0 else (far_ref, from_far_ref)
        for block in range(3):
            mine = mine_ref[slot % HALF, drafts_of(block), :].astype(F32)
            other = other_ref[place, drafts_of(block), :].astype(F32)
            window[slot, block, 8:, :] = jnp.where(local, mine, other)
            window[slot, block, 2:8, :] = mine_ref[slot % HALF, edges_of(block), :].astype(F32)[:6]
        for head in range(2):
            gates = convolve(window, conv_ref, slot, head, 1) + bias_ref[head, :][None, :]
            values = as_value(convolve(window, conv_ref, slot, head, 2))
            forget = jax.nn.sigmoid(gates)
            inside = position < length
            weights = jnp.where(inside, 1.0 - forget, 0.0)
            factors = jnp.where(inside, forget, 1.0)
            after = later(factors, 1)
            for shift in (1, 2, 4, 8):
                after = after * later(after, shift)
            weight_high, weight_low = split(weights * after)
            value_high, value_low = split(values)
            left[slot, head] = jnp.concatenate([weight_high, weight_low, weight_high], axis=0)
            right[slot, head] = jnp.concatenate([value_high, value_high, value_low], axis=0)
            lane = 2 * slot + head
            decays[lane : lane + 1, :] = (factors * after)[:1, :]
        for block in range(3):
            turned = pltpu.roll(window[slot, block], 38 - 2 * length, 0)
            for step in range(CONV - 1):
                edges_out_ref[row, step, :, block_of(block)] = turned[
                    2 * step : 2 * step + 2
                ].astype(BF)
    columns = jnp.transpose(decays[...])
    for copy in state_copies:
        copy.wait()
    for slot in range(ROWS):
        row = row_of(slot // HALF, slot % HALF)
        for head in range(2):
            lane = 2 * slot + head
            update = lax.dot_general(
                left[slot, head], right[slot, head], (((0,), (0,)), ((), ())),
                preferred_element_type=F32,
            )
            kept_ref[row, head] = columns[:, lane : lane + 1] * states[row, head] + update


def keep_call(owner, accept, near, far, from_near, from_far, states, conv, bias):
    shape = jax.ShapeDtypeStruct
    return call(
        keep, (shape(states.shape, F32), shape((ROWS, CONV - 1, 2, 3 * DK), BF)),
        [SM, SM, VM, VM, VM, VM, HB, VM, VM],
        [
            pltpu.VMEM(states.shape, F32),
            pltpu.VMEM((ROWS, 3, 40, DK), F32),
            pltpu.VMEM((ROWS, 2, 3 * DRAFT, DK), BF),
            pltpu.VMEM((ROWS, 2, 3 * DRAFT, DK), BF),
            pltpu.VMEM((2 * ROWS, DK), F32),
            pltpu.SemaphoreType.DMA((ROWS,)),
        ],
        20_000_000, 3_000_000, owner, accept, near, far, from_near, from_far, states, conv, bias,
    )


def project(
    own_ref, first_ref, second_ref, weight_ref, from_first_ref, from_both_ref, chip_ref,
    resid_ref, stream_ref,
):
    width = stream_ref.shape[1]
    depth = from_first_ref.shape[0]
    columns = columns_of(0, width)

    def product(rows, part):
        return jnp.dot(rows, part, preferred_element_type=F32)

    total = product(own_ref[...], weight_ref[:, columns])
    total = total + product(first_ref[...], from_first_ref[...])
    total = total + product(second_ref[0], chip_ref[:depth])
    parity = lax.axis_index("req") % 2
    half = depth // 2
    mine = pl.ds(pl.multiple_of(parity * half, half), half)
    other = pl.ds(pl.multiple_of((1 - parity) * half, half), half)
    total = total + product(second_ref[1, :, mine], from_both_ref[...])
    total = total + product(second_ref[1, :, other], chip_ref[depth:])
    stream_ref[...] = (resid_ref[:, columns].astype(F32) + total).astype(BF)


def project_call(mixed, first, second, weight, from_first, from_both, chip, resid):
    slots, model = resid.shape
    return call(
        project, jax.ShapeDtypeStruct((slots, model // 4), BF), [VM] * 8, [],
        140_000_000, 3_000_000, mixed, first, second, weight, from_first, from_both, chip, resid,
    )


def ffn(
    length_ref, own_ref, first_ref, second_ref, gain_ref, gate_ref, up_ref, down_ref,
    own_out_ref, second_out_ref, pair_out_ref, normed_scr,
):
    width = own_ref.shape[1]
    parts = (
        (0, own_ref[...]), (first_step(), first_ref[...]),
        (second_step(), second_ref[0]), (2, second_ref[1]),
    )
    total = None
    for _, rows in parts:
        block = rows.astype(F32)
        square = jnp.sum(block * block, axis=-1, keepdims=True)
        total = square if total is None else total + square
    scale = lax.rsqrt(total / (4 * width) + 1e-05)
    for step, rows in parts:
        columns = columns_of(step, width)
        normed_scr[:, columns] = (rows.astype(F32) * scale * gain_ref[:, columns]).astype(BF)
    normed = normed_scr[...]
    dims = (((1,), (1,)), ((), ()))
    gate = lax.dot_general(normed, gate_ref[...], dims, preferred_element_type=F32)
    up = lax.dot_general(normed, up_ref[...], dims, preferred_element_type=F32)
    hidden = (gate * jax.nn.sigmoid(gate) * up).astype(BF)
    me = lax.axis_index("req")
    position = lax.broadcasted_iota(jnp.int32, (DRAFT, 1), 0)
    live = jnp.concatenate(
        [(position < length_ref[me * ROWS + row]).astype(F32) for row in range(ROWS)], axis=0
    )

    def down(step):
        part = jnp.dot(hidden, down_ref[:, columns_of(step, width)], preferred_element_type=F32)
        return part * live

    pair_out_ref[0] = down(first_step()).astype(BF)
    pair_out_ref[1] = down(2).astype(BF)
    second_out_ref[...] = down(second_step())
    own_out_ref[...] = down(0) + own_ref[...].astype(F32) * live


def ffn_call(lengths, own, first, second, gain, gate_t, up_t, down):
    slots, width = own.shape
    shape = jax.ShapeDtypeStruct
    return call(
        ffn,
        (shape((slots, width), F32), shape((slots, width), F32), shape((2, slots, width), BF)),
        [SM] + [VM] * 7,
        [pltpu.VMEM((slots, 4 * width), BF)],
        1_100_000_000, 9_000_000, lengths, own, first, second, gain, gate_t, up_t, down,
    )


def in_hbm(array):
    return pltpu.with_memory_space_constraint(array, pltpu.HBM)


def swapped(block, steps):
    groups, count = lax.axis_size("grp"), lax.axis_size("req")
    pairs = [
        (g * count + d, (g ^ steps[d % 2]) * count + d) for g in range(groups) for d in range(count)
    ]
    return lax.ppermute(block, ("grp", "req"), pairs)


FIRST, SECOND, BOTH = (1, 3), (3, 1), (2, 2)


def shards(
    mix_inputs,
    conv_weight,
    forget_bias,
    norm_gain,
    out_weight,
    resid,
    ffn_gain,
    gate_weight,
    up_weight,
    down_weight,
    held_states,
    held_edges,
    draft_lengths,
    accepted,
    owner_row,
):
    slots = ROWS * DRAFT
    owner_row, accepted, draft_lengths = in_hbm(owner_row), in_hbm(accepted), in_hbm(draft_lengths)
    count = lax.axis_size("req")
    states = in_hbm(held_states)
    far, near, *cuts = pack_call(
        states, in_hbm(held_edges), in_hbm(mix_inputs), in_hbm(out_weight)
    )
    across = [(i, (i + (1 if i % 2 else -1)) % count) for i in range(count)]
    from_far = lax.ppermute(far, "req", across)
    from_near = lax.ppermute(near, "req", [(i, i ^ 1) for i in range(count)])
    from_first = swapped(cuts[0], FIRST)
    from_both = swapped(cuts[1], BOTH)
    near_mixed, queries, forget, values, conv, bias, gain = mix_near_call(
        owner_row, near, far, from_near,
        in_hbm(conv_weight), in_hbm(forget_bias), in_hbm(norm_gain),
    )
    mixed = mix_far_call(
        owner_row, near_mixed, far, from_far, queries, forget, values, conv, gain
    ).reshape(slots, -1)
    mixed, gate_weight, from_first, from_both = lax.optimization_barrier(
        (mixed, gate_weight, from_first, from_both)
    )
    first = swapped(mixed, FIRST)
    chip = lax.ppermute(
        jnp.concatenate([from_first, from_both]), "req", [(i, i ^ 1) for i in range(count)]
    )
    (gate_t,) = fetch_call(in_hbm(gate_weight.T))
    first, gate_t, up_weight = lax.optimization_barrier((first, gate_t, up_weight))
    second = swapped(jnp.stack([mixed, first]), SECOND)
    (up_t,) = fetch_call(in_hbm(up_weight.T))
    second, up_t = lax.optimization_barrier((second, up_t))
    stream = project_call(mixed, first, second, out_weight, from_first, from_both, chip, resid.reshape(slots, -1))
    stream, down_weight = lax.optimization_barrier((stream, down_weight))
    first = swapped(stream, FIRST)
    (down,) = fetch_call(in_hbm(down_weight))
    first, down, from_near, from_far = lax.optimization_barrier((first, down, from_near, from_far))
    second = swapped(jnp.stack([stream, first]), SECOND)
    kept_states, kept_edges = keep_call(
        owner_row, accepted, near, far, from_near, from_far, states, conv, bias
    )
    second, kept_states, kept_edges = lax.optimization_barrier((second, kept_states, kept_edges))
    own_part, for_second, pair = ffn_call(
        draft_lengths, stream, first, second, ffn_gain[None, :], gate_t, up_t, down
    )
    pair = swapped(pair, FIRST)
    second = swapped((for_second + pair[1].astype(F32)).astype(BF), SECOND)
    layer_out = (own_part + pair[0].astype(F32) + second.astype(F32)).astype(BF)
    return (layer_out.reshape(ROWS, DRAFT, -1), kept_states, kept_edges)


def solution(mesh):
    return jax.shard_map(
        shards,
        mesh=mesh,
        in_specs=(
            P("req", None, "grp", None),
            P(None, "grp", None),
            P("grp", None),
            P("grp", None),
            P("grp", None),
            P("req", None, None),
            P(),
            P(None, "grp"),
            P(None, "grp"),
            P("grp", None),
            P("req", "grp", None, None),
            P("req", None, "grp", None),
            P(),
            P(),
            P(),
        ),
        out_specs=(P("req", None, "grp"), P("req", "grp", None, None), P("req", None, "grp", None)),
        check_vma=False,
    )
```

```python
import jax
import jax.numpy as jnp
from jax import lax
from jax.experimental import pallas as pl
from jax.experimental.pallas import tpu as pltpu
from jax.sharding import PartitionSpec as P

DK = 128
DRAFT = 16
CONV = 4
HALF = 4
ROWS = 2 * HALF
BF = jnp.bfloat16
PARAMS = pltpu.CompilerParams(vmem_limit_bytes=12 * 1024 * 1024)
F32 = jnp.float32
EDGES_AT = 2 * DK
DRAFTS_AT = EDGES_AT + 3 * DRAFT
PACKED = DRAFTS_AT + 3 * 2 * DRAFT
VM = pl.BlockSpec(memory_space=pltpu.VMEM)
SM = pl.BlockSpec(memory_space=pltpu.SMEM)
HB = pl.BlockSpec(memory_space=pltpu.HBM)


def row_of(half, place):
    parity = lax.axis_index("req") % 2
    base = (1 - parity if half == 0 else parity) * HALF
    return base + place


def source_of(owner_ref, row):
    me = lax.axis_index("req")
    partner = owner_ref[me * ROWS + row]
    return partner, partner // ROWS == me, partner % HALF


def block_of(block):
    return slice(block * DK, (block + 1) * DK)


def edges_of(block):
    return slice(EDGES_AT + block * DRAFT, EDGES_AT + (block + 1) * DRAFT)


def drafts_of(block):
    return slice(DRAFTS_AT + block * 2 * DRAFT, DRAFTS_AT + (block + 1) * 2 * DRAFT)


def call(kernel, out_shape, in_specs, scratch, flops, moved, *args):
    return pl.pallas_call(
        kernel,
        name=kernel.__name__,
        out_shape=out_shape,
        in_specs=in_specs,
        out_specs=jax.tree.map(lambda _: VM, out_shape),
        scratch_shapes=scratch,
        compiler_params=PARAMS,
        cost_estimate=pl.CostEstimate(flops=flops, bytes_accessed=moved, transcendentals=0),
    )(*args)


def columns_of(step, width):
    place = lax.bitwise_xor(lax.axis_index("grp"), step)
    return pl.ds(pl.multiple_of(place * width, width), width)


def pack(
    state_ref, edge_ref, draft_ref, weight_ref, far_ref, near_ref, one_ref, three_ref,
    states, edges, drafts, sems,
):
    width = one_ref.shape[1]
    cuts = [
        pltpu.make_async_copy(
            weight_ref.at[:, columns_of(step, width)], out_ref, sems.at[ROWS + 2 + i]
        )
        for i, (step, out_ref) in enumerate(((1, one_ref), (3, three_ref)))
    ]
    copies = [
        pltpu.make_async_copy(state_ref.at[row], states.at[row], sems.at[row])
        for row in range(ROWS)
    ]
    edge_copy = pltpu.make_async_copy(edge_ref, edges, sems.at[ROWS])
    draft_copy = pltpu.make_async_copy(draft_ref, drafts, sems.at[ROWS + 1])
    draft_copy.start()
    edge_copy.start()
    for copy in copies:
        copy.start()
    for copy in cuts:
        copy.start()
    edge_copy.wait()
    draft_copy.wait()
    for half, out_ref in ((1, far_ref), (0, near_ref)):
        for place in range(HALF):
            row = row_of(half, place)
            for block in range(3):
                columns = block_of(block)
                out_ref[place, edges_of(block), :] = jnp.zeros((DRAFT, DK), BF)
                start = EDGES_AT + block * DRAFT
                for step in range(CONV - 1):
                    out_ref[place, start + 2 * step : start + 2 * step + 2, :] = edges[
                        row, step, :, columns
                    ]
                start = DRAFTS_AT + block * 2 * DRAFT
                for step in range(DRAFT):
                    out_ref[place, start + 2 * step : start + 2 * step + 2, :] = drafts[
                        row, step, :, columns
                    ]
    for copy in copies:
        copy.wait()
    for half, out_ref in ((1, far_ref), (0, near_ref)):
        for place in range(HALF):
            for head in range(2):
                out_ref[place, block_of(head), :] = states[row_of(half, place), head].astype(BF)
    for copy in cuts:
        copy.wait()


def pack_call(states, edges, drafts, weight):
    half = jax.ShapeDtypeStruct((HALF, PACKED, DK), BF)
    cut = jax.ShapeDtypeStruct((weight.shape[0], weight.shape[1] // 4), BF)
    return call(
        pack, (half, half, cut, cut), [HB] * 4,
        [
            pltpu.VMEM(states.shape, F32),
            pltpu.VMEM(edges.shape, BF),
            pltpu.VMEM(drafts.shape, BF),
            pltpu.SemaphoreType.DMA((ROWS + 4,)),
        ],
        1_000_000, 3_000_000, states, edges, drafts, weight,
    )


def convolve(window, conv_ref, slot, head, block):
    total = None
    for shift in range(CONV):
        taps = conv_ref[shift, head, block_of(block)]
        rows = window[slot, block, pl.ds(2 + 2 * shift + head, DRAFT, stride=2), :]
        term = taps[None, :] * rows
        total = term if total is None else total + term
    return total


def as_query(x):
    return x * jax.nn.sigmoid(x) * DK ** (-0.5)


def as_value(x):
    return x * jax.nn.sigmoid(x)


def prepare(slots, own_refs, window, conv_ref, bias_ref, query_ref, forget_ref, value_ref):
    for slot in slots:
        own_ref = own_refs[slot // HALF]
        for block in range(3):
            window[slot, block, :8, :] = jnp.zeros((8, DK), F32)
            window[slot, block, 8:, :] = own_ref[slot % HALF, drafts_of(block), :].astype(F32)
    half = DRAFT // 2
    for slot in slots:
        for head in range(2):
            queries, gates, values = [
                convolve(window, conv_ref, slot, head, block) for block in range(3)
            ]
            place = slot % HALF
            query_ref[place, head, :half] = queries[:half]
            query_ref[place, head, half:] = as_query(queries[half:])
            gates = gates + bias_ref[head, :][None, :]
            forget_ref[place, head, :half] = gates[:half]
            forget_ref[place, head, half:] = jax.nn.sigmoid(gates[half:])
            value_ref[place, head, :half] = values[:half]
            value_ref[place, head, half:] = as_value(values[half:])


def mix(
    side, owner_ref, mine_ref, other_ref, query_ref, forget_ref, value_ref, conv_ref, gain_ref,
    edges, states, query_scr, forget_scr, value_scr, store,
):
    half = DRAFT // 2
    for slot in range(HALF):
        _, local, place = source_of(owner_ref, row_of(side, slot))
        for block in range(3):
            mine = mine_ref[slot, edges_of(block), :].astype(F32)
            other = other_ref[place, edges_of(block), :].astype(F32)
            edges[slot, block, :DRAFT, :] = jnp.where(local, mine, other)
            edges[slot, block, DRAFT:, :] = jnp.zeros((8, DK), F32)

        @pl.when(local)
        def _():
            states[slot] = mine_ref[slot, : 2 * DK, :]

        @pl.when(jnp.logical_not(local))
        def _():
            states[slot] = other_ref[place, : 2 * DK, :]

    sub_iota = lax.broadcasted_iota(jnp.int32, (1, DRAFT, DK), 1)

    def pair(step, _):
        base = step * 2
        for sub in range(2):
            slot = base + sub
            for head in range(2):
                lane = sub * 2 + head
                for block, (in_ref, out, act) in enumerate(
                    (
                        (query_ref, query_scr, as_query),
                        (forget_ref, forget_scr, jax.nn.sigmoid),
                        (value_ref, value_scr, as_value),
                    )
                ):
                    first = in_ref[slot, head, :half]
                    for shift in range(CONV - 1):
                        taps = conv_ref[shift, head, block_of(block)]
                        rows = edges[slot, block, pl.ds(2 * shift + head, half, stride=2), :]
                        first = first + taps[None, :] * rows
                    out[lane, :half] = act(first)
                    out[lane, half:] = in_ref[slot, head, half:]
        queries = query_scr[...]
        forget = forget_scr[...]
        values = value_scr[...]
        weights = jnp.zeros((4, DRAFT, DK), F32)
        decay = jnp.ones((4, 1, DK), F32)
        head_rows = []
        query_rows = []
        for t in range(DRAFT):
            forget_t = forget[:, t : t + 1, :]
            query_t = queries[:, t : t + 1, :]
            decay = decay * forget_t
            weights = jnp.where(sub_iota == t, 1.0 - forget_t, weights * forget_t)
            scores = jnp.sum(weights * query_t, axis=-1, keepdims=True)
            head_rows.append(jnp.sum(scores * values, axis=1, keepdims=True))
            query_rows.append(query_t * decay)
        local_out = jnp.concatenate(head_rows, axis=1)
        decayed = jnp.concatenate(query_rows, axis=1)
        for sub in range(2):
            slot = base + sub
            for head in range(2):
                lane = sub * 2 + head
                fine = decayed[lane]
                coarse = fine.astype(BF)
                stacked = jnp.concatenate([coarse, (fine - coarse.astype(F32)).astype(BF)], axis=0)
                both = jnp.dot(
                    stacked, states[slot, block_of(head), :], preferred_element_type=F32
                )
                out = local_out[lane] + (both[:DRAFT] + both[DRAFT:])
                scale = lax.rsqrt(jnp.mean(out * out, axis=-1, keepdims=True) + 1e-05)
                store(slot, head, (out * scale * gain_ref[head, :][None, :]).astype(BF))
        return 0

    lax.fori_loop(0, HALF // 2, pair, 0)


MIX_SCRATCH = [
    pltpu.VMEM((HALF, 3, 24, DK), F32),
    pltpu.VMEM((HALF, 2 * DK, DK), BF),
    pltpu.VMEM((4, DRAFT, DK), F32),
    pltpu.VMEM((4, DRAFT, DK), F32),
    pltpu.VMEM((4, DRAFT, DK), F32),
]


def mix_near(
    owner_ref, near_ref, far_ref, from_near_ref, conv_hbm, bias_hbm, gain_hbm,
    mixed_ref, query_ref, forget_ref, value_ref, conv_ref, bias_ref, gain_ref,
    window, near_query, near_forget, near_value, edges, states, query_scr, forget_scr, value_scr,
    sems,
):
    pairs = ((conv_hbm, conv_ref), (bias_hbm, bias_ref), (gain_hbm, gain_ref))
    copies = [
        pltpu.make_async_copy(src, dst, sems.at[i]) for i, (src, dst) in enumerate(pairs)
    ]
    for copy in copies:
        copy.start()
    for copy in copies:
        copy.wait()
    own_refs = (near_ref, far_ref)
    prepare(
        range(HALF), own_refs, window, conv_ref, bias_ref, near_query, near_forget, near_value
    )
    prepare(
        range(HALF, ROWS), own_refs, window, conv_ref, bias_ref, query_ref, forget_ref, value_ref
    )

    def store(slot, head, block):
        mixed_ref[slot, :, block_of(head)] = block

    mix(
        0, owner_ref, near_ref, from_near_ref, near_query, near_forget, near_value, conv_ref,
        gain_ref, edges, states, query_scr, forget_scr, value_scr, store,
    )


def mix_near_call(owner, near, far, from_near, conv, bias, gain):
    shape = jax.ShapeDtypeStruct
    rows = (HALF, 2, DRAFT, DK)
    copied = [shape(x.shape, x.dtype) for x in (conv, bias, gain)]
    return call(
        mix_near,
        (shape((HALF, DRAFT, 2 * DK), BF), *[shape(rows, F32)] * 3, *copied),
        [SM, VM, VM, VM, HB, HB, HB],
        [pltpu.VMEM((ROWS, 3, 40, DK), F32)]
        + [pltpu.VMEM(rows, F32)] * 3
        + MIX_SCRATCH
        + [pltpu.SemaphoreType.DMA((3,))],
        15_000_000, 3_000_000, owner, near, far, from_near, conv, bias, gain,
    )


def mix_far(
    owner_ref, near_mixed_ref, far_ref, from_far_ref, query_ref, forget_ref, value_ref,
    conv_ref, gain_ref, weight_ref, mixed_ref, part_ref,
    edges, states, query_scr, forget_scr, value_scr,
):
    parity = lax.axis_index("req") % 2
    for slot in range(HALF):
        mixed_ref[row_of(0, slot)] = near_mixed_ref[slot]

    def store(slot, head, block):
        mixed_ref[parity * HALF + slot, :, block_of(head)] = block

    mix(
        1, owner_ref, far_ref, from_far_ref, query_ref, forget_ref, value_ref, conv_ref,
        gain_ref, edges, states, query_scr, forget_scr, value_scr, store,
    )
    rows = mixed_ref[...].reshape(ROWS * DRAFT, 2 * DK)
    block = weight_ref[:, columns_of(2, part_ref.shape[1])]
    part_ref[...] = jnp.dot(rows, block, preferred_element_type=F32).astype(BF)


def mix_far_call(owner, near_mixed, far, from_far, queries, forget, values, conv, gain, weight):
    shape = jax.ShapeDtypeStruct
    return call(
        mix_far,
        (
            shape((ROWS, DRAFT, 2 * DK), BF),
            shape((ROWS * DRAFT, weight.shape[1] // 4), BF),
        ),
        [SM] + [VM] * 9, MIX_SCRATCH,
        50_000_000, 2_000_000,
        owner, near_mixed, far, from_far, queries, forget, values, conv, gain, weight,
    )


def fetch(*refs):
    count = len(refs) // 2
    sems = refs[-1]
    copies = [
        pltpu.make_async_copy(refs[i], refs[count + i], sems.at[i]) for i in range(count)
    ]
    for copy in copies:
        copy.start()
    for copy in copies:
        copy.wait()


def fetch_call(*arrays):
    return call(
        fetch, tuple(jax.ShapeDtypeStruct(x.shape, x.dtype) for x in arrays), [HB] * len(arrays),
        [pltpu.SemaphoreType.DMA((len(arrays),))], 0, 17_000_000, *arrays,
    )


def mixer(
    owner_ref, near_ref, far_ref, from_near_ref, from_far_ref, query_ref, forget_ref, value_ref,
    conv_ref, bias_ref, gain_ref, mixed_ref, edges, states, query_scr, forget_scr, value_scr,
):
    half = DRAFT // 2
    for slot in range(ROWS):
        side = slot // HALF
        _, local, place = source_of(owner_ref, row_of(side, slot % HALF))
        mine_ref, other_ref = (near_ref, from_near_ref) if side == 0 else (far_ref, from_far_ref)
        for block in range(3):
            mine = mine_ref[slot % HALF, edges_of(block), :].astype(F32)
            other = other_ref[place, edges_of(block), :].astype(F32)
            edges[slot, block, :DRAFT, :] = jnp.where(local, mine, other)
            edges[slot, block, DRAFT:, :] = jnp.zeros((8, DK), F32)

        @pl.when(local)
        def _():
            states[slot] = mine_ref[slot % HALF, : 2 * DK, :]

        @pl.when(jnp.logical_not(local))
        def _():
            states[slot] = other_ref[place, : 2 * DK, :]

    sub_iota = lax.broadcasted_iota(jnp.int32, (1, DRAFT, DK), 1)

    def pair(step, _):
        base = step * 2
        for sub in range(2):
            slot = base + sub
            for head in range(2):
                lane = sub * 2 + head
                for block, (in_ref, out, act) in enumerate(
                    (
                        (query_ref, query_scr, as_query),
                        (forget_ref, forget_scr, jax.nn.sigmoid),
                        (value_ref, value_scr, as_value),
                    )
                ):
                    first = in_ref[slot, head, :half]
                    for shift in range(CONV - 1):
                        taps = conv_ref[shift, head, block_of(block)]
                        rows = edges[slot, block, pl.ds(2 * shift + head, half, stride=2), :]
                        first = first + taps[None, :] * rows
                    out[lane, :half] = act(first)
                    out[lane, half:] = in_ref[slot, head, half:]
        queries = query_scr[...]
        forget = forget_scr[...]
        values = value_scr[...]
        weights = jnp.zeros((4, DRAFT, DK), F32)
        decay = jnp.ones((4, 1, DK), F32)
        head_rows = []
        query_rows = []
        for t in range(DRAFT):
            forget_t = forget[:, t : t + 1, :]
            query_t = queries[:, t : t + 1, :]
            decay = decay * forget_t
            weights = jnp.where(sub_iota == t, 1.0 - forget_t, weights * forget_t)
            scores = jnp.sum(weights * query_t, axis=-1, keepdims=True)
            head_rows.append(jnp.sum(scores * values, axis=1, keepdims=True))
            query_rows.append(query_t * decay)
        local_out = jnp.concatenate(head_rows, axis=1)
        decayed = jnp.concatenate(query_rows, axis=1)
        for sub in range(2):
            slot = base + sub
            parity = lax.axis_index("req") % 2
            near_row = (1 - parity) * HALF + slot
            far_row = parity * HALF + slot - HALF
            row = jnp.where(slot < HALF, near_row, far_row)
            for head in range(2):
                lane = sub * 2 + head
                fine = decayed[lane]
                coarse = fine.astype(BF)
                stacked = jnp.concatenate([coarse, (fine - coarse.astype(F32)).astype(BF)], axis=0)
                both = jnp.dot(
                    stacked, states[slot, block_of(head), :], preferred_element_type=F32
                )
                out = local_out[lane] + (both[:DRAFT] + both[DRAFT:])
                scale = lax.rsqrt(jnp.mean(out * out, axis=-1, keepdims=True) + 1e-05)
                mixed_ref[row, :, block_of(head)] = (
                    out * scale * gain_ref[head, :][None, :]
                ).astype(BF)
        return 0

    lax.fori_loop(0, ROWS // 2, pair, 0)


def mixer_call(owner, near, far, from_near, from_far, queries, forget, values, conv, bias, gain):
    return call(
        mixer, jax.ShapeDtypeStruct((ROWS, DRAFT, 2 * DK), BF), [SM] + [VM] * 10,
        [
            pltpu.VMEM((ROWS, 3, 24, DK), F32),
            pltpu.VMEM((ROWS, 2 * DK, DK), BF),
            pltpu.VMEM((4, DRAFT, DK), F32),
            pltpu.VMEM((4, DRAFT, DK), F32),
            pltpu.VMEM((4, DRAFT, DK), F32),
        ],
        20_000_000, 2_000_000,
        owner, near, far, from_near, from_far, queries, forget, values, conv, bias, gain,
    )


def later(x, shift):
    return jnp.concatenate([x[shift:], jnp.ones((shift, DK), F32)], axis=0)


def split(x):
    coarse = x.astype(BF)
    return coarse, (x - coarse.astype(F32)).astype(BF)


def keep(
    owner_ref, accept_ref, near_ref, far_ref, from_near_ref, from_far_ref, state_ref, conv_ref,
    bias_ref, kept_ref, edges_out_ref, states, window, left, right, decays, sems,
):
    state_copies = [
        pltpu.make_async_copy(state_ref.at[row], states.at[row], sems.at[row])
        for row in range(ROWS)
    ]
    for copy in state_copies:
        copy.start()
    position = lax.broadcasted_iota(jnp.int32, (DRAFT, DK), 0)
    for slot in range(ROWS):
        side = slot // HALF
        row = row_of(side, slot % HALF)
        partner, local, place = source_of(owner_ref, row)
        length = accept_ref[partner]
        mine_ref, other_ref = (near_ref, from_near_ref) if side == 0 else (far_ref, from_far_ref)
        for block in range(3):
            mine = mine_ref[slot % HALF, drafts_of(block), :].astype(F32)
            other = other_ref[place, drafts_of(block), :].astype(F32)
            window[slot, block, 8:, :] = jnp.where(local, mine, other)
            window[slot, block, 2:8, :] = mine_ref[slot % HALF, edges_of(block), :].astype(F32)[:6]
        for head in range(2):
            gates = convolve(window, conv_ref, slot, head, 1) + bias_ref[head, :][None, :]
            values = as_value(convolve(window, conv_ref, slot, head, 2))
            forget = jax.nn.sigmoid(gates)
            inside = position < length
            weights = jnp.where(inside, 1.0 - forget, 0.0)
            factors = jnp.where(inside, forget, 1.0)
            after = later(factors, 1)
            for shift in (1, 2, 4, 8):
                after = after * later(after, shift)
            weight_high, weight_low = split(weights * after)
            value_high, value_low = split(values)
            left[slot, head] = jnp.concatenate([weight_high, weight_low, weight_high], axis=0)
            right[slot, head] = jnp.concatenate([value_high, value_high, value_low], axis=0)
            lane = 2 * slot + head
            decays[lane : lane + 1, :] = (factors * after)[:1, :]
        for block in range(3):
            turned = pltpu.roll(window[slot, block], 38 - 2 * length, 0)
            for step in range(CONV - 1):
                edges_out_ref[row, step, :, block_of(block)] = turned[
                    2 * step : 2 * step + 2
                ].astype(BF)
    columns = jnp.transpose(decays[...])
    for copy in state_copies:
        copy.wait()
    for slot in range(ROWS):
        row = row_of(slot // HALF, slot % HALF)
        for head in range(2):
            lane = 2 * slot + head
            update = lax.dot_general(
                left[slot, head], right[slot, head], (((0,), (0,)), ((), ())),
                preferred_element_type=F32,
            )
            kept_ref[row, head] = columns[:, lane : lane + 1] * states[row, head] + update


def keep_call(owner, accept, near, far, from_near, from_far, states, conv, bias):
    shape = jax.ShapeDtypeStruct
    return call(
        keep, (shape(states.shape, F32), shape((ROWS, CONV - 1, 2, 3 * DK), BF)),
        [SM, SM, VM, VM, VM, VM, HB, VM, VM],
        [
            pltpu.VMEM(states.shape, F32),
            pltpu.VMEM((ROWS, 3, 40, DK), F32),
            pltpu.VMEM((ROWS, 2, 3 * DRAFT, DK), BF),
            pltpu.VMEM((ROWS, 2, 3 * DRAFT, DK), BF),
            pltpu.VMEM((2 * ROWS, DK), F32),
            pltpu.SemaphoreType.DMA((ROWS,)),
        ],
        20_000_000, 3_000_000, owner, accept, near, far, from_near, from_far, states, conv, bias,
    )


def project(
    own_ref, one_ref, three_ref, weight_ref, from_one_ref, from_three_ref, part_ref,
    resid_ref, stream_ref,
):
    width = stream_ref.shape[1]
    columns = columns_of(0, width)
    total = jnp.dot(own_ref[...], weight_ref[:, columns], preferred_element_type=F32)
    total = total + jnp.dot(one_ref[...], from_one_ref[...], preferred_element_type=F32)
    total = total + jnp.dot(three_ref[...], from_three_ref[...], preferred_element_type=F32)
    total = total + part_ref[...].astype(F32)
    stream_ref[...] = (resid_ref[:, columns].astype(F32) + total).astype(BF)


def project_call(mixed, one, three, weight, parts, part, resid):
    slots, model = resid.shape
    return call(
        project, jax.ShapeDtypeStruct((slots, model // 4), BF), [VM] * 8, [],
        100_000_000, 3_000_000, mixed, one, three, weight, *parts, part, resid,
    )


def ffn_kernel(
    length_ref, own_ref, next_ref, far_ref, prev_ref, gain_ref, gate_ref, up_ref, down_ref,
    own_out_ref, next_out_ref, far_out_ref, prev_out_ref, normed_scr,
):
    width = own_ref.shape[1]
    parts = ((0, own_ref), (1, next_ref), (2, far_ref), (3, prev_ref))
    total = None
    for _, ref in parts:
        block = ref[...].astype(F32)
        square = jnp.sum(block * block, axis=-1, keepdims=True)
        total = square if total is None else total + square
    scale = lax.rsqrt(total / (4 * width) + 1e-05)
    for step, ref in parts:
        columns = columns_of(step, width)
        normed_scr[:, columns] = (ref[...].astype(F32) * scale * gain_ref[:, columns]).astype(BF)
    normed = normed_scr[...]
    dims = (((1,), (1,)), ((), ()))
    gate = lax.dot_general(normed, gate_ref[...], dims, preferred_element_type=F32)
    up = lax.dot_general(normed, up_ref[...], dims, preferred_element_type=F32)
    hidden = (gate * jax.nn.sigmoid(gate) * up).astype(BF)
    me = lax.axis_index("req")
    position = lax.broadcasted_iota(jnp.int32, (DRAFT, 1), 0)
    live = jnp.concatenate(
        [(position < length_ref[me * ROWS + row]).astype(F32) for row in range(ROWS)], axis=0
    )
    for step, out_ref in ((2, far_out_ref), (1, next_out_ref), (3, prev_out_ref)):
        part = jnp.dot(hidden, down_ref[:, columns_of(step, width)], preferred_element_type=F32)
        out_ref[...] = (part * live).astype(BF)
    part = jnp.dot(hidden, down_ref[:, columns_of(0, width)], preferred_element_type=F32)
    own_out_ref[...] = (part + own_ref[...].astype(F32)) * live


def ffn(lengths, own, following, far, preceding, gain, gate_t, up_t, down):
    slots, width = own.shape
    shape = jax.ShapeDtypeStruct
    return pl.pallas_call(
        ffn_kernel,
        name="ffn",
        out_shape=(
            shape((slots, width), F32),
            shape((slots, width), BF),
            shape((slots, width), BF),
            shape((slots, width), BF),
        ),
        in_specs=[SM] + [VM] * 8,
        out_specs=tuple([VM] * 4),
        scratch_shapes=[pltpu.VMEM((slots, 4 * width), BF)],
        compiler_params=PARAMS,
        cost_estimate=pl.CostEstimate(
            flops=1_100_000_000, bytes_accessed=9_000_000, transcendentals=100_000
        ),
    )(lengths, own, following, far, preceding, gain, gate_t, up_t, down)


def in_hbm(array):
    return pltpu.with_memory_space_constraint(array, pltpu.HBM)


def swapped(block, step):
    return lax.ppermute(block, "grp", [(i, i ^ step) for i in range(4)])


def shards(
    mix_inputs,
    conv_weight,
    forget_bias,
    norm_gain,
    out_weight,
    resid,
    ffn_gain,
    gate_weight,
    up_weight,
    down_weight,
    held_states,
    held_edges,
    draft_lengths,
    accepted,
    owner_row,
):
    slots = ROWS * DRAFT
    owner_row, accepted, draft_lengths = in_hbm(owner_row), in_hbm(accepted), in_hbm(draft_lengths)
    count = lax.axis_size("req")
    states = in_hbm(held_states)
    far, near, *cuts = pack_call(
        states, in_hbm(held_edges), in_hbm(mix_inputs), in_hbm(out_weight)
    )
    across = [(i, (i + (1 if i % 2 else -1)) % count) for i in range(count)]
    from_far = lax.ppermute(far, "req", across)
    from_near = lax.ppermute(near, "req", [(i, i ^ 1) for i in range(count)])
    parts = [swapped(cut, step) for step, cut in ((1, cuts[0]), (3, cuts[1]))]
    near_mixed, queries, forget, values, conv, bias, gain = mix_near_call(
        owner_row, near, far, from_near,
        in_hbm(conv_weight), in_hbm(forget_bias), in_hbm(norm_gain),
    )
    mixed, part = mix_far_call(
        owner_row, near_mixed, far, from_far, queries, forget, values, conv, gain, out_weight
    )
    mixed = mixed.reshape(slots, -1)
    mixed, part, gate_weight, up_weight, down_weight = lax.optimization_barrier(
        (mixed, part, gate_weight, up_weight, down_weight)
    )
    part = swapped(part, 2)
    one = swapped(mixed, 1)
    three = swapped(mixed, 3)
    gate_t, up_t, down = fetch_call(
        in_hbm(gate_weight.T), in_hbm(up_weight.T), in_hbm(down_weight)
    )
    part, one, three, gate_t, up_t, down = lax.optimization_barrier(
        (part, one, three, gate_t, up_t, down)
    )
    stream = project_call(mixed, one, three, out_weight, parts, part, resid.reshape(slots, -1))
    stream, from_near, from_far = lax.optimization_barrier((stream, from_near, from_far))
    two = swapped(stream, 2)
    one = swapped(stream, 1)
    three = swapped(stream, 3)
    kept_states, kept_edges = keep_call(
        owner_row, accepted, near, far, from_near, from_far, states, conv, bias
    )
    one, two, three, kept_states, kept_edges = lax.optimization_barrier(
        (one, two, three, kept_states, kept_edges)
    )
    own_part, to_one, to_two, to_three = ffn(
        draft_lengths, stream, one, two, three, ffn_gain[None, :], gate_t, up_t, down
    )
    two = swapped(to_two, 2)
    one = swapped(to_one, 1)
    three = swapped(to_three, 3)
    layer_out = (own_part + two.astype(F32) + one.astype(F32) + three.astype(F32)).astype(BF)
    return (layer_out.reshape(ROWS, DRAFT, -1), kept_states, kept_edges)


def solution(mesh):
    return jax.shard_map(
        shards,
        mesh=mesh,
        in_specs=(
            P("req", None, "grp", None),
            P(None, "grp", None),
            P("grp", None),
            P("grp", None),
            P("grp", None),
            P("req", None, None),
            P(),
            P(None, "grp"),
            P(None, "grp"),
            P("grp", None),
            P("req", "grp", None, None),
            P("req", None, "grp", None),
            P(),
            P(),
            P(),
        ),
        out_specs=(P("req", None, "grp"), P("req", "grp", None, None), P("req", None, "grp", None)),
        check_vma=False,
    )
```

```python
import jax
import jax.numpy as jnp
from jax import lax
from jax.experimental import pallas as pl
from jax.experimental.pallas import tpu as pltpu
from jax.sharding import PartitionSpec as P

DK = 128
DRAFT = 16
CONV = 4
HALF = 4
ROWS = 2 * HALF
BF = jnp.bfloat16
PARAMS = pltpu.CompilerParams(vmem_limit_bytes=12 * 1024 * 1024)
F32 = jnp.float32
EDGES_AT = 2 * DK
DRAFTS_AT = EDGES_AT + 3 * DRAFT
PACKED = DRAFTS_AT + 3 * 2 * DRAFT
VM = pl.BlockSpec(memory_space=pltpu.VMEM)
SM = pl.BlockSpec(memory_space=pltpu.SMEM)
HB = pl.BlockSpec(memory_space=pltpu.HBM)


def row_of(half, place):
    parity = lax.axis_index("req") % 2
    base = (1 - parity if half == 0 else parity) * HALF
    return base + place


def source_of(owner_ref, row):
    me = lax.axis_index("req")
    partner = owner_ref[me * ROWS + row]
    return partner, partner // ROWS == me, partner % HALF


def block_of(block):
    return slice(block * DK, (block + 1) * DK)


def edges_of(block):
    return slice(EDGES_AT + block * DRAFT, EDGES_AT + (block + 1) * DRAFT)


def drafts_of(block):
    return slice(DRAFTS_AT + block * 2 * DRAFT, DRAFTS_AT + (block + 1) * 2 * DRAFT)


def call(kernel, out_shape, in_specs, scratch, flops, moved, *args):
    return pl.pallas_call(
        kernel,
        name=kernel.__name__,
        out_shape=out_shape,
        in_specs=in_specs,
        out_specs=jax.tree.map(lambda _: VM, out_shape),
        scratch_shapes=scratch,
        compiler_params=PARAMS,
        cost_estimate=pl.CostEstimate(flops=flops, bytes_accessed=moved, transcendentals=0),
    )(*args)


def columns_of(step, width):
    place = lax.bitwise_xor(lax.axis_index("grp"), step)
    return pl.ds(pl.multiple_of(place * width, width), width)


def pack(
    state_ref, edge_ref, draft_ref, weight_ref, far_ref, near_ref, one_ref, three_ref,
    states, edges, drafts, sems,
):
    width = one_ref.shape[1]
    cuts = [
        pltpu.make_async_copy(
            weight_ref.at[:, columns_of(step, width)], out_ref, sems.at[ROWS + 2 + i]
        )
        for i, (step, out_ref) in enumerate(((1, one_ref), (3, three_ref)))
    ]
    copies = [
        pltpu.make_async_copy(state_ref.at[row], states.at[row], sems.at[row])
        for row in range(ROWS)
    ]
    edge_copy = pltpu.make_async_copy(edge_ref, edges, sems.at[ROWS])
    draft_copy = pltpu.make_async_copy(draft_ref, drafts, sems.at[ROWS + 1])
    draft_copy.start()
    edge_copy.start()
    for copy in copies:
        copy.start()
    for copy in cuts:
        copy.start()
    edge_copy.wait()
    draft_copy.wait()
    for half, out_ref in ((1, far_ref), (0, near_ref)):
        for place in range(HALF):
            row = row_of(half, place)
            for block in range(3):
                columns = block_of(block)
                out_ref[place, edges_of(block), :] = jnp.zeros((DRAFT, DK), BF)
                start = EDGES_AT + block * DRAFT
                for step in range(CONV - 1):
                    out_ref[place, start + 2 * step : start + 2 * step + 2, :] = edges[
                        row, step, :, columns
                    ]
                start = DRAFTS_AT + block * 2 * DRAFT
                for step in range(DRAFT):
                    out_ref[place, start + 2 * step : start + 2 * step + 2, :] = drafts[
                        row, step, :, columns
                    ]
    for copy in copies:
        copy.wait()
    for half, out_ref in ((1, far_ref), (0, near_ref)):
        for place in range(HALF):
            for head in range(2):
                out_ref[place, block_of(head), :] = states[row_of(half, place), head].astype(BF)
    for copy in cuts:
        copy.wait()


def pack_call(states, edges, drafts, weight):
    half = jax.ShapeDtypeStruct((HALF, PACKED, DK), BF)
    cut = jax.ShapeDtypeStruct((weight.shape[0], weight.shape[1] // 4), BF)
    return call(
        pack, (half, half, cut, cut), [HB] * 4,
        [
            pltpu.VMEM(states.shape, F32),
            pltpu.VMEM(edges.shape, BF),
            pltpu.VMEM(drafts.shape, BF),
            pltpu.SemaphoreType.DMA((ROWS + 4,)),
        ],
        1_000_000, 3_000_000, states, edges, drafts, weight,
    )


def convolve(window, conv_ref, slot, head, block):
    total = None
    for shift in range(CONV):
        taps = conv_ref[shift, head, block_of(block)]
        rows = window[slot, block, pl.ds(2 + 2 * shift + head, DRAFT, stride=2), :]
        term = taps[None, :] * rows
        total = term if total is None else total + term
    return total


def as_query(x):
    return x * jax.nn.sigmoid(x) * DK ** (-0.5)


def as_value(x):
    return x * jax.nn.sigmoid(x)


def prepare(slots, own_refs, window, conv_ref, bias_ref, query_ref, forget_ref, value_ref):
    for slot in slots:
        own_ref = own_refs[slot // HALF]
        for block in range(3):
            window[slot, block, :8, :] = jnp.zeros((8, DK), F32)
            window[slot, block, 8:, :] = own_ref[slot % HALF, drafts_of(block), :].astype(F32)
    half = DRAFT // 2
    for slot in slots:
        for head in range(2):
            queries, gates, values = [
                convolve(window, conv_ref, slot, head, block) for block in range(3)
            ]
            place = slot % HALF
            query_ref[place, head, :half] = queries[:half]
            query_ref[place, head, half:] = as_query(queries[half:])
            gates = gates + bias_ref[head, :][None, :]
            forget_ref[place, head, :half] = gates[:half]
            forget_ref[place, head, half:] = jax.nn.sigmoid(gates[half:])
            value_ref[place, head, :half] = values[:half]
            value_ref[place, head, half:] = as_value(values[half:])


def mix(
    side, owner_ref, mine_ref, other_ref, query_ref, forget_ref, value_ref, conv_ref, gain_ref,
    edges, states, query_scr, forget_scr, value_scr, store,
):
    half = DRAFT // 2
    for slot in range(HALF):
        _, local, place = source_of(owner_ref, row_of(side, slot))
        for block in range(3):
            mine = mine_ref[slot, edges_of(block), :].astype(F32)
            other = other_ref[place, edges_of(block), :].astype(F32)
            edges[slot, block, :DRAFT, :] = jnp.where(local, mine, other)
            edges[slot, block, DRAFT:, :] = jnp.zeros((8, DK), F32)

        @pl.when(local)
        def _():
            states[slot] = mine_ref[slot, : 2 * DK, :]

        @pl.when(jnp.logical_not(local))
        def _():
            states[slot] = other_ref[place, : 2 * DK, :]

    sub_iota = lax.broadcasted_iota(jnp.int32, (1, DRAFT, DK), 1)

    def pair(step, _):
        base = step * 2
        for sub in range(2):
            slot = base + sub
            for head in range(2):
                lane = sub * 2 + head
                for block, (in_ref, out, act) in enumerate(
                    (
                        (query_ref, query_scr, as_query),
                        (forget_ref, forget_scr, jax.nn.sigmoid),
                        (value_ref, value_scr, as_value),
                    )
                ):
                    first = in_ref[slot, head, :half]
                    for shift in range(CONV - 1):
                        taps = conv_ref[shift, head, block_of(block)]
                        rows = edges[slot, block, pl.ds(2 * shift + head, half, stride=2), :]
                        first = first + taps[None, :] * rows
                    out[lane, :half] = act(first)
                    out[lane, half:] = in_ref[slot, head, half:]
        queries = query_scr[...]
        forget = forget_scr[...]
        values = value_scr[...]
        weights = jnp.zeros((4, DRAFT, DK), F32)
        decay = jnp.ones((4, 1, DK), F32)
        head_rows = []
        query_rows = []
        for t in range(DRAFT):
            forget_t = forget[:, t : t + 1, :]
            query_t = queries[:, t : t + 1, :]
            decay = decay * forget_t
            weights = jnp.where(sub_iota == t, 1.0 - forget_t, weights * forget_t)
            scores = jnp.sum(weights * query_t, axis=-1, keepdims=True)
            head_rows.append(jnp.sum(scores * values, axis=1, keepdims=True))
            query_rows.append(query_t * decay)
        local_out = jnp.concatenate(head_rows, axis=1)
        decayed = jnp.concatenate(query_rows, axis=1)
        for sub in range(2):
            slot = base + sub
            for head in range(2):
                lane = sub * 2 + head
                fine = decayed[lane]
                coarse = fine.astype(BF)
                stacked = jnp.concatenate([coarse, (fine - coarse.astype(F32)).astype(BF)], axis=0)
                both = jnp.dot(
                    stacked, states[slot, block_of(head), :], preferred_element_type=F32
                )
                out = local_out[lane] + (both[:DRAFT] + both[DRAFT:])
                scale = lax.rsqrt(jnp.mean(out * out, axis=-1, keepdims=True) + 1e-05)
                store(slot, head, (out * scale * gain_ref[head, :][None, :]).astype(BF))
        return 0

    lax.fori_loop(0, HALF // 2, pair, 0)


MIX_SCRATCH = [
    pltpu.VMEM((HALF, 3, 24, DK), F32),
    pltpu.VMEM((HALF, 2 * DK, DK), BF),
    pltpu.VMEM((4, DRAFT, DK), F32),
    pltpu.VMEM((4, DRAFT, DK), F32),
    pltpu.VMEM((4, DRAFT, DK), F32),
]


def mix_near(
    owner_ref, near_ref, far_ref, from_near_ref, conv_hbm, bias_hbm, gain_hbm,
    mixed_ref, query_ref, forget_ref, value_ref, conv_ref, bias_ref, gain_ref,
    window, near_query, near_forget, near_value, edges, states, query_scr, forget_scr, value_scr,
    sems,
):
    pairs = ((conv_hbm, conv_ref), (bias_hbm, bias_ref), (gain_hbm, gain_ref))
    copies = [
        pltpu.make_async_copy(src, dst, sems.at[i]) for i, (src, dst) in enumerate(pairs)
    ]
    for copy in copies:
        copy.start()
    for copy in copies:
        copy.wait()
    own_refs = (near_ref, far_ref)
    prepare(
        range(HALF), own_refs, window, conv_ref, bias_ref, near_query, near_forget, near_value
    )
    prepare(
        range(HALF, ROWS), own_refs, window, conv_ref, bias_ref, query_ref, forget_ref, value_ref
    )

    def store(slot, head, block):
        mixed_ref[slot, :, block_of(head)] = block

    mix(
        0, owner_ref, near_ref, from_near_ref, near_query, near_forget, near_value, conv_ref,
        gain_ref, edges, states, query_scr, forget_scr, value_scr, store,
    )


def mix_near_call(owner, near, far, from_near, conv, bias, gain):
    shape = jax.ShapeDtypeStruct
    rows = (HALF, 2, DRAFT, DK)
    copied = [shape(x.shape, x.dtype) for x in (conv, bias, gain)]
    return call(
        mix_near,
        (shape((HALF, DRAFT, 2 * DK), BF), *[shape(rows, F32)] * 3, *copied),
        [SM, VM, VM, VM, HB, HB, HB],
        [pltpu.VMEM((ROWS, 3, 40, DK), F32)]
        + [pltpu.VMEM(rows, F32)] * 3
        + MIX_SCRATCH
        + [pltpu.SemaphoreType.DMA((3,))],
        15_000_000, 3_000_000, owner, near, far, from_near, conv, bias, gain,
    )


def mix_far(
    owner_ref, near_mixed_ref, far_ref, from_far_ref, query_ref, forget_ref, value_ref,
    conv_ref, gain_ref, weight_ref, mixed_ref, part_ref,
    edges, states, query_scr, forget_scr, value_scr,
):
    parity = lax.axis_index("req") % 2
    for slot in range(HALF):
        mixed_ref[row_of(0, slot)] = near_mixed_ref[slot]

    def store(slot, head, block):
        mixed_ref[parity * HALF + slot, :, block_of(head)] = block

    mix(
        1, owner_ref, far_ref, from_far_ref, query_ref, forget_ref, value_ref, conv_ref,
        gain_ref, edges, states, query_scr, forget_scr, value_scr, store,
    )
    rows = mixed_ref[...].reshape(ROWS * DRAFT, 2 * DK)
    block = weight_ref[:, columns_of(2, part_ref.shape[1])]
    part_ref[...] = jnp.dot(rows, block, preferred_element_type=F32).astype(BF)


def mix_far_call(owner, near_mixed, far, from_far, queries, forget, values, conv, gain, weight):
    shape = jax.ShapeDtypeStruct
    return call(
        mix_far,
        (
            shape((ROWS, DRAFT, 2 * DK), BF),
            shape((ROWS * DRAFT, weight.shape[1] // 4), BF),
        ),
        [SM] + [VM] * 9, MIX_SCRATCH,
        50_000_000, 2_000_000,
        owner, near_mixed, far, from_far, queries, forget, values, conv, gain, weight,
    )


def fetch(*refs):
    count = len(refs) // 2
    sems = refs[-1]
    copies = [
        pltpu.make_async_copy(refs[i], refs[count + i], sems.at[i]) for i in range(count)
    ]
    for copy in copies:
        copy.start()
    for copy in copies:
        copy.wait()


def fetch_call(*arrays):
    return call(
        fetch, tuple(jax.ShapeDtypeStruct(x.shape, x.dtype) for x in arrays), [HB] * len(arrays),
        [pltpu.SemaphoreType.DMA((len(arrays),))], 0, 17_000_000, *arrays,
    )


def mixer(
    owner_ref, near_ref, far_ref, from_near_ref, from_far_ref, query_ref, forget_ref, value_ref,
    conv_ref, bias_ref, gain_ref, mixed_ref, edges, states, query_scr, forget_scr, value_scr,
):
    half = DRAFT // 2
    for slot in range(ROWS):
        side = slot // HALF
        _, local, place = source_of(owner_ref, row_of(side, slot % HALF))
        mine_ref, other_ref = (near_ref, from_near_ref) if side == 0 else (far_ref, from_far_ref)
        for block in range(3):
            mine = mine_ref[slot % HALF, edges_of(block), :].astype(F32)
            other = other_ref[place, edges_of(block), :].astype(F32)
            edges[slot, block, :DRAFT, :] = jnp.where(local, mine, other)
            edges[slot, block, DRAFT:, :] = jnp.zeros((8, DK), F32)

        @pl.when(local)
        def _():
            states[slot] = mine_ref[slot % HALF, : 2 * DK, :]

        @pl.when(jnp.logical_not(local))
        def _():
            states[slot] = other_ref[place, : 2 * DK, :]

    sub_iota = lax.broadcasted_iota(jnp.int32, (1, DRAFT, DK), 1)

    def pair(step, _):
        base = step * 2
        for sub in range(2):
            slot = base + sub
            for head in range(2):
                lane = sub * 2 + head
                for block, (in_ref, out, act) in enumerate(
                    (
                        (query_ref, query_scr, as_query),
                        (forget_ref, forget_scr, jax.nn.sigmoid),
                        (value_ref, value_scr, as_value),
                    )
                ):
                    first = in_ref[slot, head, :half]
                    for shift in range(CONV - 1):
                        taps = conv_ref[shift, head, block_of(block)]
                        rows = edges[slot, block, pl.ds(2 * shift + head, half, stride=2), :]
                        first = first + taps[None, :] * rows
                    out[lane, :half] = act(first)
                    out[lane, half:] = in_ref[slot, head, half:]
        queries = query_scr[...]
        forget = forget_scr[...]
        values = value_scr[...]
        weights = jnp.zeros((4, DRAFT, DK), F32)
        decay = jnp.ones((4, 1, DK), F32)
        head_rows = []
        query_rows = []
        for t in range(DRAFT):
            forget_t = forget[:, t : t + 1, :]
            query_t = queries[:, t : t + 1, :]
            decay = decay * forget_t
            weights = jnp.where(sub_iota == t, 1.0 - forget_t, weights * forget_t)
            scores = jnp.sum(weights * query_t, axis=-1, keepdims=True)
            head_rows.append(jnp.sum(scores * values, axis=1, keepdims=True))
            query_rows.append(query_t * decay)
        local_out = jnp.concatenate(head_rows, axis=1)
        decayed = jnp.concatenate(query_rows, axis=1)
        for sub in range(2):
            slot = base + sub
            parity = lax.axis_index("req") % 2
            near_row = (1 - parity) * HALF + slot
            far_row = parity * HALF + slot - HALF
            row = jnp.where(slot < HALF, near_row, far_row)
            for head in range(2):
                lane = sub * 2 + head
                fine = decayed[lane]
                coarse = fine.astype(BF)
                stacked = jnp.concatenate([coarse, (fine - coarse.astype(F32)).astype(BF)], axis=0)
                both = jnp.dot(
                    stacked, states[slot, block_of(head), :], preferred_element_type=F32
                )
                out = local_out[lane] + (both[:DRAFT] + both[DRAFT:])
                scale = lax.rsqrt(jnp.mean(out * out, axis=-1, keepdims=True) + 1e-05)
                mixed_ref[row, :, block_of(head)] = (
                    out * scale * gain_ref[head, :][None, :]
                ).astype(BF)
        return 0

    lax.fori_loop(0, ROWS // 2, pair, 0)


def mixer_call(owner, near, far, from_near, from_far, queries, forget, values, conv, bias, gain):
    return call(
        mixer, jax.ShapeDtypeStruct((ROWS, DRAFT, 2 * DK), BF), [SM] + [VM] * 10,
        [
            pltpu.VMEM((ROWS, 3, 24, DK), F32),
            pltpu.VMEM((ROWS, 2 * DK, DK), BF),
            pltpu.VMEM((4, DRAFT, DK), F32),
            pltpu.VMEM((4, DRAFT, DK), F32),
            pltpu.VMEM((4, DRAFT, DK), F32),
        ],
        20_000_000, 2_000_000,
        owner, near, far, from_near, from_far, queries, forget, values, conv, bias, gain,
    )


def later(x, shift):
    return jnp.concatenate([x[shift:], jnp.ones((shift, DK), F32)], axis=0)


def split(x):
    coarse = x.astype(BF)
    return coarse, (x - coarse.astype(F32)).astype(BF)


def keep(
    owner_ref, accept_ref, near_ref, far_ref, from_near_ref, from_far_ref, state_ref, conv_ref,
    bias_ref, kept_ref, edges_out_ref, states, window, left, right, decays, sems,
):
    state_copies = [
        pltpu.make_async_copy(state_ref.at[row], states.at[row], sems.at[row])
        for row in range(ROWS)
    ]
    for copy in state_copies:
        copy.start()
    position = lax.broadcasted_iota(jnp.int32, (DRAFT, DK), 0)
    for slot in range(ROWS):
        side = slot // HALF
        row = row_of(side, slot % HALF)
        partner, local, place = source_of(owner_ref, row)
        length = accept_ref[partner]
        mine_ref, other_ref = (near_ref, from_near_ref) if side == 0 else (far_ref, from_far_ref)
        for block in range(3):
            mine = mine_ref[slot % HALF, drafts_of(block), :].astype(F32)
            other = other_ref[place, drafts_of(block), :].astype(F32)
            window[slot, block, 8:, :] = jnp.where(local, mine, other)
            window[slot, block, 2:8, :] = mine_ref[slot % HALF, edges_of(block), :].astype(F32)[:6]
        for head in range(2):
            gates = convolve(window, conv_ref, slot, head, 1) + bias_ref[head, :][None, :]
            values = as_value(convolve(window, conv_ref, slot, head, 2))
            forget = jax.nn.sigmoid(gates)
            inside = position < length
            weights = jnp.where(inside, 1.0 - forget, 0.0)
            factors = jnp.where(inside, forget, 1.0)
            after = later(factors, 1)
            for shift in (1, 2, 4, 8):
                after = after * later(after, shift)
            weight_high, weight_low = split(weights * after)
            value_high, value_low = split(values)
            left[slot, head] = jnp.concatenate([weight_high, weight_low, weight_high], axis=0)
            right[slot, head] = jnp.concatenate([value_high, value_high, value_low], axis=0)
            lane = 2 * slot + head
            decays[lane : lane + 1, :] = (factors * after)[:1, :]
        for block in range(3):
            turned = pltpu.roll(window[slot, block], 38 - 2 * length, 0)
            for step in range(CONV - 1):
                edges_out_ref[row, step, :, block_of(block)] = turned[
                    2 * step : 2 * step + 2
                ].astype(BF)
    columns = jnp.transpose(decays[...])
    for copy in state_copies:
        copy.wait()
    for slot in range(ROWS):
        row = row_of(slot // HALF, slot % HALF)
        for head in range(2):
            lane = 2 * slot + head
            update = lax.dot_general(
                left[slot, head], right[slot, head], (((0,), (0,)), ((), ())),
                preferred_element_type=F32,
            )
            kept_ref[row, head] = columns[:, lane : lane + 1] * states[row, head] + update


def keep_call(owner, accept, near, far, from_near, from_far, states, conv, bias):
    shape = jax.ShapeDtypeStruct
    return call(
        keep, (shape(states.shape, F32), shape((ROWS, CONV - 1, 2, 3 * DK), BF)),
        [SM, SM, VM, VM, VM, VM, HB, VM, VM],
        [
            pltpu.VMEM(states.shape, F32),
            pltpu.VMEM((ROWS, 3, 40, DK), F32),
            pltpu.VMEM((ROWS, 2, 3 * DRAFT, DK), BF),
            pltpu.VMEM((ROWS, 2, 3 * DRAFT, DK), BF),
            pltpu.VMEM((2 * ROWS, DK), F32),
            pltpu.SemaphoreType.DMA((ROWS,)),
        ],
        20_000_000, 3_000_000, owner, accept, near, far, from_near, from_far, states, conv, bias,
    )


def project(
    own_ref, one_ref, three_ref, weight_ref, from_one_ref, from_three_ref, part_ref,
    resid_ref, stream_ref,
):
    width = stream_ref.shape[1]
    columns = columns_of(0, width)
    total = jnp.dot(own_ref[...], weight_ref[:, columns], preferred_element_type=F32)
    total = total + jnp.dot(one_ref[...], from_one_ref[...], preferred_element_type=F32)
    total = total + jnp.dot(three_ref[...], from_three_ref[...], preferred_element_type=F32)
    total = total + part_ref[...].astype(F32)
    stream_ref[...] = (resid_ref[:, columns].astype(F32) + total).astype(BF)


def project_call(mixed, one, three, weight, parts, part, resid):
    slots, model = resid.shape
    return call(
        project, jax.ShapeDtypeStruct((slots, model // 4), BF), [VM] * 8, [],
        100_000_000, 3_000_000, mixed, one, three, weight, *parts, part, resid,
    )


NT = (((1,), (1,)), ((), ()))


def gated(rows, step, gain_ref, gate_ref, up_ref):
    block = rows.astype(F32)
    square = jnp.sum(block * block, axis=-1, keepdims=True)
    columns = columns_of(step, rows.shape[1])
    scaled = (block * gain_ref[:, columns]).astype(BF)
    gate = lax.dot_general(scaled, gate_ref[:, columns], NT, preferred_element_type=F32)
    up = lax.dot_general(scaled, up_ref[:, columns], NT, preferred_element_type=F32)
    return square, gate, up


def ffn_first(
    own_ref, two_ref, three_ref, gain_ref, gate_ref, up_ref, square_ref, gate_out_ref, up_out_ref,
):
    total = None
    for step, ref in ((0, own_ref), (2, two_ref), (3, three_ref)):
        parts = gated(ref[...], step, gain_ref, gate_ref, up_ref)
        total = parts if total is None else [x + y for x, y in zip(total, parts)]
    square_ref[...] = jnp.broadcast_to(total[0], square_ref.shape)
    gate_out_ref[...] = total[1]
    up_out_ref[...] = total[2]


def ffn_first_call(own, two, three, gain, gate_t, up_t):
    slots, hidden = own.shape[0], gate_t.shape[0]
    shape = jax.ShapeDtypeStruct
    return call(
        ffn_first,
        (shape((slots, DK), F32), shape((slots, hidden), F32), shape((slots, hidden), F32)),
        [VM] * 6, [], 550_000_000, 5_000_000, own, two, three, gain, gate_t, up_t,
    )


def ffn_last(
    length_ref, own_ref, one_ref, gain_ref, gate_ref, up_ref, down_ref,
    square_ref, gate_in_ref, up_in_ref, own_out_ref, one_out_ref, two_out_ref, three_out_ref,
):
    width = own_ref.shape[1]
    square, gate, up = gated(one_ref[...], 1, gain_ref, gate_ref, up_ref)
    total = square + square_ref[:, :1]
    scale = lax.rsqrt(total / (4 * width) + 1e-05)
    gate = (gate + gate_in_ref[...]) * scale
    up = (up + up_in_ref[...]) * scale
    hidden = (gate * jax.nn.sigmoid(gate) * up).astype(BF)
    me = lax.axis_index("req")
    position = lax.broadcasted_iota(jnp.int32, (DRAFT, 1), 0)
    live = jnp.concatenate(
        [(position < length_ref[me * ROWS + row]).astype(F32) for row in range(ROWS)], axis=0
    )
    for step, out_ref in ((2, two_out_ref), (1, one_out_ref), (3, three_out_ref)):
        part = jnp.dot(hidden, down_ref[:, columns_of(step, width)], preferred_element_type=F32)
        out_ref[...] = (part * live).astype(BF)
    part = jnp.dot(hidden, down_ref[:, columns_of(0, width)], preferred_element_type=F32)
    own_out_ref[...] = (part + own_ref[...].astype(F32)) * live


def ffn_last_call(lengths, own, one, gain, gate_t, up_t, down, *partial):
    slots, width = own.shape
    shape = jax.ShapeDtypeStruct
    part = shape((slots, width), BF)
    return call(
        ffn_last, (shape((slots, width), F32), part, part, part), [SM] + [VM] * 9, [],
        550_000_000, 5_000_000, lengths, own, one, gain, gate_t, up_t, down, *partial,
    )


def in_hbm(array):
    return pltpu.with_memory_space_constraint(array, pltpu.HBM)


def swapped(block, step):
    return lax.ppermute(block, "grp", [(i, i ^ step) for i in range(4)])


def shards(
    mix_inputs,
    conv_weight,
    forget_bias,
    norm_gain,
    out_weight,
    resid,
    ffn_gain,
    gate_weight,
    up_weight,
    down_weight,
    held_states,
    held_edges,
    draft_lengths,
    accepted,
    owner_row,
):
    slots = ROWS * DRAFT
    owner_row, accepted, draft_lengths = in_hbm(owner_row), in_hbm(accepted), in_hbm(draft_lengths)
    count = lax.axis_size("req")
    states = in_hbm(held_states)
    far, near, *cuts = pack_call(
        states, in_hbm(held_edges), in_hbm(mix_inputs), in_hbm(out_weight)
    )
    across = [(i, (i + (1 if i % 2 else -1)) % count) for i in range(count)]
    from_far = lax.ppermute(far, "req", across)
    from_near = lax.ppermute(near, "req", [(i, i ^ 1) for i in range(count)])
    parts = [swapped(cut, step) for step, cut in ((1, cuts[0]), (3, cuts[1]))]
    near_mixed, queries, forget, values, conv, bias, gain = mix_near_call(
        owner_row, near, far, from_near,
        in_hbm(conv_weight), in_hbm(forget_bias), in_hbm(norm_gain),
    )
    mixed, part = mix_far_call(
        owner_row, near_mixed, far, from_far, queries, forget, values, conv, gain, out_weight
    )
    mixed = mixed.reshape(slots, -1)
    mixed, part, gate_weight, up_weight, down_weight = lax.optimization_barrier(
        (mixed, part, gate_weight, up_weight, down_weight)
    )
    part = swapped(part, 2)
    one = swapped(mixed, 1)
    three = swapped(mixed, 3)
    gate_t, up_t, down = fetch_call(
        in_hbm(gate_weight.T), in_hbm(up_weight.T), in_hbm(down_weight)
    )
    part, one, three, gate_t, up_t, down = lax.optimization_barrier(
        (part, one, three, gate_t, up_t, down)
    )
    stream = project_call(mixed, one, three, out_weight, parts, part, resid.reshape(slots, -1))
    two = swapped(stream, 2)
    three = swapped(stream, 3)
    one = swapped(stream, 1)
    gain_row = ffn_gain[None, :]
    partial = ffn_first_call(stream, two, three, gain_row, gate_t, up_t)
    own_part, to_one, to_two, to_three = ffn_last_call(
        draft_lengths, stream, one, gain_row, gate_t, up_t, down, *partial
    )
    two = swapped(to_two, 2)
    one = swapped(to_one, 1)
    three = swapped(to_three, 3)
    own_part, from_near, from_far = lax.optimization_barrier((own_part, from_near, from_far))
    kept_states, kept_edges = keep_call(
        owner_row, accepted, near, far, from_near, from_far, states, conv, bias
    )
    layer_out = (own_part + two.astype(F32) + one.astype(F32) + three.astype(F32)).astype(BF)
    return (layer_out.reshape(ROWS, DRAFT, -1), kept_states, kept_edges)


def solution(mesh):
    return jax.shard_map(
        shards,
        mesh=mesh,
        in_specs=(
            P("req", None, "grp", None),
            P(None, "grp", None),
            P("grp", None),
            P("grp", None),
            P("grp", None),
            P("req", None, None),
            P(),
            P(None, "grp"),
            P(None, "grp"),
            P("grp", None),
            P("req", "grp", None, None),
            P("req", None, "grp", None),
            P(),
            P(),
            P(),
        ),
        out_specs=(P("req", None, "grp"), P("req", "grp", None, None), P("req", None, "grp", None)),
        check_vma=False,
    )
```

```python
import jax
import jax.numpy as jnp
from jax import lax
from jax.experimental import pallas as pl
from jax.experimental.pallas import tpu as pltpu
from jax.sharding import PartitionSpec as P

DK = 128
DRAFT = 16
CONV = 4
HALF = 4
ROWS = 2 * HALF
BF = jnp.bfloat16
PARAMS = pltpu.CompilerParams(vmem_limit_bytes=12 * 1024 * 1024)
F32 = jnp.float32
EDGES_AT = 2 * DK
DRAFTS_AT = EDGES_AT + 3 * DRAFT
PACKED = DRAFTS_AT + 3 * 2 * DRAFT
VM = pl.BlockSpec(memory_space=pltpu.VMEM)
SM = pl.BlockSpec(memory_space=pltpu.SMEM)
HB = pl.BlockSpec(memory_space=pltpu.HBM)


def row_of(half, place):
    parity = lax.axis_index("req") % 2
    base = (1 - parity if half == 0 else parity) * HALF
    return base + place


def source_of(owner_ref, row):
    me = lax.axis_index("req")
    partner = owner_ref[me * ROWS + row]
    return partner, partner // ROWS == me, partner % HALF


def block_of(block):
    return slice(block * DK, (block + 1) * DK)


def edges_of(block):
    return slice(EDGES_AT + block * DRAFT, EDGES_AT + (block + 1) * DRAFT)


def drafts_of(block):
    return slice(DRAFTS_AT + block * 2 * DRAFT, DRAFTS_AT + (block + 1) * 2 * DRAFT)


def call(kernel, out_shape, in_specs, scratch, flops, moved, *args):
    return pl.pallas_call(
        kernel,
        name=kernel.__name__,
        out_shape=out_shape,
        in_specs=in_specs,
        out_specs=jax.tree.map(lambda _: VM, out_shape),
        scratch_shapes=scratch,
        compiler_params=PARAMS,
        cost_estimate=pl.CostEstimate(flops=flops, bytes_accessed=moved, transcendentals=0),
    )(*args)


def columns_of(step, width):
    place = lax.bitwise_xor(lax.axis_index("grp"), step)
    return pl.ds(pl.multiple_of(place * width, width), width)


def pack(
    state_ref, edge_ref, draft_ref, weight_ref, far_ref, near_ref, one_ref, three_ref,
    states, edges, drafts, sems,
):
    width = one_ref.shape[1]
    cuts = [
        pltpu.make_async_copy(
            weight_ref.at[:, columns_of(step, width)], out_ref, sems.at[ROWS + 2 + i]
        )
        for i, (step, out_ref) in enumerate(((1, one_ref), (3, three_ref)))
    ]
    copies = [
        pltpu.make_async_copy(state_ref.at[row], states.at[row], sems.at[row])
        for row in range(ROWS)
    ]
    edge_copy = pltpu.make_async_copy(edge_ref, edges, sems.at[ROWS])
    draft_copy = pltpu.make_async_copy(draft_ref, drafts, sems.at[ROWS + 1])
    draft_copy.start()
    edge_copy.start()
    for copy in copies:
        copy.start()
    for copy in cuts:
        copy.start()
    edge_copy.wait()
    draft_copy.wait()
    for half, out_ref in ((1, far_ref), (0, near_ref)):
        for place in range(HALF):
            row = row_of(half, place)
            for block in range(3):
                columns = block_of(block)
                out_ref[place, edges_of(block), :] = jnp.zeros((DRAFT, DK), BF)
                start = EDGES_AT + block * DRAFT
                for step in range(CONV - 1):
                    out_ref[place, start + 2 * step : start + 2 * step + 2, :] = edges[
                        row, step, :, columns
                    ]
                start = DRAFTS_AT + block * 2 * DRAFT
                for step in range(DRAFT):
                    out_ref[place, start + 2 * step : start + 2 * step + 2, :] = drafts[
                        row, step, :, columns
                    ]
    for copy in copies:
        copy.wait()
    for half, out_ref in ((1, far_ref), (0, near_ref)):
        for place in range(HALF):
            for head in range(2):
                out_ref[place, block_of(head), :] = states[row_of(half, place), head].astype(BF)
    for copy in cuts:
        copy.wait()


def pack_call(states, edges, drafts, weight):
    half = jax.ShapeDtypeStruct((HALF, PACKED, DK), BF)
    cut = jax.ShapeDtypeStruct((weight.shape[0], weight.shape[1] // 4), BF)
    return call(
        pack, (half, half, cut, cut), [HB] * 4,
        [
            pltpu.VMEM(states.shape, F32),
            pltpu.VMEM(edges.shape, BF),
            pltpu.VMEM(drafts.shape, BF),
            pltpu.SemaphoreType.DMA((ROWS + 4,)),
        ],
        1_000_000, 3_000_000, states, edges, drafts, weight,
    )


def convolve(window, conv_ref, slot, head, block):
    total = None
    for shift in range(CONV):
        taps = conv_ref[shift, head, block_of(block)]
        rows = window[slot, block, pl.ds(2 + 2 * shift + head, DRAFT, stride=2), :]
        term = taps[None, :] * rows
        total = term if total is None else total + term
    return total


def as_query(x):
    return x * jax.nn.sigmoid(x) * DK ** (-0.5)


def as_value(x):
    return x * jax.nn.sigmoid(x)


def prepare(slots, own_refs, window, conv_ref, bias_ref, query_ref, forget_ref, value_ref):
    for slot in slots:
        own_ref = own_refs[slot // HALF]
        for block in range(3):
            window[slot, block, :8, :] = jnp.zeros((8, DK), F32)
            window[slot, block, 8:, :] = own_ref[slot % HALF, drafts_of(block), :].astype(F32)
    half = DRAFT // 2
    for slot in slots:
        for head in range(2):
            queries, gates, values = [
                convolve(window, conv_ref, slot, head, block) for block in range(3)
            ]
            place = slot % HALF
            query_ref[place, head, :half] = queries[:half]
            query_ref[place, head, half:] = as_query(queries[half:])
            gates = gates + bias_ref[head, :][None, :]
            forget_ref[place, head, :half] = gates[:half]
            forget_ref[place, head, half:] = jax.nn.sigmoid(gates[half:])
            value_ref[place, head, :half] = values[:half]
            value_ref[place, head, half:] = as_value(values[half:])


def mix(
    side, owner_ref, mine_ref, other_ref, query_ref, forget_ref, value_ref, conv_ref, gain_ref,
    edges, states, query_scr, forget_scr, value_scr, store,
):
    half = DRAFT // 2
    for slot in range(HALF):
        _, local, place = source_of(owner_ref, row_of(side, slot))
        for block in range(3):
            mine = mine_ref[slot, edges_of(block), :].astype(F32)
            other = other_ref[place, edges_of(block), :].astype(F32)
            edges[slot, block, :DRAFT, :] = jnp.where(local, mine, other)
            edges[slot, block, DRAFT:, :] = jnp.zeros((8, DK), F32)

        @pl.when(local)
        def _():
            states[slot] = mine_ref[slot, : 2 * DK, :]

        @pl.when(jnp.logical_not(local))
        def _():
            states[slot] = other_ref[place, : 2 * DK, :]

    sub_iota = lax.broadcasted_iota(jnp.int32, (1, DRAFT, DK), 1)

    def pair(step, _):
        base = step * 2
        for sub in range(2):
            slot = base + sub
            for head in range(2):
                lane = sub * 2 + head
                for block, (in_ref, out, act) in enumerate(
                    (
                        (query_ref, query_scr, as_query),
                        (forget_ref, forget_scr, jax.nn.sigmoid),
                        (value_ref, value_scr, as_value),
                    )
                ):
                    first = in_ref[slot, head, :half]
                    for shift in range(CONV - 1):
                        taps = conv_ref[shift, head, block_of(block)]
                        rows = edges[slot, block, pl.ds(2 * shift + head, half, stride=2), :]
                        first = first + taps[None, :] * rows
                    out[lane, :half] = act(first)
                    out[lane, half:] = in_ref[slot, head, half:]
        queries = query_scr[...]
        forget = forget_scr[...]
        values = value_scr[...]
        weights = jnp.zeros((4, DRAFT, DK), F32)
        decay = jnp.ones((4, 1, DK), F32)
        head_rows = []
        query_rows = []
        for t in range(DRAFT):
            forget_t = forget[:, t : t + 1, :]
            query_t = queries[:, t : t + 1, :]
            decay = decay * forget_t
            weights = jnp.where(sub_iota == t, 1.0 - forget_t, weights * forget_t)
            scores = jnp.sum(weights * query_t, axis=-1, keepdims=True)
            head_rows.append(jnp.sum(scores * values, axis=1, keepdims=True))
            query_rows.append(query_t * decay)
        local_out = jnp.concatenate(head_rows, axis=1)
        decayed = jnp.concatenate(query_rows, axis=1)
        for sub in range(2):
            slot = base + sub
            for head in range(2):
                lane = sub * 2 + head
                fine = decayed[lane]
                coarse = fine.astype(BF)
                stacked = jnp.concatenate([coarse, (fine - coarse.astype(F32)).astype(BF)], axis=0)
                both = jnp.dot(
                    stacked, states[slot, block_of(head), :], preferred_element_type=F32
                )
                out = local_out[lane] + (both[:DRAFT] + both[DRAFT:])
                scale = lax.rsqrt(jnp.mean(out * out, axis=-1, keepdims=True) + 1e-05)
                store(slot, head, (out * scale * gain_ref[head, :][None, :]).astype(BF))
        return 0

    lax.fori_loop(0, HALF // 2, pair, 0)


MIX_SCRATCH = [
    pltpu.VMEM((HALF, 3, 24, DK), F32),
    pltpu.VMEM((HALF, 2 * DK, DK), BF),
    pltpu.VMEM((4, DRAFT, DK), F32),
    pltpu.VMEM((4, DRAFT, DK), F32),
    pltpu.VMEM((4, DRAFT, DK), F32),
]


def mix_near(
    owner_ref, near_ref, far_ref, from_near_ref, conv_hbm, bias_hbm, gain_hbm,
    mixed_ref, query_ref, forget_ref, value_ref, conv_ref, bias_ref, gain_ref,
    window, near_query, near_forget, near_value, edges, states, query_scr, forget_scr, value_scr,
    sems,
):
    pairs = ((conv_hbm, conv_ref), (bias_hbm, bias_ref), (gain_hbm, gain_ref))
    copies = [
        pltpu.make_async_copy(src, dst, sems.at[i]) for i, (src, dst) in enumerate(pairs)
    ]
    for copy in copies:
        copy.start()
    for copy in copies:
        copy.wait()
    own_refs = (near_ref, far_ref)
    prepare(
        range(HALF), own_refs, window, conv_ref, bias_ref, near_query, near_forget, near_value
    )
    prepare(
        range(HALF, ROWS), own_refs, window, conv_ref, bias_ref, query_ref, forget_ref, value_ref
    )

    def store(slot, head, block):
        mixed_ref[slot, :, block_of(head)] = block

    mix(
        0, owner_ref, near_ref, from_near_ref, near_query, near_forget, near_value, conv_ref,
        gain_ref, edges, states, query_scr, forget_scr, value_scr, store,
    )


def mix_near_call(owner, near, far, from_near, conv, bias, gain):
    shape = jax.ShapeDtypeStruct
    rows = (HALF, 2, DRAFT, DK)
    copied = [shape(x.shape, x.dtype) for x in (conv, bias, gain)]
    return call(
        mix_near,
        (shape((HALF, DRAFT, 2 * DK), BF), *[shape(rows, F32)] * 3, *copied),
        [SM, VM, VM, VM, HB, HB, HB],
        [pltpu.VMEM((ROWS, 3, 40, DK), F32)]
        + [pltpu.VMEM(rows, F32)] * 3
        + MIX_SCRATCH
        + [pltpu.SemaphoreType.DMA((3,))],
        15_000_000, 3_000_000, owner, near, far, from_near, conv, bias, gain,
    )


def mix_far(
    owner_ref, near_mixed_ref, far_ref, from_far_ref, query_ref, forget_ref, value_ref,
    conv_ref, gain_ref, weight_ref, mixed_ref, part_ref,
    edges, states, query_scr, forget_scr, value_scr,
):
    parity = lax.axis_index("req") % 2
    for slot in range(HALF):
        mixed_ref[row_of(0, slot)] = near_mixed_ref[slot]

    def store(slot, head, block):
        mixed_ref[parity * HALF + slot, :, block_of(head)] = block

    mix(
        1, owner_ref, far_ref, from_far_ref, query_ref, forget_ref, value_ref, conv_ref,
        gain_ref, edges, states, query_scr, forget_scr, value_scr, store,
    )
    rows = mixed_ref[...].reshape(ROWS * DRAFT, 2 * DK)
    block = weight_ref[:, columns_of(2, part_ref.shape[1])]
    part_ref[...] = jnp.dot(rows, block, preferred_element_type=F32).astype(BF)


def mix_far_call(owner, near_mixed, far, from_far, queries, forget, values, conv, gain, weight):
    shape = jax.ShapeDtypeStruct
    return call(
        mix_far,
        (
            shape((ROWS, DRAFT, 2 * DK), BF),
            shape((ROWS * DRAFT, weight.shape[1] // 4), BF),
        ),
        [SM] + [VM] * 9, MIX_SCRATCH,
        50_000_000, 2_000_000,
        owner, near_mixed, far, from_far, queries, forget, values, conv, gain, weight,
    )


def later(x, shift):
    return jnp.concatenate([x[shift:], jnp.ones((shift, DK), F32)], axis=0)


def split(x):
    coarse = x.astype(BF)
    return coarse, (x - coarse.astype(F32)).astype(BF)


def keep(
    owner_ref, accept_ref, near_ref, far_ref, from_near_ref, from_far_ref, state_ref, conv_ref,
    bias_ref, kept_ref, edges_out_ref, states, window, left, right, decays, sems,
):
    state_copies = [
        pltpu.make_async_copy(state_ref.at[row], states.at[row], sems.at[row])
        for row in range(ROWS)
    ]
    for copy in state_copies:
        copy.start()
    position = lax.broadcasted_iota(jnp.int32, (DRAFT, DK), 0)
    for slot in range(ROWS):
        side = slot // HALF
        row = row_of(side, slot % HALF)
        partner, local, place = source_of(owner_ref, row)
        length = accept_ref[partner]
        mine_ref, other_ref = (near_ref, from_near_ref) if side == 0 else (far_ref, from_far_ref)
        for block in range(3):
            mine = mine_ref[slot % HALF, drafts_of(block), :].astype(F32)
            other = other_ref[place, drafts_of(block), :].astype(F32)
            window[slot, block, 8:, :] = jnp.where(local, mine, other)
            window[slot, block, 2:8, :] = mine_ref[slot % HALF, edges_of(block), :].astype(F32)[:6]
        for head in range(2):
            gates = convolve(window, conv_ref, slot, head, 1) + bias_ref[head, :][None, :]
            values = as_value(convolve(window, conv_ref, slot, head, 2))
            forget = jax.nn.sigmoid(gates)
            inside = position < length
            weights = jnp.where(inside, 1.0 - forget, 0.0)
            factors = jnp.where(inside, forget, 1.0)
            after = later(factors, 1)
            for shift in (1, 2, 4, 8):
                after = after * later(after, shift)
            weight_high, weight_low = split(weights * after)
            value_high, value_low = split(values)
            left[slot, head] = jnp.concatenate([weight_high, weight_low, weight_high], axis=0)
            right[slot, head] = jnp.concatenate([value_high, value_high, value_low], axis=0)
            lane = 2 * slot + head
            decays[lane : lane + 1, :] = (factors * after)[:1, :]
        for block in range(3):
            turned = pltpu.roll(window[slot, block], 38 - 2 * length, 0)
            for step in range(CONV - 1):
                edges_out_ref[row, step, :, block_of(block)] = turned[
                    2 * step : 2 * step + 2
                ].astype(BF)
    columns = jnp.transpose(decays[...])
    for copy in state_copies:
        copy.wait()
    for slot in range(ROWS):
        row = row_of(slot // HALF, slot % HALF)
        for head in range(2):
            lane = 2 * slot + head
            update = lax.dot_general(
                left[slot, head], right[slot, head], (((0,), (0,)), ((), ())),
                preferred_element_type=F32,
            )
            kept_ref[row, head] = columns[:, lane : lane + 1] * states[row, head] + update


def keep_call(owner, accept, near, far, from_near, from_far, states, conv, bias):
    shape = jax.ShapeDtypeStruct
    return call(
        keep, (shape(states.shape, F32), shape((ROWS, CONV - 1, 2, 3 * DK), BF)),
        [SM, SM, VM, VM, VM, VM, HB, VM, VM],
        [
            pltpu.VMEM(states.shape, F32),
            pltpu.VMEM((ROWS, 3, 40, DK), F32),
            pltpu.VMEM((ROWS, 2, 3 * DRAFT, DK), BF),
            pltpu.VMEM((ROWS, 2, 3 * DRAFT, DK), BF),
            pltpu.VMEM((2 * ROWS, DK), F32),
            pltpu.SemaphoreType.DMA((ROWS,)),
        ],
        20_000_000, 3_000_000, owner, accept, near, far, from_near, from_far, states, conv, bias,
    )


def project(
    own_ref, one_ref, three_ref, weight_ref, from_one_ref, from_three_ref, part_ref,
    resid_ref, stream_ref,
):
    width = stream_ref.shape[1]
    columns = columns_of(0, width)
    total = jnp.dot(own_ref[...], weight_ref[:, columns], preferred_element_type=F32)
    total = total + jnp.dot(one_ref[...], from_one_ref[...], preferred_element_type=F32)
    total = total + jnp.dot(three_ref[...], from_three_ref[...], preferred_element_type=F32)
    total = total + part_ref[...].astype(F32)
    stream_ref[...] = (resid_ref[:, columns].astype(F32) + total).astype(BF)


def project_call(mixed, one, three, weight, parts, part, resid):
    slots, model = resid.shape
    return call(
        project, jax.ShapeDtypeStruct((slots, model // 4), BF), [VM] * 8, [],
        100_000_000, 3_000_000, mixed, one, three, weight, *parts, part, resid,
    )


NT = (((1,), (1,)), ((), ()))


def gated(rows, step, gain_ref, gate_ref, up_ref):
    block = rows.astype(F32)
    square = jnp.sum(block * block, axis=-1, keepdims=True)
    columns = columns_of(step, rows.shape[1])
    scaled = (block * gain_ref[:, columns]).astype(BF)
    gate = lax.dot_general(scaled, gate_ref[:, columns], NT, preferred_element_type=F32)
    up = lax.dot_general(scaled, up_ref[:, columns], NT, preferred_element_type=F32)
    return square, gate, up


def ffn_first(
    own_ref, two_ref, three_ref, gain_ref, gate_ref, up_ref, square_ref, gate_out_ref, up_out_ref,
):
    total = None
    for step, ref in ((0, own_ref), (2, two_ref), (3, three_ref)):
        parts = gated(ref[...], step, gain_ref, gate_ref, up_ref)
        total = parts if total is None else [x + y for x, y in zip(total, parts)]
    square_ref[...] = jnp.broadcast_to(total[0], square_ref.shape)
    gate_out_ref[...] = total[1]
    up_out_ref[...] = total[2]


def ffn_first_call(own, two, three, gain, gate_t, up_t):
    slots, hidden = own.shape[0], gate_t.shape[0]
    shape = jax.ShapeDtypeStruct
    return call(
        ffn_first,
        (shape((slots, DK), F32), shape((slots, hidden), F32), shape((slots, hidden), F32)),
        [VM] * 6, [], 550_000_000, 5_000_000, own, two, three, gain, gate_t, up_t,
    )


def ffn_last(
    length_ref, own_ref, one_ref, gain_ref, gate_ref, up_ref, down_ref,
    square_ref, gate_in_ref, up_in_ref, own_out_ref, one_out_ref, two_out_ref, three_out_ref,
):
    width = own_ref.shape[1]
    square, gate, up = gated(one_ref[...], 1, gain_ref, gate_ref, up_ref)
    total = square + square_ref[:, :1]
    scale = lax.rsqrt(total / (4 * width) + 1e-05)
    gate = (gate + gate_in_ref[...]) * scale
    up = (up + up_in_ref[...]) * scale
    hidden = (gate * jax.nn.sigmoid(gate) * up).astype(BF)
    me = lax.axis_index("req")
    position = lax.broadcasted_iota(jnp.int32, (DRAFT, 1), 0)
    live = jnp.concatenate(
        [(position < length_ref[me * ROWS + row]).astype(F32) for row in range(ROWS)], axis=0
    )
    for step, out_ref in ((2, two_out_ref), (1, one_out_ref), (3, three_out_ref)):
        part = jnp.dot(hidden, down_ref[:, columns_of(step, width)], preferred_element_type=F32)
        out_ref[...] = (part * live).astype(BF)
    part = jnp.dot(hidden, down_ref[:, columns_of(0, width)], preferred_element_type=F32)
    own_out_ref[...] = (part + own_ref[...].astype(F32)) * live


def ffn_last_call(lengths, own, one, gain, gate_t, up_t, down, *partial):
    slots, width = own.shape
    shape = jax.ShapeDtypeStruct
    part = shape((slots, width), BF)
    return call(
        ffn_last, (shape((slots, width), F32), part, part, part), [SM] + [VM] * 9, [],
        550_000_000, 5_000_000, lengths, own, one, gain, gate_t, up_t, down, *partial,
    )


def in_hbm(array):
    return pltpu.with_memory_space_constraint(array, pltpu.HBM)


def swapped(block, step):
    return lax.ppermute(block, "grp", [(i, i ^ step) for i in range(4)])


def shards(
    mix_inputs,
    conv_weight,
    forget_bias,
    norm_gain,
    out_weight,
    resid,
    ffn_gain,
    gate_weight,
    up_weight,
    down_weight,
    held_states,
    held_edges,
    draft_lengths,
    accepted,
    owner_row,
):
    slots = ROWS * DRAFT
    owner_row, accepted, draft_lengths = in_hbm(owner_row), in_hbm(accepted), in_hbm(draft_lengths)
    count = lax.axis_size("req")
    states = in_hbm(held_states)
    far, near, *cuts = pack_call(
        states, in_hbm(held_edges), in_hbm(mix_inputs), in_hbm(out_weight)
    )
    across = [(i, (i + (1 if i % 2 else -1)) % count) for i in range(count)]
    from_far = lax.ppermute(far, "req", across)
    from_near = lax.ppermute(near, "req", [(i, i ^ 1) for i in range(count)])
    parts = [swapped(cut, step) for step, cut in ((1, cuts[0]), (3, cuts[1]))]
    near_mixed, queries, forget, values, conv, bias, gain = mix_near_call(
        owner_row, near, far, from_near,
        in_hbm(conv_weight), in_hbm(forget_bias), in_hbm(norm_gain),
    )
    mixed, part = mix_far_call(
        owner_row, near_mixed, far, from_far, queries, forget, values, conv, gain, out_weight
    )
    mixed = mixed.reshape(slots, -1)
    part = swapped(part, 2)
    one = swapped(mixed, 1)
    three = swapped(mixed, 3)
    gate_t, up_t, down = gate_weight.T, up_weight.T, down_weight
    stream = project_call(mixed, one, three, out_weight, parts, part, resid.reshape(slots, -1))
    two = swapped(stream, 2)
    three = swapped(stream, 3)
    one = swapped(stream, 1)
    gain_row = ffn_gain[None, :]
    partial = ffn_first_call(stream, two, three, gain_row, gate_t, up_t)
    own_part, to_one, to_two, to_three = ffn_last_call(
        draft_lengths, stream, one, gain_row, gate_t, up_t, down, *partial
    )
    two = swapped(to_two, 2)
    one = swapped(to_one, 1)
    three = swapped(to_three, 3)
    own_part, from_near, from_far = lax.optimization_barrier((own_part, from_near, from_far))
    kept_states, kept_edges = keep_call(
        owner_row, accepted, near, far, from_near, from_far, states, conv, bias
    )
    layer_out = (own_part + two.astype(F32) + one.astype(F32) + three.astype(F32)).astype(BF)
    return (layer_out.reshape(ROWS, DRAFT, -1), kept_states, kept_edges)


def solution(mesh):
    return jax.shard_map(
        shards,
        mesh=mesh,
        in_specs=(
            P("req", None, "grp", None),
            P(None, "grp", None),
            P("grp", None),
            P("grp", None),
            P("grp", None),
            P("req", None, None),
            P(),
            P(None, "grp"),
            P(None, "grp"),
            P("grp", None),
            P("req", "grp", None, None),
            P("req", None, "grp", None),
            P(),
            P(),
            P(),
        ),
        out_specs=(P("req", None, "grp"), P("req", "grp", None, None), P("req", None, "grp", None)),
        check_vma=False,
    )
```

```python
import jax
import jax.numpy as jnp
from jax import lax
from jax.experimental import pallas as pl
from jax.experimental.pallas import tpu as pltpu
from jax.sharding import PartitionSpec as P

DK = 128
DRAFT = 16
CONV = 4
HALF = 4
ROWS = 2 * HALF
BF = jnp.bfloat16
PARAMS = pltpu.CompilerParams(vmem_limit_bytes=12 * 1024 * 1024)
F32 = jnp.float32
EDGES_AT = 2 * DK
DRAFTS_AT = EDGES_AT + 3 * DRAFT
PACKED = DRAFTS_AT + 3 * 2 * DRAFT
VM = pl.BlockSpec(memory_space=pltpu.VMEM)
SM = pl.BlockSpec(memory_space=pltpu.SMEM)
HB = pl.BlockSpec(memory_space=pltpu.HBM)


def row_of(half, place):
    parity = lax.axis_index("req") % 2
    base = (1 - parity if half == 0 else parity) * HALF
    return base + place


def source_of(owner_ref, row):
    me = lax.axis_index("req")
    partner = owner_ref[me * ROWS + row]
    return partner, partner // ROWS == me, partner % HALF


def block_of(block):
    return slice(block * DK, (block + 1) * DK)


def edges_of(block):
    return slice(EDGES_AT + block * DRAFT, EDGES_AT + (block + 1) * DRAFT)


def drafts_of(block):
    return slice(DRAFTS_AT + block * 2 * DRAFT, DRAFTS_AT + (block + 1) * 2 * DRAFT)


def call(kernel, out_shape, in_specs, scratch, flops, moved, *args):
    return pl.pallas_call(
        kernel,
        name=kernel.__name__,
        out_shape=out_shape,
        in_specs=in_specs,
        out_specs=jax.tree.map(lambda _: VM, out_shape),
        scratch_shapes=scratch,
        compiler_params=PARAMS,
        cost_estimate=pl.CostEstimate(flops=flops, bytes_accessed=moved, transcendentals=0),
    )(*args)


def columns_of(step, width):
    place = lax.bitwise_xor(lax.axis_index("grp"), step)
    return pl.ds(pl.multiple_of(place * width, width), width)


def fill_pack(half, out_ref, state_ref, edge_ref, draft_ref, states, edges, drafts, sems):
    rows = pl.ds(row_of(half, 0), HALF)
    state_copy = pltpu.make_async_copy(state_ref.at[rows], states, sems.at[0])
    edge_copy = pltpu.make_async_copy(edge_ref.at[rows], edges, sems.at[1])
    draft_copy = pltpu.make_async_copy(draft_ref.at[rows], drafts, sems.at[2])
    draft_copy.start()
    edge_copy.start()
    state_copy.start()
    edge_copy.wait()
    draft_copy.wait()
    for place in range(HALF):
        for block in range(3):
            columns = block_of(block)
            out_ref[place, edges_of(block), :] = jnp.zeros((DRAFT, DK), BF)
            start = EDGES_AT + block * DRAFT
            for step in range(CONV - 1):
                out_ref[place, start + 2 * step : start + 2 * step + 2, :] = edges[
                    place, step, :, columns
                ]
            start = DRAFTS_AT + block * 2 * DRAFT
            for step in range(DRAFT):
                out_ref[place, start + 2 * step : start + 2 * step + 2, :] = drafts[
                    place, step, :, columns
                ]
    state_copy.wait()
    for place in range(HALF):
        for head in range(2):
            out_ref[place, block_of(head), :] = states[place, head].astype(BF)


def pack_far(state_ref, edge_ref, draft_ref, far_ref, states, edges, drafts, sems):
    fill_pack(1, far_ref, state_ref, edge_ref, draft_ref, states, edges, drafts, sems)


def pack_near(
    state_ref, edge_ref, draft_ref, weight_ref, near_ref, one_ref, three_ref,
    states, edges, drafts, sems,
):
    width = one_ref.shape[1]
    cuts = [
        pltpu.make_async_copy(
            weight_ref.at[:, columns_of(step, width)], out_ref, sems.at[3 + i]
        )
        for i, (step, out_ref) in enumerate(((1, one_ref), (3, three_ref)))
    ]
    for copy in cuts:
        copy.start()
    fill_pack(0, near_ref, state_ref, edge_ref, draft_ref, states, edges, drafts, sems)
    for copy in cuts:
        copy.wait()


def pack_scratch(states, edges, drafts):
    return [
        pltpu.VMEM((HALF, *states.shape[1:]), F32),
        pltpu.VMEM((HALF, *edges.shape[1:]), BF),
        pltpu.VMEM((HALF, *drafts.shape[1:]), BF),
        pltpu.SemaphoreType.DMA((5,)),
    ]


def pack_far_call(*args):
    half = jax.ShapeDtypeStruct((HALF, PACKED + DRAFT, DK), BF)
    return call(pack_far, half, [HB] * 3, pack_scratch(*args), 500_000, 1_000_000, *args)


def pack_near_call(states, edges, drafts, weight):
    half = jax.ShapeDtypeStruct((HALF, PACKED, DK), BF)
    cut = jax.ShapeDtypeStruct((weight.shape[0], weight.shape[1] // 4), BF)
    return call(
        pack_near, (half, cut, cut), [HB] * 4, pack_scratch(states, edges, drafts),
        500_000, 2_000_000, states, edges, drafts, weight,
    )


def convolve(window, conv_ref, slot, head, block):
    total = None
    for shift in range(CONV):
        taps = conv_ref[shift, head, block_of(block)]
        rows = window[slot, block, pl.ds(2 + 2 * shift + head, DRAFT, stride=2), :]
        term = taps[None, :] * rows
        total = term if total is None else total + term
    return total


def as_query(x):
    return x * jax.nn.sigmoid(x) * DK ** (-0.5)


def as_value(x):
    return x * jax.nn.sigmoid(x)


def prepare(slots, own_refs, window, conv_ref, bias_ref, query_ref, forget_ref, value_ref):
    for slot in slots:
        own_ref = own_refs[slot // HALF]
        for block in range(3):
            window[slot, block, :8, :] = jnp.zeros((8, DK), F32)
            window[slot, block, 8:, :] = own_ref[slot % HALF, drafts_of(block), :].astype(F32)
    half = DRAFT // 2
    for slot in slots:
        for head in range(2):
            queries, gates, values = [
                convolve(window, conv_ref, slot, head, block) for block in range(3)
            ]
            place = slot % HALF
            query_ref[place, head, :half] = queries[:half]
            query_ref[place, head, half:] = as_query(queries[half:])
            gates = gates + bias_ref[head, :][None, :]
            forget_ref[place, head, :half] = gates[:half]
            forget_ref[place, head, half:] = jax.nn.sigmoid(gates[half:])
            value_ref[place, head, :half] = values[:half]
            value_ref[place, head, half:] = as_value(values[half:])


def mix(
    side, owner_ref, mine_ref, other_ref, query_ref, forget_ref, value_ref, conv_ref, gain_ref,
    edges, states, query_scr, forget_scr, value_scr, store,
):
    half = DRAFT // 2
    for slot in range(HALF):
        _, local, place = source_of(owner_ref, row_of(side, slot))
        for block in range(3):
            mine = mine_ref[slot, edges_of(block), :].astype(F32)
            other = other_ref[place, edges_of(block), :].astype(F32)
            edges[slot, block, :DRAFT, :] = jnp.where(local, mine, other)
            edges[slot, block, DRAFT:, :] = jnp.zeros((8, DK), F32)

        @pl.when(local)
        def _():
            states[slot] = mine_ref[slot, : 2 * DK, :]

        @pl.when(jnp.logical_not(local))
        def _():
            states[slot] = other_ref[place, : 2 * DK, :]

    sub_iota = lax.broadcasted_iota(jnp.int32, (1, DRAFT, DK), 1)

    def pair(step, _):
        base = step * 2
        for sub in range(2):
            slot = base + sub
            for head in range(2):
                lane = sub * 2 + head
                for block, (in_ref, out, act) in enumerate(
                    (
                        (query_ref, query_scr, as_query),
                        (forget_ref, forget_scr, jax.nn.sigmoid),
                        (value_ref, value_scr, as_value),
                    )
                ):
                    first = in_ref[slot, head, :half]
                    for shift in range(CONV - 1):
                        taps = conv_ref[shift, head, block_of(block)]
                        rows = edges[slot, block, pl.ds(2 * shift + head, half, stride=2), :]
                        first = first + taps[None, :] * rows
                    out[lane, :half] = act(first)
                    out[lane, half:] = in_ref[slot, head, half:]
        queries = query_scr[...]
        forget = forget_scr[...]
        values = value_scr[...]
        weights = jnp.zeros((4, DRAFT, DK), F32)
        decay = jnp.ones((4, 1, DK), F32)
        head_rows = []
        query_rows = []
        for t in range(DRAFT):
            forget_t = forget[:, t : t + 1, :]
            query_t = queries[:, t : t + 1, :]
            decay = decay * forget_t
            weights = jnp.where(sub_iota == t, 1.0 - forget_t, weights * forget_t)
            scores = jnp.sum(weights * query_t, axis=-1, keepdims=True)
            head_rows.append(jnp.sum(scores * values, axis=1, keepdims=True))
            query_rows.append(query_t * decay)
        local_out = jnp.concatenate(head_rows, axis=1)
        decayed = jnp.concatenate(query_rows, axis=1)
        for sub in range(2):
            slot = base + sub
            for head in range(2):
                lane = sub * 2 + head
                fine = decayed[lane]
                coarse = fine.astype(BF)
                stacked = jnp.concatenate([coarse, (fine - coarse.astype(F32)).astype(BF)], axis=0)
                both = jnp.dot(
                    stacked, states[slot, block_of(head), :], preferred_element_type=F32
                )
                out = local_out[lane] + (both[:DRAFT] + both[DRAFT:])
                scale = lax.rsqrt(jnp.mean(out * out, axis=-1, keepdims=True) + 1e-05)
                store(slot, head, (out * scale * gain_ref[head, :][None, :]).astype(BF))
        return 0

    lax.fori_loop(0, HALF // 2, pair, 0)


MIX_SCRATCH = [
    pltpu.VMEM((HALF, 3, 24, DK), F32),
    pltpu.VMEM((HALF, 2 * DK, DK), BF),
    pltpu.VMEM((4, DRAFT, DK), F32),
    pltpu.VMEM((4, DRAFT, DK), F32),
    pltpu.VMEM((4, DRAFT, DK), F32),
]


def mix_near(
    owner_ref, near_ref, far_ref, from_near_ref, conv_hbm, bias_hbm, gain_hbm,
    mixed_ref, query_ref, forget_ref, value_ref, conv_ref, bias_ref, gain_ref,
    window, near_query, near_forget, near_value, edges, states, query_scr, forget_scr, value_scr,
    sems,
):
    pairs = ((conv_hbm, conv_ref), (bias_hbm, bias_ref), (gain_hbm, gain_ref))
    copies = [
        pltpu.make_async_copy(src, dst, sems.at[i]) for i, (src, dst) in enumerate(pairs)
    ]
    for copy in copies:
        copy.start()
    for copy in copies:
        copy.wait()
    own_refs = (near_ref, far_ref)
    prepare(
        range(HALF), own_refs, window, conv_ref, bias_ref, near_query, near_forget, near_value
    )
    prepare(
        range(HALF, ROWS), own_refs, window, conv_ref, bias_ref, query_ref, forget_ref, value_ref
    )

    def store(slot, head, block):
        mixed_ref[slot, :, block_of(head)] = block

    mix(
        0, owner_ref, near_ref, from_near_ref, near_query, near_forget, near_value, conv_ref,
        gain_ref, edges, states, query_scr, forget_scr, value_scr, store,
    )


def mix_near_call(owner, near, far, from_near, conv, bias, gain):
    shape = jax.ShapeDtypeStruct
    rows = (HALF, 2, DRAFT, DK)
    copied = [shape(x.shape, x.dtype) for x in (conv, bias, gain)]
    return call(
        mix_near,
        (shape((HALF, DRAFT, 2 * DK), BF), *[shape(rows, F32)] * 3, *copied),
        [SM, VM, VM, VM, HB, HB, HB],
        [pltpu.VMEM((ROWS, 3, 40, DK), F32)]
        + [pltpu.VMEM(rows, F32)] * 3
        + MIX_SCRATCH
        + [pltpu.SemaphoreType.DMA((3,))],
        15_000_000, 3_000_000, owner, near, far, from_near, conv, bias, gain,
    )


def mix_far(
    owner_ref, near_mixed_ref, far_ref, from_far_ref, query_ref, forget_ref, value_ref,
    conv_ref, gain_ref, weight_ref, mixed_ref, part_ref,
    edges, states, query_scr, forget_scr, value_scr,
):
    parity = lax.axis_index("req") % 2
    for slot in range(HALF):
        mixed_ref[row_of(0, slot)] = near_mixed_ref[slot]

    def store(slot, head, block):
        mixed_ref[parity * HALF + slot, :, block_of(head)] = block

    mix(
        1, owner_ref, far_ref, from_far_ref, query_ref, forget_ref, value_ref, conv_ref,
        gain_ref, edges, states, query_scr, forget_scr, value_scr, store,
    )
    rows = mixed_ref[...].reshape(ROWS * DRAFT, 2 * DK)
    block = weight_ref[:, columns_of(2, part_ref.shape[1])]
    part_ref[...] = jnp.dot(rows, block, preferred_element_type=F32).astype(BF)


def mix_far_call(owner, near_mixed, far, from_far, queries, forget, values, conv, gain, weight):
    shape = jax.ShapeDtypeStruct
    return call(
        mix_far,
        (
            shape((ROWS, DRAFT, 2 * DK), BF),
            shape((ROWS * DRAFT, weight.shape[1] // 4), BF),
        ),
        [SM] + [VM] * 9, MIX_SCRATCH,
        50_000_000, 2_000_000,
        owner, near_mixed, far, from_far, queries, forget, values, conv, gain, weight,
    )


def later(x, shift):
    return jnp.concatenate([x[shift:], jnp.ones((shift, DK), F32)], axis=0)


def split(x):
    coarse = x.astype(BF)
    return coarse, (x - coarse.astype(F32)).astype(BF)


def keep(
    owner_ref, accept_ref, near_ref, far_ref, from_near_ref, from_far_ref, state_ref, conv_ref,
    bias_ref, kept_ref, edges_out_ref, states, window, left, right, decays, sems,
):
    state_copies = [
        pltpu.make_async_copy(state_ref.at[row], states.at[row], sems.at[row])
        for row in range(ROWS)
    ]
    for copy in state_copies:
        copy.start()
    position = lax.broadcasted_iota(jnp.int32, (DRAFT, DK), 0)
    for slot in range(ROWS):
        side = slot // HALF
        row = row_of(side, slot % HALF)
        partner, local, place = source_of(owner_ref, row)
        length = accept_ref[partner]
        mine_ref, other_ref = (near_ref, from_near_ref) if side == 0 else (far_ref, from_far_ref)
        for block in range(3):
            mine = mine_ref[slot % HALF, drafts_of(block), :].astype(F32)
            other = other_ref[place, drafts_of(block), :].astype(F32)
            window[slot, block, 8:, :] = jnp.where(local, mine, other)
            window[slot, block, 2:8, :] = mine_ref[slot % HALF, edges_of(block), :].astype(F32)[:6]
        for head in range(2):
            gates = convolve(window, conv_ref, slot, head, 1) + bias_ref[head, :][None, :]
            values = as_value(convolve(window, conv_ref, slot, head, 2))
            forget = jax.nn.sigmoid(gates)
            inside = position < length
            weights = jnp.where(inside, 1.0 - forget, 0.0)
            factors = jnp.where(inside, forget, 1.0)
            after = later(factors, 1)
            for shift in (1, 2, 4, 8):
                after = after * later(after, shift)
            weight_high, weight_low = split(weights * after)
            value_high, value_low = split(values)
            left[slot, head] = jnp.concatenate([weight_high, weight_low, weight_high], axis=0)
            right[slot, head] = jnp.concatenate([value_high, value_high, value_low], axis=0)
            lane = 2 * slot + head
            decays[lane : lane + 1, :] = (factors * after)[:1, :]
        for block in range(3):
            turned = pltpu.roll(window[slot, block], 38 - 2 * length, 0)
            for step in range(CONV - 1):
                edges_out_ref[row, step, :, block_of(block)] = turned[
                    2 * step : 2 * step + 2
                ].astype(BF)
    columns = jnp.transpose(decays[...])
    for copy in state_copies:
        copy.wait()
    for slot in range(ROWS):
        row = row_of(slot // HALF, slot % HALF)
        for head in range(2):
            lane = 2 * slot + head
            update = lax.dot_general(
                left[slot, head], right[slot, head], (((0,), (0,)), ((), ())),
                preferred_element_type=F32,
            )
            kept_ref[row, head] = columns[:, lane : lane + 1] * states[row, head] + update


def keep_call(owner, accept, near, far, from_near, from_far, states, conv, bias):
    shape = jax.ShapeDtypeStruct
    return call(
        keep, (shape(states.shape, F32), shape((ROWS, CONV - 1, 2, 3 * DK), BF)),
        [SM, SM, VM, VM, VM, VM, HB, VM, VM],
        [
            pltpu.VMEM(states.shape, F32),
            pltpu.VMEM((ROWS, 3, 40, DK), F32),
            pltpu.VMEM((ROWS, 2, 3 * DRAFT, DK), BF),
            pltpu.VMEM((ROWS, 2, 3 * DRAFT, DK), BF),
            pltpu.VMEM((2 * ROWS, DK), F32),
            pltpu.SemaphoreType.DMA((ROWS,)),
        ],
        20_000_000, 3_000_000, owner, accept, near, far, from_near, from_far, states, conv, bias,
    )


def project(
    own_ref, one_ref, three_ref, weight_ref, from_one_ref, from_three_ref, part_ref,
    resid_ref, stream_ref,
):
    width = stream_ref.shape[1]
    columns = columns_of(0, width)
    total = jnp.dot(own_ref[...], weight_ref[:, columns], preferred_element_type=F32)
    total = total + jnp.dot(one_ref[...], from_one_ref[...], preferred_element_type=F32)
    total = total + jnp.dot(three_ref[...], from_three_ref[...], preferred_element_type=F32)
    total = total + part_ref[...].astype(F32)
    stream_ref[...] = (resid_ref[:, columns].astype(F32) + total).astype(BF)


def project_call(mixed, one, three, weight, parts, part, resid):
    slots, model = resid.shape
    return call(
        project, jax.ShapeDtypeStruct((slots, model // 4), BF), [VM] * 8, [],
        100_000_000, 3_000_000, mixed, one, three, weight, *parts, part, resid,
    )


NT = (((1,), (1,)), ((), ()))


def gated(rows, step, gain_ref, gate_ref, up_ref):
    block = rows.astype(F32)
    square = jnp.sum(block * block, axis=-1, keepdims=True)
    columns = columns_of(step, rows.shape[1])
    scaled = (block * gain_ref[:, columns]).astype(BF)
    gate = lax.dot_general(scaled, gate_ref[:, columns], NT, preferred_element_type=F32)
    up = lax.dot_general(scaled, up_ref[:, columns], NT, preferred_element_type=F32)
    return square, gate, up


def ffn_first(
    own_ref, two_ref, three_ref, gain_ref, gate_ref, up_ref, square_ref, gate_out_ref, up_out_ref,
):
    total = None
    for step, ref in ((0, own_ref), (2, two_ref), (3, three_ref)):
        parts = gated(ref[...], step, gain_ref, gate_ref, up_ref)
        total = parts if total is None else [x + y for x, y in zip(total, parts)]
    square_ref[...] = jnp.broadcast_to(total[0], square_ref.shape)
    gate_out_ref[...] = total[1]
    up_out_ref[...] = total[2]


def ffn_first_call(own, two, three, gain, gate_t, up_t):
    slots, hidden = own.shape[0], gate_t.shape[0]
    shape = jax.ShapeDtypeStruct
    return call(
        ffn_first,
        (shape((slots, DK), F32), shape((slots, hidden), F32), shape((slots, hidden), F32)),
        [VM] * 6, [], 550_000_000, 5_000_000, own, two, three, gain, gate_t, up_t,
    )


def ffn_last(
    length_ref, own_ref, one_ref, gain_ref, gate_ref, up_ref, down_ref,
    square_ref, gate_in_ref, up_in_ref, own_out_ref, one_out_ref, two_out_ref, three_out_ref,
):
    width = own_ref.shape[1]
    square, gate, up = gated(one_ref[...], 1, gain_ref, gate_ref, up_ref)
    total = square + square_ref[:, :1]
    scale = lax.rsqrt(total / (4 * width) + 1e-05)
    gate = (gate + gate_in_ref[...]) * scale
    up = (up + up_in_ref[...]) * scale
    hidden = (gate * jax.nn.sigmoid(gate) * up).astype(BF)
    me = lax.axis_index("req")
    position = lax.broadcasted_iota(jnp.int32, (DRAFT, 1), 0)
    live = jnp.concatenate(
        [(position < length_ref[me * ROWS + row]).astype(F32) for row in range(ROWS)], axis=0
    )
    for step, out_ref in ((2, two_out_ref), (1, one_out_ref), (3, three_out_ref)):
        part = jnp.dot(hidden, down_ref[:, columns_of(step, width)], preferred_element_type=F32)
        out_ref[...] = (part * live).astype(BF)
    part = jnp.dot(hidden, down_ref[:, columns_of(0, width)], preferred_element_type=F32)
    own_out_ref[...] = (part + own_ref[...].astype(F32)) * live


def ffn_last_call(lengths, own, one, gain, gate_t, up_t, down, *partial):
    slots, width = own.shape
    shape = jax.ShapeDtypeStruct
    part = shape((slots, width), BF)
    return call(
        ffn_last, (shape((slots, width), F32), part, part, part), [SM] + [VM] * 9, [],
        550_000_000, 5_000_000, lengths, own, one, gain, gate_t, up_t, down, *partial,
    )


def in_hbm(array):
    return pltpu.with_memory_space_constraint(array, pltpu.HBM)


def swapped(block, step):
    return lax.ppermute(block, "grp", [(i, i ^ step) for i in range(4)])


def shards(
    mix_inputs,
    conv_weight,
    forget_bias,
    norm_gain,
    out_weight,
    resid,
    ffn_gain,
    gate_weight,
    up_weight,
    down_weight,
    held_states,
    held_edges,
    draft_lengths,
    accepted,
    owner_row,
):
    slots = ROWS * DRAFT
    owner_row, accepted, draft_lengths = in_hbm(owner_row), in_hbm(accepted), in_hbm(draft_lengths)
    count = lax.axis_size("req")
    states = in_hbm(held_states)
    across = [(i, (i + (1 if i % 2 else -1)) % count) for i in range(count)]
    held, drafts = in_hbm(held_edges), in_hbm(mix_inputs)
    far = pack_far_call(states, held, drafts)
    from_far = lax.ppermute(far, "req", across)
    near, *cuts = pack_near_call(states, held, drafts, in_hbm(out_weight))
    from_near = lax.ppermute(near, "req", [(i, i ^ 1) for i in range(count)])
    parts = [swapped(cut, step) for step, cut in ((1, cuts[0]), (3, cuts[1]))]
    near_mixed, queries, forget, values, conv, bias, gain = mix_near_call(
        owner_row, near, far, from_near,
        in_hbm(conv_weight), in_hbm(forget_bias), in_hbm(norm_gain),
    )
    mixed, part = mix_far_call(
        owner_row, near_mixed, far, from_far, queries, forget, values, conv, gain, out_weight
    )
    mixed = mixed.reshape(slots, -1)
    part = swapped(part, 2)
    one = swapped(mixed, 1)
    three = swapped(mixed, 3)
    gate_t, up_t, down = gate_weight.T, up_weight.T, down_weight
    stream = project_call(mixed, one, three, out_weight, parts, part, resid.reshape(slots, -1))
    two = swapped(stream, 2)
    three = swapped(stream, 3)
    one = swapped(stream, 1)
    gain_row = ffn_gain[None, :]
    partial = ffn_first_call(stream, two, three, gain_row, gate_t, up_t)
    own_part, to_one, to_two, to_three = ffn_last_call(
        draft_lengths, stream, one, gain_row, gate_t, up_t, down, *partial
    )
    two = swapped(to_two, 2)
    one = swapped(to_one, 1)
    three = swapped(to_three, 3)
    own_part, from_near, from_far = lax.optimization_barrier((own_part, from_near, from_far))
    kept_states, kept_edges = keep_call(
        owner_row, accepted, near, far, from_near, from_far, states, conv, bias
    )
    layer_out = (own_part + two.astype(F32) + one.astype(F32) + three.astype(F32)).astype(BF)
    return (layer_out.reshape(ROWS, DRAFT, -1), kept_states, kept_edges)


def solution(mesh):
    return jax.shard_map(
        shards,
        mesh=mesh,
        in_specs=(
            P("req", None, "grp", None),
            P(None, "grp", None),
            P("grp", None),
            P("grp", None),
            P("grp", None),
            P("req", None, None),
            P(),
            P(None, "grp"),
            P(None, "grp"),
            P("grp", None),
            P("req", "grp", None, None),
            P("req", None, "grp", None),
            P(),
            P(),
            P(),
        ),
        out_specs=(P("req", None, "grp"), P("req", "grp", None, None), P("req", None, "grp", None)),
        check_vma=False,
    )
```

```python
import jax
import jax.numpy as jnp
from jax import lax
from jax.experimental import pallas as pl
from jax.experimental.pallas import tpu as pltpu
from jax.sharding import PartitionSpec as P

DK = 128
DRAFT = 16
CONV = 4
HALF = 4
ROWS = 2 * HALF
BF = jnp.bfloat16
PARAMS = pltpu.CompilerParams(vmem_limit_bytes=12 * 1024 * 1024)
F32 = jnp.float32
EDGES_AT = 2 * DK
DRAFTS_AT = EDGES_AT + 3 * DRAFT
PACKED = DRAFTS_AT + 3 * 2 * DRAFT
VM = pl.BlockSpec(memory_space=pltpu.VMEM)
SM = pl.BlockSpec(memory_space=pltpu.SMEM)
HB = pl.BlockSpec(memory_space=pltpu.HBM)


def row_of(half, place):
    parity = lax.axis_index("req") % 2
    base = (1 - parity if half == 0 else parity) * HALF
    return base + place


def source_of(owner_ref, row):
    me = lax.axis_index("req")
    partner = owner_ref[me * ROWS + row]
    return partner, partner // ROWS == me, partner % HALF


def block_of(block):
    return slice(block * DK, (block + 1) * DK)


def edges_of(block):
    return slice(EDGES_AT + block * DRAFT, EDGES_AT + (block + 1) * DRAFT)


def drafts_of(block):
    return slice(DRAFTS_AT + block * 2 * DRAFT, DRAFTS_AT + (block + 1) * 2 * DRAFT)


def call(kernel, out_shape, in_specs, scratch, flops, moved, *args):
    return pl.pallas_call(
        kernel,
        name=kernel.__name__,
        out_shape=out_shape,
        in_specs=in_specs,
        out_specs=jax.tree.map(lambda _: VM, out_shape),
        scratch_shapes=scratch,
        compiler_params=PARAMS,
        cost_estimate=pl.CostEstimate(flops=flops, bytes_accessed=moved, transcendentals=0),
    )(*args)


def columns_of(step, width):
    place = lax.bitwise_xor(lax.axis_index("grp"), step)
    return pl.ds(pl.multiple_of(place * width, width), width)


def fill_pack(half, out_ref, state_ref, edge_ref, draft_ref, states, edges, drafts, sems):
    rows = pl.ds(row_of(half, 0), HALF)
    state_copy = pltpu.make_async_copy(state_ref.at[rows], states, sems.at[0])
    edge_copy = pltpu.make_async_copy(edge_ref.at[rows], edges, sems.at[1])
    draft_copy = pltpu.make_async_copy(draft_ref.at[rows], drafts, sems.at[2])
    draft_copy.start()
    edge_copy.start()
    state_copy.start()
    edge_copy.wait()
    draft_copy.wait()
    for place in range(HALF):
        for block in range(3):
            columns = block_of(block)
            out_ref[place, edges_of(block), :] = jnp.zeros((DRAFT, DK), BF)
            start = EDGES_AT + block * DRAFT
            for step in range(CONV - 1):
                out_ref[place, start + 2 * step : start + 2 * step + 2, :] = edges[
                    place, step, :, columns
                ]
            start = DRAFTS_AT + block * 2 * DRAFT
            for step in range(DRAFT):
                out_ref[place, start + 2 * step : start + 2 * step + 2, :] = drafts[
                    place, step, :, columns
                ]
    state_copy.wait()
    for place in range(HALF):
        for head in range(2):
            out_ref[place, block_of(head), :] = states[place, head].astype(BF)


def pack_far(state_ref, edge_ref, draft_ref, far_ref, states, edges, drafts, sems):
    fill_pack(1, far_ref, state_ref, edge_ref, draft_ref, states, edges, drafts, sems)


def pack_near(
    state_ref, edge_ref, draft_ref, weight_ref, near_ref, one_ref, three_ref,
    states, edges, drafts, sems,
):
    width = one_ref.shape[1]
    cuts = [
        pltpu.make_async_copy(
            weight_ref.at[:, columns_of(step, width)], out_ref, sems.at[3 + i]
        )
        for i, (step, out_ref) in enumerate(((1, one_ref), (3, three_ref)))
    ]
    for copy in cuts:
        copy.start()
    fill_pack(0, near_ref, state_ref, edge_ref, draft_ref, states, edges, drafts, sems)
    for copy in cuts:
        copy.wait()


def pack_scratch(states, edges, drafts):
    return [
        pltpu.VMEM((HALF, *states.shape[1:]), F32),
        pltpu.VMEM((HALF, *edges.shape[1:]), BF),
        pltpu.VMEM((HALF, *drafts.shape[1:]), BF),
        pltpu.SemaphoreType.DMA((5,)),
    ]


def pack_far_call(*args):
    half = jax.ShapeDtypeStruct((HALF, PACKED + DRAFT, DK), BF)
    return call(pack_far, half, [HB] * 3, pack_scratch(*args), 500_000, 1_000_000, *args)


def pack_near_call(states, edges, drafts, weight):
    half = jax.ShapeDtypeStruct((HALF, PACKED, DK), BF)
    cut = jax.ShapeDtypeStruct((weight.shape[0], weight.shape[1] // 4), BF)
    return call(
        pack_near, (half, cut, cut), [HB] * 4, pack_scratch(states, edges, drafts),
        500_000, 2_000_000, states, edges, drafts, weight,
    )


def convolve(window, conv_ref, slot, head, block):
    total = None
    for shift in range(CONV):
        taps = conv_ref[shift, head, block_of(block)]
        rows = window[slot, block, pl.ds(2 + 2 * shift + head, DRAFT, stride=2), :]
        term = taps[None, :] * rows
        total = term if total is None else total + term
    return total


def as_query(x):
    return x * jax.nn.sigmoid(x) * DK ** (-0.5)


def as_value(x):
    return x * jax.nn.sigmoid(x)


def prepare(slots, own_refs, window, conv_ref, bias_ref, query_ref, forget_ref, value_ref):
    for slot in slots:
        own_ref = own_refs[slot // HALF]
        for block in range(3):
            window[slot, block, :8, :] = jnp.zeros((8, DK), F32)
            window[slot, block, 8:, :] = own_ref[slot % HALF, drafts_of(block), :].astype(F32)
    half = DRAFT // 2
    for slot in slots:
        for head in range(2):
            queries, gates, values = [
                convolve(window, conv_ref, slot, head, block) for block in range(3)
            ]
            place = slot % HALF
            query_ref[place, head, :half] = queries[:half]
            query_ref[place, head, half:] = as_query(queries[half:])
            gates = gates + bias_ref[head, :][None, :]
            forget_ref[place, head, :half] = gates[:half]
            forget_ref[place, head, half:] = jax.nn.sigmoid(gates[half:])
            value_ref[place, head, :half] = values[:half]
            value_ref[place, head, half:] = as_value(values[half:])


def mix(
    side, owner_ref, mine_ref, other_ref, query_ref, forget_ref, value_ref, conv_ref, gain_ref,
    edges, states, query_scr, forget_scr, value_scr, store,
):
    half = DRAFT // 2
    for slot in range(HALF):
        _, local, place = source_of(owner_ref, row_of(side, slot))
        for block in range(3):
            mine = mine_ref[slot, edges_of(block), :].astype(F32)
            other = other_ref[place, edges_of(block), :].astype(F32)
            edges[slot, block, :DRAFT, :] = jnp.where(local, mine, other)
            edges[slot, block, DRAFT:, :] = jnp.zeros((8, DK), F32)

        @pl.when(local)
        def _():
            states[slot] = mine_ref[slot, : 2 * DK, :]

        @pl.when(jnp.logical_not(local))
        def _():
            states[slot] = other_ref[place, : 2 * DK, :]

    sub_iota = lax.broadcasted_iota(jnp.int32, (1, DRAFT, DK), 1)

    def pair(step, _):
        base = step * 2
        for sub in range(2):
            slot = base + sub
            for head in range(2):
                lane = sub * 2 + head
                for block, (in_ref, out, act) in enumerate(
                    (
                        (query_ref, query_scr, as_query),
                        (forget_ref, forget_scr, jax.nn.sigmoid),
                        (value_ref, value_scr, as_value),
                    )
                ):
                    first = in_ref[slot, head, :half]
                    for shift in range(CONV - 1):
                        taps = conv_ref[shift, head, block_of(block)]
                        rows = edges[slot, block, pl.ds(2 * shift + head, half, stride=2), :]
                        first = first + taps[None, :] * rows
                    out[4 * step + lane, :half] = act(first)
                    out[4 * step + lane, half:] = in_ref[slot, head, half:]
        lanes = slice(4 * step, 4 * step + 4)
        queries = query_scr[lanes]
        forget = forget_scr[lanes]
        values = value_scr[lanes]
        weights = jnp.zeros((4, DRAFT, DK), F32)
        decay = jnp.ones((4, 1, DK), F32)
        head_rows = []
        query_rows = []
        for t in range(DRAFT):
            forget_t = forget[:, t : t + 1, :]
            query_t = queries[:, t : t + 1, :]
            decay = decay * forget_t
            weights = jnp.where(sub_iota == t, 1.0 - forget_t, weights * forget_t)
            scores = jnp.sum(weights * query_t, axis=-1, keepdims=True)
            head_rows.append(jnp.sum(scores * values, axis=1, keepdims=True))
            query_rows.append(query_t * decay)
        local_out = jnp.concatenate(head_rows, axis=1)
        decayed = jnp.concatenate(query_rows, axis=1)
        for sub in range(2):
            slot = base + sub
            for head in range(2):
                lane = sub * 2 + head
                fine = decayed[lane]
                coarse = fine.astype(BF)
                stacked = jnp.concatenate([coarse, (fine - coarse.astype(F32)).astype(BF)], axis=0)
                both = jnp.dot(
                    stacked, states[slot, block_of(head), :], preferred_element_type=F32
                )
                out = local_out[lane] + (both[:DRAFT] + both[DRAFT:])
                scale = lax.rsqrt(jnp.mean(out * out, axis=-1, keepdims=True) + 1e-05)
                store(slot, head, (out * scale * gain_ref[head, :][None, :]).astype(BF))
        return 0

    for step in range(HALF // 2):
        pair(step, 0)


MIX_SCRATCH = [
    pltpu.VMEM((HALF, 3, 24, DK), F32),
    pltpu.VMEM((HALF, 2 * DK, DK), BF),
    pltpu.VMEM((8, DRAFT, DK), F32),
    pltpu.VMEM((8, DRAFT, DK), F32),
    pltpu.VMEM((8, DRAFT, DK), F32),
]


def mix_near(
    owner_ref, near_ref, far_ref, from_near_ref, conv_hbm, bias_hbm, gain_hbm,
    mixed_ref, query_ref, forget_ref, value_ref, conv_ref, bias_ref, gain_ref,
    window, near_query, near_forget, near_value, edges, states, query_scr, forget_scr, value_scr,
    sems,
):
    pairs = ((conv_hbm, conv_ref), (bias_hbm, bias_ref), (gain_hbm, gain_ref))
    copies = [
        pltpu.make_async_copy(src, dst, sems.at[i]) for i, (src, dst) in enumerate(pairs)
    ]
    for copy in copies:
        copy.start()
    for copy in copies:
        copy.wait()
    own_refs = (near_ref, far_ref)
    prepare(
        range(HALF), own_refs, window, conv_ref, bias_ref, near_query, near_forget, near_value
    )
    prepare(
        range(HALF, ROWS), own_refs, window, conv_ref, bias_ref, query_ref, forget_ref, value_ref
    )

    def store(slot, head, block):
        mixed_ref[slot, :, block_of(head)] = block

    mix(
        0, owner_ref, near_ref, from_near_ref, near_query, near_forget, near_value, conv_ref,
        gain_ref, edges, states, query_scr, forget_scr, value_scr, store,
    )


def mix_near_call(owner, near, far, from_near, conv, bias, gain):
    shape = jax.ShapeDtypeStruct
    rows = (HALF, 2, DRAFT, DK)
    copied = [shape(x.shape, x.dtype) for x in (conv, bias, gain)]
    return call(
        mix_near,
        (shape((HALF, DRAFT, 2 * DK), BF), *[shape(rows, F32)] * 3, *copied),
        [SM, VM, VM, VM, HB, HB, HB],
        [pltpu.VMEM((ROWS, 3, 40, DK), F32)]
        + [pltpu.VMEM(rows, F32)] * 3
        + MIX_SCRATCH
        + [pltpu.SemaphoreType.DMA((3,))],
        15_000_000, 3_000_000, owner, near, far, from_near, conv, bias, gain,
    )


def mix_far(
    owner_ref, near_mixed_ref, far_ref, from_far_ref, query_ref, forget_ref, value_ref,
    conv_ref, gain_ref, weight_ref, mixed_ref, part_ref,
    edges, states, query_scr, forget_scr, value_scr,
):
    parity = lax.axis_index("req") % 2
    for slot in range(HALF):
        mixed_ref[row_of(0, slot)] = near_mixed_ref[slot]

    def store(slot, head, block):
        mixed_ref[parity * HALF + slot, :, block_of(head)] = block

    mix(
        1, owner_ref, far_ref, from_far_ref, query_ref, forget_ref, value_ref, conv_ref,
        gain_ref, edges, states, query_scr, forget_scr, value_scr, store,
    )
    rows = mixed_ref[...].reshape(ROWS * DRAFT, 2 * DK)
    block = weight_ref[:, columns_of(2, part_ref.shape[1])]
    part_ref[...] = jnp.dot(rows, block, preferred_element_type=F32).astype(BF)


def mix_far_call(owner, near_mixed, far, from_far, queries, forget, values, conv, gain, weight):
    shape = jax.ShapeDtypeStruct
    return call(
        mix_far,
        (
            shape((ROWS, DRAFT, 2 * DK), BF),
            shape((ROWS * DRAFT, weight.shape[1] // 4), BF),
        ),
        [SM] + [VM] * 9, MIX_SCRATCH,
        50_000_000, 2_000_000,
        owner, near_mixed, far, from_far, queries, forget, values, conv, gain, weight,
    )


def later(x, shift):
    return jnp.concatenate([x[shift:], jnp.ones((shift, DK), F32)], axis=0)


def split(x):
    coarse = x.astype(BF)
    return coarse, (x - coarse.astype(F32)).astype(BF)


def keep(
    owner_ref, accept_ref, near_ref, far_ref, from_near_ref, from_far_ref, state_ref, conv_ref,
    bias_ref, kept_ref, edges_out_ref, states, window, left, right, decays, sems,
):
    state_copies = [
        pltpu.make_async_copy(state_ref.at[row], states.at[row], sems.at[row])
        for row in range(ROWS)
    ]
    for copy in state_copies:
        copy.start()
    position = lax.broadcasted_iota(jnp.int32, (DRAFT, DK), 0)
    for slot in range(ROWS):
        side = slot // HALF
        row = row_of(side, slot % HALF)
        partner, local, place = source_of(owner_ref, row)
        length = accept_ref[partner]
        mine_ref, other_ref = (near_ref, from_near_ref) if side == 0 else (far_ref, from_far_ref)
        for block in range(3):
            mine = mine_ref[slot % HALF, drafts_of(block), :].astype(F32)
            other = other_ref[place, drafts_of(block), :].astype(F32)
            window[slot, block, 8:, :] = jnp.where(local, mine, other)
            window[slot, block, 2:8, :] = mine_ref[slot % HALF, edges_of(block), :].astype(F32)[:6]
        for head in range(2):
            gates = convolve(window, conv_ref, slot, head, 1) + bias_ref[head, :][None, :]
            values = as_value(convolve(window, conv_ref, slot, head, 2))
            forget = jax.nn.sigmoid(gates)
            inside = position < length
            weights = jnp.where(inside, 1.0 - forget, 0.0)
            factors = jnp.where(inside, forget, 1.0)
            after = later(factors, 1)
            for shift in (1, 2, 4, 8):
                after = after * later(after, shift)
            weight_high, weight_low = split(weights * after)
            value_high, value_low = split(values)
            left[slot, head] = jnp.concatenate([weight_high, weight_low, weight_high], axis=0)
            right[slot, head] = jnp.concatenate([value_high, value_high, value_low], axis=0)
            lane = 2 * slot + head
            decays[lane : lane + 1, :] = (factors * after)[:1, :]
        for block in range(3):
            turned = pltpu.roll(window[slot, block], 38 - 2 * length, 0)
            for step in range(CONV - 1):
                edges_out_ref[row, step, :, block_of(block)] = turned[
                    2 * step : 2 * step + 2
                ].astype(BF)
    columns = jnp.transpose(decays[...])
    for copy in state_copies:
        copy.wait()
    for slot in range(ROWS):
        row = row_of(slot // HALF, slot % HALF)
        for head in range(2):
            lane = 2 * slot + head
            update = lax.dot_general(
                left[slot, head], right[slot, head], (((0,), (0,)), ((), ())),
                preferred_element_type=F32,
            )
            kept_ref[row, head] = columns[:, lane : lane + 1] * states[row, head] + update


def keep_call(owner, accept, near, far, from_near, from_far, states, conv, bias):
    shape = jax.ShapeDtypeStruct
    return call(
        keep, (shape(states.shape, F32), shape((ROWS, CONV - 1, 2, 3 * DK), BF)),
        [SM, SM, VM, VM, VM, VM, HB, VM, VM],
        [
            pltpu.VMEM(states.shape, F32),
            pltpu.VMEM((ROWS, 3, 40, DK), F32),
            pltpu.VMEM((ROWS, 2, 3 * DRAFT, DK), BF),
            pltpu.VMEM((ROWS, 2, 3 * DRAFT, DK), BF),
            pltpu.VMEM((2 * ROWS, DK), F32),
            pltpu.SemaphoreType.DMA((ROWS,)),
        ],
        20_000_000, 3_000_000, owner, accept, near, far, from_near, from_far, states, conv, bias,
    )


def project(
    own_ref, one_ref, three_ref, weight_ref, from_one_ref, from_three_ref, part_ref,
    resid_ref, stream_ref,
):
    width = stream_ref.shape[1]
    columns = columns_of(0, width)
    total = jnp.dot(own_ref[...], weight_ref[:, columns], preferred_element_type=F32)
    total = total + jnp.dot(one_ref[...], from_one_ref[...], preferred_element_type=F32)
    total = total + jnp.dot(three_ref[...], from_three_ref[...], preferred_element_type=F32)
    total = total + part_ref[...].astype(F32)
    stream_ref[...] = (resid_ref[:, columns].astype(F32) + total).astype(BF)


def project_call(mixed, one, three, weight, parts, part, resid):
    slots, model = resid.shape
    return call(
        project, jax.ShapeDtypeStruct((slots, model // 4), BF), [VM] * 8, [],
        100_000_000, 3_000_000, mixed, one, three, weight, *parts, part, resid,
    )


NT = (((1,), (1,)), ((), ()))


def gated(rows, step, gain_ref, gate_ref, up_ref):
    block = rows.astype(F32)
    square = jnp.sum(block * block, axis=-1, keepdims=True)
    columns = columns_of(step, rows.shape[1])
    scaled = (block * gain_ref[:, columns]).astype(BF)
    gate = lax.dot_general(scaled, gate_ref[:, columns], NT, preferred_element_type=F32)
    up = lax.dot_general(scaled, up_ref[:, columns], NT, preferred_element_type=F32)
    return square, gate, up


def ffn_first(
    own_ref, two_ref, three_ref, gain_ref, gate_ref, up_ref, square_ref, gate_out_ref, up_out_ref,
):
    total = None
    for step, ref in ((0, own_ref), (2, two_ref), (3, three_ref)):
        parts = gated(ref[...], step, gain_ref, gate_ref, up_ref)
        total = parts if total is None else [x + y for x, y in zip(total, parts)]
    square_ref[...] = jnp.broadcast_to(total[0], square_ref.shape)
    gate_out_ref[...] = total[1]
    up_out_ref[...] = total[2]


def ffn_first_call(own, two, three, gain, gate_t, up_t):
    slots, hidden = own.shape[0], gate_t.shape[0]
    shape = jax.ShapeDtypeStruct
    return call(
        ffn_first,
        (shape((slots, DK), F32), shape((slots, hidden), F32), shape((slots, hidden), F32)),
        [VM] * 6, [], 550_000_000, 5_000_000, own, two, three, gain, gate_t, up_t,
    )


def ffn_last(
    length_ref, own_ref, one_ref, gain_ref, gate_ref, up_ref, down_ref,
    square_ref, gate_in_ref, up_in_ref, own_out_ref, one_out_ref, two_out_ref, three_out_ref,
):
    width = own_ref.shape[1]
    square, gate, up = gated(one_ref[...], 1, gain_ref, gate_ref, up_ref)
    total = square + square_ref[:, :1]
    scale = lax.rsqrt(total / (4 * width) + 1e-05)
    gate = (gate + gate_in_ref[...]) * scale
    up = (up + up_in_ref[...]) * scale
    hidden = (gate * jax.nn.sigmoid(gate) * up).astype(BF)
    me = lax.axis_index("req")
    position = lax.broadcasted_iota(jnp.int32, (DRAFT, 1), 0)
    live = jnp.concatenate(
        [(position < length_ref[me * ROWS + row]).astype(F32) for row in range(ROWS)], axis=0
    )
    for step, out_ref in ((2, two_out_ref), (1, one_out_ref), (3, three_out_ref)):
        part = jnp.dot(hidden, down_ref[:, columns_of(step, width)], preferred_element_type=F32)
        out_ref[...] = (part * live).astype(BF)
    part = jnp.dot(hidden, down_ref[:, columns_of(0, width)], preferred_element_type=F32)
    own_out_ref[...] = (part + own_ref[...].astype(F32)) * live


def ffn_last_call(lengths, own, one, gain, gate_t, up_t, down, *partial):
    slots, width = own.shape
    shape = jax.ShapeDtypeStruct
    part = shape((slots, width), BF)
    return call(
        ffn_last, (shape((slots, width), F32), part, part, part), [SM] + [VM] * 9, [],
        550_000_000, 5_000_000, lengths, own, one, gain, gate_t, up_t, down, *partial,
    )


def in_hbm(array):
    return pltpu.with_memory_space_constraint(array, pltpu.HBM)


def swapped(block, step):
    return lax.ppermute(block, "grp", [(i, i ^ step) for i in range(4)])


def shards(
    mix_inputs,
    conv_weight,
    forget_bias,
    norm_gain,
    out_weight,
    resid,
    ffn_gain,
    gate_weight,
    up_weight,
    down_weight,
    held_states,
    held_edges,
    draft_lengths,
    accepted,
    owner_row,
):
    slots = ROWS * DRAFT
    owner_row, accepted, draft_lengths = in_hbm(owner_row), in_hbm(accepted), in_hbm(draft_lengths)
    count = lax.axis_size("req")
    states = in_hbm(held_states)
    across = [(i, (i + (1 if i % 2 else -1)) % count) for i in range(count)]
    held, drafts = in_hbm(held_edges), in_hbm(mix_inputs)
    far = pack_far_call(states, held, drafts)
    from_far = lax.ppermute(far, "req", across)
    near, *cuts = pack_near_call(states, held, drafts, in_hbm(out_weight))
    from_near = lax.ppermute(near, "req", [(i, i ^ 1) for i in range(count)])
    parts = [swapped(cut, step) for step, cut in ((1, cuts[0]), (3, cuts[1]))]
    near_mixed, queries, forget, values, conv, bias, gain = mix_near_call(
        owner_row, near, far, from_near,
        in_hbm(conv_weight), in_hbm(forget_bias), in_hbm(norm_gain),
    )
    mixed, part = mix_far_call(
        owner_row, near_mixed, far, from_far, queries, forget, values, conv, gain, out_weight
    )
    mixed = mixed.reshape(slots, -1)
    part = swapped(part, 2)
    one = swapped(mixed, 1)
    three = swapped(mixed, 3)
    gate_t, up_t, down = gate_weight.T, up_weight.T, down_weight
    stream = project_call(mixed, one, three, out_weight, parts, part, resid.reshape(slots, -1))
    two = swapped(stream, 2)
    three = swapped(stream, 3)
    one = swapped(stream, 1)
    gain_row = ffn_gain[None, :]
    partial = ffn_first_call(stream, two, three, gain_row, gate_t, up_t)
    own_part, to_one, to_two, to_three = ffn_last_call(
        draft_lengths, stream, one, gain_row, gate_t, up_t, down, *partial
    )
    two = swapped(to_two, 2)
    one = swapped(to_one, 1)
    three = swapped(to_three, 3)
    own_part, from_near, from_far = lax.optimization_barrier((own_part, from_near, from_far))
    kept_states, kept_edges = keep_call(
        owner_row, accepted, near, far, from_near, from_far, states, conv, bias
    )
    layer_out = (own_part + two.astype(F32) + one.astype(F32) + three.astype(F32)).astype(BF)
    return (layer_out.reshape(ROWS, DRAFT, -1), kept_states, kept_edges)


def solution(mesh):
    return jax.shard_map(
        shards,
        mesh=mesh,
        in_specs=(
            P("req", None, "grp", None),
            P(None, "grp", None),
            P("grp", None),
            P("grp", None),
            P("grp", None),
            P("req", None, None),
            P(),
            P(None, "grp"),
            P(None, "grp"),
            P("grp", None),
            P("req", "grp", None, None),
            P("req", None, "grp", None),
            P(),
            P(),
            P(),
        ),
        out_specs=(P("req", None, "grp"), P("req", "grp", None, None), P("req", None, "grp", None)),
        check_vma=False,
    )
```

```python
import jax
import jax.numpy as jnp
from jax import lax
from jax.experimental import pallas as pl
from jax.experimental.pallas import tpu as pltpu
from jax.sharding import PartitionSpec as P

DK = 128
DRAFT = 16
CONV = 4
HALF = 4
ROWS = 2 * HALF
BF = jnp.bfloat16
PARAMS = pltpu.CompilerParams(vmem_limit_bytes=12 * 1024 * 1024)
F32 = jnp.float32
EDGES_AT = 2 * DK
DRAFTS_AT = EDGES_AT + 3 * DRAFT
PACKED = DRAFTS_AT + 3 * 2 * DRAFT
VM = pl.BlockSpec(memory_space=pltpu.VMEM)
SM = pl.BlockSpec(memory_space=pltpu.SMEM)
HB = pl.BlockSpec(memory_space=pltpu.HBM)


def row_of(half, place):
    parity = lax.axis_index("req") % 2
    base = (1 - parity if half == 0 else parity) * HALF
    return base + place


def source_of(owner_ref, row):
    me = lax.axis_index("req")
    partner = owner_ref[me * ROWS + row]
    return partner, partner // ROWS == me, partner % HALF


def block_of(block):
    return slice(block * DK, (block + 1) * DK)


def edges_of(block):
    return slice(EDGES_AT + block * DRAFT, EDGES_AT + (block + 1) * DRAFT)


def drafts_of(block):
    return slice(DRAFTS_AT + block * 2 * DRAFT, DRAFTS_AT + (block + 1) * 2 * DRAFT)


def call(kernel, out_shape, in_specs, scratch, flops, moved, *args):
    return pl.pallas_call(
        kernel,
        name=kernel.__name__,
        out_shape=out_shape,
        in_specs=in_specs,
        out_specs=jax.tree.map(lambda _: VM, out_shape),
        scratch_shapes=scratch,
        compiler_params=PARAMS,
        cost_estimate=pl.CostEstimate(flops=flops, bytes_accessed=moved, transcendentals=0),
    )(*args)


def columns_of(step, width):
    place = lax.bitwise_xor(lax.axis_index("grp"), step)
    return pl.ds(pl.multiple_of(place * width, width), width)


def fill_pack(half, out_ref, state_ref, edge_ref, draft_ref, states, edges, drafts, sems):
    rows = pl.ds(row_of(half, 0), HALF)
    state_copy = pltpu.make_async_copy(state_ref.at[rows], states, sems.at[0])
    edge_copy = pltpu.make_async_copy(edge_ref.at[rows], edges, sems.at[1])
    draft_copy = pltpu.make_async_copy(draft_ref.at[rows], drafts, sems.at[2])
    draft_copy.start()
    edge_copy.start()
    state_copy.start()
    edge_copy.wait()
    draft_copy.wait()
    for place in range(HALF):
        for block in range(3):
            columns = block_of(block)
            out_ref[place, edges_of(block), :] = jnp.zeros((DRAFT, DK), BF)
            start = EDGES_AT + block * DRAFT
            for step in range(CONV - 1):
                out_ref[place, start + 2 * step : start + 2 * step + 2, :] = edges[
                    place, step, :, columns
                ]
            start = DRAFTS_AT + block * 2 * DRAFT
            for step in range(DRAFT):
                out_ref[place, start + 2 * step : start + 2 * step + 2, :] = drafts[
                    place, step, :, columns
                ]
    state_copy.wait()
    for place in range(HALF):
        for head in range(2):
            out_ref[place, block_of(head), :] = states[place, head].astype(BF)


def pack_far(state_ref, edge_ref, draft_ref, far_ref, states, edges, drafts, sems):
    fill_pack(1, far_ref, state_ref, edge_ref, draft_ref, states, edges, drafts, sems)


def pack_near(
    state_ref, edge_ref, draft_ref, weight_ref, near_ref, one_ref, three_ref,
    states, edges, drafts, sems,
):
    width = one_ref.shape[1]
    cuts = [
        pltpu.make_async_copy(
            weight_ref.at[:, columns_of(step, width)], out_ref, sems.at[3 + i]
        )
        for i, (step, out_ref) in enumerate(((1, one_ref), (3, three_ref)))
    ]
    for copy in cuts:
        copy.start()
    fill_pack(0, near_ref, state_ref, edge_ref, draft_ref, states, edges, drafts, sems)
    for copy in cuts:
        copy.wait()


def pack_scratch(states, edges, drafts):
    return [
        pltpu.VMEM((HALF, *states.shape[1:]), F32),
        pltpu.VMEM((HALF, *edges.shape[1:]), BF),
        pltpu.VMEM((HALF, *drafts.shape[1:]), BF),
        pltpu.SemaphoreType.DMA((5,)),
    ]


def pack_far_call(*args):
    half = jax.ShapeDtypeStruct((HALF, PACKED + DRAFT, DK), BF)
    return call(pack_far, half, [HB] * 3, pack_scratch(*args), 500_000, 1_000_000, *args)


def pack_near_call(states, edges, drafts, weight):
    half = jax.ShapeDtypeStruct((HALF, PACKED, DK), BF)
    cut = jax.ShapeDtypeStruct((weight.shape[0], weight.shape[1] // 4), BF)
    return call(
        pack_near, (half, cut, cut), [HB] * 4, pack_scratch(states, edges, drafts),
        500_000, 2_000_000, states, edges, drafts, weight,
    )


def convolve(window, conv_ref, slot, head, block):
    total = None
    for shift in range(CONV):
        taps = conv_ref[shift, head, block_of(block)]
        rows = window[slot, block, pl.ds(2 + 2 * shift + head, DRAFT, stride=2), :]
        term = taps[None, :] * rows
        total = term if total is None else total + term
    return total


def as_query(x):
    return x * jax.nn.sigmoid(x) * DK ** (-0.5)


def as_value(x):
    return x * jax.nn.sigmoid(x)


def prepare(slots, own_refs, window, conv_ref, bias_ref, query_ref, forget_ref, value_ref):
    for slot in slots:
        own_ref = own_refs[slot // HALF]
        for block in range(3):
            window[slot, block, :8, :] = jnp.zeros((8, DK), F32)
            window[slot, block, 8:, :] = own_ref[slot % HALF, drafts_of(block), :].astype(F32)
    half = DRAFT // 2
    for slot in slots:
        for head in range(2):
            queries, gates, values = [
                convolve(window, conv_ref, slot, head, block) for block in range(3)
            ]
            place = slot % HALF
            query_ref[place, head, :half] = queries[:half]
            query_ref[place, head, half:] = as_query(queries[half:])
            gates = gates + bias_ref[head, :][None, :]
            forget_ref[place, head, :half] = gates[:half]
            forget_ref[place, head, half:] = jax.nn.sigmoid(gates[half:])
            value_ref[place, head, :half] = values[:half]
            value_ref[place, head, half:] = as_value(values[half:])


def mix(
    side, owner_ref, mine_ref, other_ref, query_ref, forget_ref, value_ref, conv_ref, gain_ref,
    edges, states, query_scr, forget_scr, value_scr, store,
):
    half = DRAFT // 2
    for slot in range(HALF):
        _, local, place = source_of(owner_ref, row_of(side, slot))
        for block in range(3):
            mine = mine_ref[slot, edges_of(block), :].astype(F32)
            other = other_ref[place, edges_of(block), :].astype(F32)
            edges[slot, block, :DRAFT, :] = jnp.where(local, mine, other)
            edges[slot, block, DRAFT:, :] = jnp.zeros((8, DK), F32)

        @pl.when(local)
        def _():
            states[slot] = mine_ref[slot, : 2 * DK, :]

        @pl.when(jnp.logical_not(local))
        def _():
            states[slot] = other_ref[place, : 2 * DK, :]

    sub_iota = lax.broadcasted_iota(jnp.int32, (1, DRAFT, DK), 1)

    def pair(step, _):
        base = step * 2
        for sub in range(2):
            slot = base + sub
            for head in range(2):
                lane = sub * 2 + head
                for block, (in_ref, out, act) in enumerate(
                    (
                        (query_ref, query_scr, as_query),
                        (forget_ref, forget_scr, jax.nn.sigmoid),
                        (value_ref, value_scr, as_value),
                    )
                ):
                    first = in_ref[slot, head, :half]
                    for shift in range(CONV - 1):
                        taps = conv_ref[shift, head, block_of(block)]
                        rows = edges[slot, block, pl.ds(2 * shift + head, half, stride=2), :]
                        first = first + taps[None, :] * rows
                    out[4 * step + lane, :half] = act(first)
                    out[4 * step + lane, half:] = in_ref[slot, head, half:]
        lanes = slice(4 * step, 4 * step + 4)
        queries = query_scr[lanes]
        forget = forget_scr[lanes]
        values = value_scr[lanes]
        weights = jnp.zeros((4, DRAFT, DK), F32)
        decay = jnp.ones((4, 1, DK), F32)
        head_rows = []
        query_rows = []
        for t in range(DRAFT):
            forget_t = forget[:, t : t + 1, :]
            query_t = queries[:, t : t + 1, :]
            decay = decay * forget_t
            weights = jnp.where(sub_iota == t, 1.0 - forget_t, weights * forget_t)
            scores = jnp.sum(weights * query_t, axis=-1, keepdims=True)
            head_rows.append(jnp.sum(scores * values, axis=1, keepdims=True))
            query_rows.append(query_t * decay)
        local_out = jnp.concatenate(head_rows, axis=1)
        decayed = jnp.concatenate(query_rows, axis=1)
        for sub in range(2):
            slot = base + sub
            for head in range(2):
                lane = sub * 2 + head
                fine = decayed[lane]
                coarse = fine.astype(BF)
                stacked = jnp.concatenate([coarse, (fine - coarse.astype(F32)).astype(BF)], axis=0)
                both = jnp.dot(
                    stacked, states[slot, block_of(head), :], preferred_element_type=F32
                )
                out = local_out[lane] + (both[:DRAFT] + both[DRAFT:])
                scale = lax.rsqrt(jnp.mean(out * out, axis=-1, keepdims=True) + 1e-05)
                store(slot, head, (out * scale * gain_ref[head, :][None, :]).astype(BF))
        return 0

    for step in range(HALF // 2):
        pair(step, 0)


MIX_SCRATCH = [
    pltpu.VMEM((HALF, 3, 24, DK), F32),
    pltpu.VMEM((HALF, 2 * DK, DK), BF),
    pltpu.VMEM((8, DRAFT, DK), F32),
    pltpu.VMEM((8, DRAFT, DK), F32),
    pltpu.VMEM((8, DRAFT, DK), F32),
]


def mix_near(
    owner_ref, near_ref, far_ref, from_near_ref, conv_hbm, bias_hbm, gain_hbm,
    mixed_ref, query_ref, forget_ref, value_ref, conv_ref, bias_ref, gain_ref,
    window, near_query, near_forget, near_value, edges, states, query_scr, forget_scr, value_scr,
    sems,
):
    pairs = ((conv_hbm, conv_ref), (bias_hbm, bias_ref), (gain_hbm, gain_ref))
    copies = [
        pltpu.make_async_copy(src, dst, sems.at[i]) for i, (src, dst) in enumerate(pairs)
    ]
    for copy in copies:
        copy.start()
    for copy in copies:
        copy.wait()
    own_refs = (near_ref, far_ref)
    prepare(
        range(HALF), own_refs, window, conv_ref, bias_ref, near_query, near_forget, near_value
    )
    prepare(
        range(HALF, ROWS), own_refs, window, conv_ref, bias_ref, query_ref, forget_ref, value_ref
    )

    def store(slot, head, block):
        mixed_ref[slot, :, block_of(head)] = block

    mix(
        0, owner_ref, near_ref, from_near_ref, near_query, near_forget, near_value, conv_ref,
        gain_ref, edges, states, query_scr, forget_scr, value_scr, store,
    )


def mix_near_call(owner, near, far, from_near, conv, bias, gain):
    shape = jax.ShapeDtypeStruct
    rows = (HALF, 2, DRAFT, DK)
    copied = [shape(x.shape, x.dtype) for x in (conv, bias, gain)]
    return call(
        mix_near,
        (shape((HALF, DRAFT, 2 * DK), BF), *[shape(rows, F32)] * 3, *copied),
        [SM, VM, VM, VM, HB, HB, HB],
        [pltpu.VMEM((ROWS, 3, 40, DK), F32)]
        + [pltpu.VMEM(rows, F32)] * 3
        + MIX_SCRATCH
        + [pltpu.SemaphoreType.DMA((3,))],
        15_000_000, 3_000_000, owner, near, far, from_near, conv, bias, gain,
    )


def mix_far(
    owner_ref, near_mixed_ref, far_ref, from_far_ref, query_ref, forget_ref, value_ref,
    conv_ref, gain_ref, weight_ref, mixed_ref, part_ref,
    edges, states, query_scr, forget_scr, value_scr,
):
    parity = lax.axis_index("req") % 2
    for slot in range(HALF):
        mixed_ref[row_of(0, slot)] = near_mixed_ref[slot]

    def store(slot, head, block):
        mixed_ref[parity * HALF + slot, :, block_of(head)] = block

    mix(
        1, owner_ref, far_ref, from_far_ref, query_ref, forget_ref, value_ref, conv_ref,
        gain_ref, edges, states, query_scr, forget_scr, value_scr, store,
    )
    rows = mixed_ref[...].reshape(ROWS * DRAFT, 2 * DK)
    block = weight_ref[:, columns_of(2, part_ref.shape[1])]
    part_ref[...] = jnp.dot(rows, block, preferred_element_type=F32).astype(BF)


def mix_far_call(owner, near_mixed, far, from_far, queries, forget, values, conv, gain, weight):
    shape = jax.ShapeDtypeStruct
    return call(
        mix_far,
        (
            shape((ROWS, DRAFT, 2 * DK), BF),
            shape((ROWS * DRAFT, weight.shape[1] // 4), BF),
        ),
        [SM] + [VM] * 9, MIX_SCRATCH,
        50_000_000, 2_000_000,
        owner, near_mixed, far, from_far, queries, forget, values, conv, gain, weight,
    )


def later(x, shift):
    return jnp.concatenate([x[shift:], jnp.ones((shift, DK), F32)], axis=0)


def split(x):
    coarse = x.astype(BF)
    return coarse, (x - coarse.astype(F32)).astype(BF)


def keep(
    owner_ref, accept_ref, near_ref, far_ref, from_near_ref, from_far_ref, state_ref, conv_ref,
    bias_ref, kept_ref, edges_out_ref, states, window, left, right, decays, sems,
):
    state_copies = [
        pltpu.make_async_copy(state_ref.at[row], states.at[row], sems.at[row])
        for row in range(ROWS)
    ]
    for copy in state_copies:
        copy.start()
    position = lax.broadcasted_iota(jnp.int32, (DRAFT, DK), 0)
    for slot in range(ROWS):
        side = slot // HALF
        row = row_of(side, slot % HALF)
        partner, local, place = source_of(owner_ref, row)
        length = accept_ref[partner]
        mine_ref, other_ref = (near_ref, from_near_ref) if side == 0 else (far_ref, from_far_ref)
        for block in range(3):
            mine = mine_ref[slot % HALF, drafts_of(block), :].astype(F32)
            other = other_ref[place, drafts_of(block), :].astype(F32)
            window[slot, block, 8:, :] = jnp.where(local, mine, other)
            window[slot, block, 2:8, :] = mine_ref[slot % HALF, edges_of(block), :].astype(F32)[:6]
        for head in range(2):
            gates = convolve(window, conv_ref, slot, head, 1) + bias_ref[head, :][None, :]
            values = as_value(convolve(window, conv_ref, slot, head, 2))
            forget = jax.nn.sigmoid(gates)
            inside = position < length
            weights = jnp.where(inside, 1.0 - forget, 0.0)
            factors = jnp.where(inside, forget, 1.0)
            after = later(factors, 1)
            for shift in (1, 2, 4, 8):
                after = after * later(after, shift)
            weight_high, weight_low = split(weights * after)
            value_high, value_low = split(values)
            left[slot, head] = jnp.concatenate([weight_high, weight_low, weight_high], axis=0)
            right[slot, head] = jnp.concatenate([value_high, value_high, value_low], axis=0)
            lane = 2 * slot + head
            decays[lane : lane + 1, :] = (factors * after)[:1, :]
        for block in range(3):
            turned = pltpu.roll(window[slot, block], 38 - 2 * length, 0)
            for step in range(CONV - 1):
                edges_out_ref[row, step, :, block_of(block)] = turned[
                    2 * step : 2 * step + 2
                ].astype(BF)
    columns = jnp.transpose(decays[...])
    for copy in state_copies:
        copy.wait()
    for slot in range(ROWS):
        row = row_of(slot // HALF, slot % HALF)
        for head in range(2):
            lane = 2 * slot + head
            update = lax.dot_general(
                left[slot, head], right[slot, head], (((0,), (0,)), ((), ())),
                preferred_element_type=F32,
            )
            kept_ref[row, head] = columns[:, lane : lane + 1] * states[row, head] + update


def keep_call(owner, accept, near, far, from_near, from_far, states, conv, bias):
    shape = jax.ShapeDtypeStruct
    return call(
        keep, (shape(states.shape, F32), shape((ROWS, CONV - 1, 2, 3 * DK), BF)),
        [SM, SM, VM, VM, VM, VM, HB, VM, VM],
        [
            pltpu.VMEM(states.shape, F32),
            pltpu.VMEM((ROWS, 3, 40, DK), F32),
            pltpu.VMEM((ROWS, 2, 3 * DRAFT, DK), BF),
            pltpu.VMEM((ROWS, 2, 3 * DRAFT, DK), BF),
            pltpu.VMEM((2 * ROWS, DK), F32),
            pltpu.SemaphoreType.DMA((ROWS,)),
        ],
        20_000_000, 3_000_000, owner, accept, near, far, from_near, from_far, states, conv, bias,
    )


def project(
    own_ref, one_ref, three_ref, weight_ref, from_one_ref, from_three_ref, part_ref,
    resid_ref, stream_ref,
):
    width = stream_ref.shape[1]
    columns = columns_of(0, width)
    total = jnp.dot(own_ref[...], weight_ref[:, columns], preferred_element_type=F32)
    total = total + jnp.dot(one_ref[...], from_one_ref[...], preferred_element_type=F32)
    total = total + jnp.dot(three_ref[...], from_three_ref[...], preferred_element_type=F32)
    total = total + part_ref[...].astype(F32)
    stream_ref[...] = (resid_ref[:, columns].astype(F32) + total).astype(BF)


def project_call(mixed, one, three, weight, parts, part, resid):
    slots, model = resid.shape
    return call(
        project, jax.ShapeDtypeStruct((slots, model // 4), BF), [VM] * 8, [],
        100_000_000, 3_000_000, mixed, one, three, weight, *parts, part, resid,
    )


NT = (((1,), (1,)), ((), ()))


def gated(rows, step, gain_ref, gate_ref, up_ref):
    block = rows.astype(F32)
    square = jnp.sum(block * block, axis=-1, keepdims=True)
    columns = columns_of(step, rows.shape[1])
    scaled = (block * gain_ref[:, columns]).astype(BF)
    gate = lax.dot_general(scaled, gate_ref[:, columns], NT, preferred_element_type=F32)
    up = lax.dot_general(scaled, up_ref[:, columns], NT, preferred_element_type=F32)
    return square, gate, up


def ffn_first(
    own_ref, two_ref, three_ref, gain_ref, gate_ref, up_ref, square_ref, gate_out_ref, up_out_ref,
):
    total = None
    for step, ref in ((0, own_ref), (2, two_ref), (3, three_ref)):
        parts = gated(ref[...], step, gain_ref, gate_ref, up_ref)
        total = parts if total is None else [x + y for x, y in zip(total, parts)]
    square_ref[...] = jnp.broadcast_to(total[0], square_ref.shape)
    gate_out_ref[...] = total[1]
    up_out_ref[...] = total[2]


def ffn_first_call(own, two, three, gain, gate_t, up_t):
    slots, hidden = own.shape[0], gate_t.shape[0]
    shape = jax.ShapeDtypeStruct
    return call(
        ffn_first,
        (shape((slots, DK), F32), shape((slots, hidden), F32), shape((slots, hidden), F32)),
        [VM] * 6, [], 550_000_000, 5_000_000, own, two, three, gain, gate_t, up_t,
    )


def ffn_last(
    length_ref, own_ref, one_ref, gain_ref, gate_ref, up_ref, down_ref,
    square_ref, gate_in_ref, up_in_ref, own_out_ref, one_out_ref, two_out_ref, three_out_ref,
):
    width = own_ref.shape[1]
    square, gate, up = gated(one_ref[...], 1, gain_ref, gate_ref, up_ref)
    total = square + square_ref[:, :1]
    scale = lax.rsqrt(total / (4 * width) + 1e-05)
    gate = (gate + gate_in_ref[...]) * scale
    up = (up + up_in_ref[...]) * scale
    hidden = (gate * jax.nn.sigmoid(gate) * up).astype(BF)
    me = lax.axis_index("req")
    position = lax.broadcasted_iota(jnp.int32, (DRAFT, 1), 0)
    live = jnp.concatenate(
        [(position < length_ref[me * ROWS + row]).astype(F32) for row in range(ROWS)], axis=0
    )
    for step, out_ref in ((2, two_out_ref), (1, one_out_ref), (3, three_out_ref)):
        part = jnp.dot(hidden, down_ref[:, columns_of(step, width)], preferred_element_type=F32)
        out_ref[...] = (part * live).astype(BF)
    part = jnp.dot(hidden, down_ref[:, columns_of(0, width)], preferred_element_type=F32)
    own_out_ref[...] = (part + own_ref[...].astype(F32)) * live


def ffn_last_call(lengths, own, one, gain, gate_t, up_t, down, *partial):
    slots, width = own.shape
    shape = jax.ShapeDtypeStruct
    part = shape((slots, width), BF)
    return call(
        ffn_last, (shape((slots, width), F32), part, part, part), [SM] + [VM] * 9, [],
        550_000_000, 5_000_000, lengths, own, one, gain, gate_t, up_t, down, *partial,
    )


def in_hbm(array):
    return pltpu.with_memory_space_constraint(array, pltpu.HBM)


def swapped(block, step):
    return lax.ppermute(block, "grp", [(i, i ^ step) for i in range(4)])


def shards(
    mix_inputs,
    conv_weight,
    forget_bias,
    norm_gain,
    out_weight,
    resid,
    ffn_gain,
    gate_weight,
    up_weight,
    down_weight,
    held_states,
    held_edges,
    draft_lengths,
    accepted,
    owner_row,
):
    slots = ROWS * DRAFT
    owner_row, accepted, draft_lengths = in_hbm(owner_row), in_hbm(accepted), in_hbm(draft_lengths)
    count = lax.axis_size("req")
    states = in_hbm(held_states)
    across = [(i, (i + (1 if i % 2 else -1)) % count) for i in range(count)]
    held, drafts = in_hbm(held_edges), in_hbm(mix_inputs)
    far = pack_far_call(states, held, drafts)
    from_far = lax.ppermute(far, "req", across)
    near, *cuts = pack_near_call(states, held, drafts, in_hbm(out_weight))
    from_near = lax.ppermute(near, "req", [(i, i ^ 1) for i in range(count)])
    parts = [swapped(cut, step) for step, cut in ((1, cuts[0]), (3, cuts[1]))]
    near_mixed, queries, forget, values, conv, bias, gain = mix_near_call(
        owner_row, near, far, from_near,
        in_hbm(conv_weight), in_hbm(forget_bias), in_hbm(norm_gain),
    )
    mixed, part = mix_far_call(
        owner_row, near_mixed, far, from_far, queries, forget, values, conv, gain, out_weight
    )
    mixed = mixed.reshape(slots, -1)
    part = swapped(part, 2)
    one = swapped(mixed, 1)
    three = swapped(mixed, 3)
    gate_t, up_t, down = gate_weight.T, up_weight.T, down_weight
    stream = project_call(mixed, one, three, out_weight, parts, part, resid.reshape(slots, -1))
    two = swapped(stream, 2)
    three = swapped(stream, 3)
    one = swapped(stream, 1)
    gain_row = ffn_gain[None, :]
    partial = ffn_first_call(stream, two, three, gain_row, gate_t, up_t)
    own_part, to_one, to_two, to_three = ffn_last_call(
        draft_lengths, stream, one, gain_row, gate_t, up_t, down, *partial
    )
    three = swapped(to_three, 3)
    two = swapped(to_two, 2)
    one = swapped(to_one, 1)
    own_part, from_near, from_far = lax.optimization_barrier((own_part, from_near, from_far))
    kept_states, kept_edges = keep_call(
        owner_row, accepted, near, far, from_near, from_far, states, conv, bias
    )
    layer_out = (own_part + three.astype(F32) + two.astype(F32) + one.astype(F32)).astype(BF)
    return (layer_out.reshape(ROWS, DRAFT, -1), kept_states, kept_edges)


def solution(mesh):
    return jax.shard_map(
        shards,
        mesh=mesh,
        in_specs=(
            P("req", None, "grp", None),
            P(None, "grp", None),
            P("grp", None),
            P("grp", None),
            P("grp", None),
            P("req", None, None),
            P(),
            P(None, "grp"),
            P(None, "grp"),
            P("grp", None),
            P("req", "grp", None, None),
            P("req", None, "grp", None),
            P(),
            P(),
            P(),
        ),
        out_specs=(P("req", None, "grp"), P("req", "grp", None, None), P("req", None, "grp", None)),
        check_vma=False,
    )
```
